32 devices in a mesh: member: 2 (over y), wave: 4 (over z), level: 2 (over x), fld: 2 (over core).
Axes of the slice: x: 2, y: 2, z: 4, core: 2. Of those that a mesh axis runs over, the one named last changes fastest.
Arguments:
- grid_state: bfloat16 [256, 2, 256, 1536], P(('member', 'level'), 'fld', 'wave'), parts along dimension 0, may hold values from -6 to 6
- legendre: bfloat16 [512, 2, 256, 256], P(('wave', 'level'), 'fld'), may hold values from -0.375 to 0.375
- wave_order: int32 [512], replicated, may hold values from 0 to 511, each once
- lat_order: int32 [256], replicated, may hold values from 0 to 255, each once
- eig_rates: float32 [128], replicated, may hold values from 0.1 to 4
- modes_in: bfloat16 [128, 128], replicated, may hold values from -0.5 to 0.5
- modes_out: bfloat16 [128, 128], replicated, may hold values from -0.5 to 0.5
Outputs:
- new_state: bfloat16 [256, 2, 256, 1536], P(('member', 'level'), 'fld', 'wave'), parts along dimension 0
The draws below stay inside these ranges and needn't reach their ends.
There are 2 independent parts, one for each index of `member`. The reference program is written for one: setup_inputs(seed, part) draws one part's arguments, and reference() takes and returns one part's arrays. A program takes and returns all parts, laid end to end along the dimension named above; an argument that names none is the same for every part. Nothing has to cross between parts.
Inputs may be any that keep to these rules, and one draw needn't show every extreme that they name: Slot s holds zonal wavenumber wave_order[s]; every wavenumber 0 to 511 is held by exactly one slot. Latitude row r lies at Gaussian latitude index lat_order[r] counted from the equator, the same in both hemispheres; every index appears once.
All inputs are finite; a program needn't handle non-finite values.
Results may differ from the reference program's by a relative error of at most 0.0098.
Values may be sent and summed in bfloat16 or wider, within the bound.
No kernel may reach another device: no remote copies, remote signals or barrier semaphores. Data moves between devices by JAX's collectives and lax.ppermute only.
A program may use at most 128 MiB of HBM per device.

```python
import math
import jax
import jax.numpy as jnp
from jax import lax

LON = 1536
LATH = 256
M = 512
NH = 256
LEV = 128
ITERS = 1


def level_of(rng, extent, split, least, high):
    loudness = 1.0
    for dim, parts in split:
        steps = jax.random.uniform(jax.random.fold_in(jax.random.fold_in(rng, 6), dim), (parts,), jnp.float32, least / len(split), high / len(split))
        loudness = loudness * jnp.repeat(jnp.exp(steps), extent[dim] // parts).reshape((-1,) + (1,) * (len(extent) - 1 - dim))
    return loudness


def scatter_about(stream_key, extent, deviation, bound, cuts=(), kind=jnp.bfloat16):
    entries = jax.random.normal(stream_key, extent, jnp.float32) * deviation
    if len(cuts) > 0:
        entries = level_of(stream_key, extent, cuts, -0.22, 0.18) * entries
    return jnp.clip(entries, min=-bound, max=bound).astype(kind)


def setup_inputs(seed: int = 0, part: int = 0) -> dict:
    key_list = jax.random.split(jax.random.key(seed), 8)
    own_keys = jax.random.split(jax.random.fold_in(key_list[7], part), 8)
    grid_state = scatter_about(own_keys[0], (LEV, 2, LATH, LON), 1.0, 6.0, ((0, 2), (1, 2), (2, 4)))
    legendre = scatter_about(key_list[1], (M, 2, LATH, NH), NH ** -0.5, 0.375, ((0, 8), (1, 2)))
    wave_order = jax.random.permutation(key_list[2], M).astype(jnp.int32)
    lat_order = jax.random.permutation(key_list[3], LATH).astype(jnp.int32)
    eig_rates = jnp.clip(jnp.exp(jax.random.uniform(key_list[4], (LEV,), jnp.float32, math.log(0.1), math.log(4.0))), 0.1, 4.0)
    modes_in = scatter_about(key_list[5], (LEV, LEV), LEV ** -0.5, 0.5)
    modes_out = scatter_about(key_list[6], (LEV, LEV), LEV ** -0.5, 0.5)
    return dict(grid_state=grid_state, legendre=legendre, wave_order=wave_order, lat_order=lat_order, eig_rates=eig_rates, modes_in=modes_in, modes_out=modes_out)


tau_scale = 2.0

def fourier_table(wave_order, lon_count):
    longitude = jnp.arange(lon_count, dtype=jnp.int32)
    phase_index = longitude[:, None] * wave_order[None, :].astype(jnp.int32) % lon_count
    angles = phase_index.astype(jnp.float32) * (2.0 * math.pi / lon_count)
    weight_scale = math.sqrt(2.0 / lon_count)
    return jnp.concatenate([jnp.cos(angles) * weight_scale, -jnp.sin(angles) * weight_scale], axis=1).astype(jnp.bfloat16)

def rounded(values):
    return lax.optimization_barrier(values.astype(jnp.bfloat16)).astype(jnp.float32)

def reference(grid_state, legendre, wave_order, lat_order, eig_rates, modes_in, modes_out):
    highest = lax.Precision.HIGHEST
    wave_table = fourier_table(wave_order, LON).astype(jnp.float32)
    sine = jnp.sin((lat_order.astype(jnp.float32) + 0.5) * (math.pi / (2.0 * LATH)))
    hemi_sign = jnp.array([1.0, -1.0], dtype=jnp.float32)
    coupling = (0.5 * hemi_sign)[None, :, None, None] * sine[None, None, :, None]
    parity = jnp.arange(2, dtype=jnp.int32)
    degree = wave_order.astype(jnp.int32)[:, None, None] + 2 * jnp.arange(NH, dtype=jnp.int32)[None, None, :] + parity[None, :, None]
    in_triangle = (degree <= M - 1).astype(jnp.float32)
    degree_f = degree.astype(jnp.float32)
    damp_ratio = tau_scale * degree_f * (degree_f + 1.0) / float(M * (M - 1))
    factor = 1.0 / (1.0 + damp_ratio[..., None] * eig_rates[None, None, None, :])
    table_f = legendre.astype(jnp.float32)
    inward = modes_in.astype(jnp.float32)
    outward = modes_out.astype(jnp.float32)
    initial = grid_state.astype(jnp.float32)
    current = grid_state
    for iteration in range(ITERS):
        forcing = (initial + coupling * jnp.tanh(current.astype(jnp.float32))).astype(jnp.bfloat16)
        fourier_rows = jnp.einsum('lhrg,gk->lhrk', forcing.astype(jnp.float32), wave_table, precision=highest)
        fourier_rows = rounded(fourier_rows).reshape(LEV, 2, LATH, 2, M)
        mirrored = jnp.stack([fourier_rows[:, 0] + fourier_rows[:, 1], fourier_rows[:, 0] - fourier_rows[:, 1]], axis=1)
        mirrored = rounded(mirrored)
        spectral = jnp.einsum('lprcs,sprj->spjcl', mirrored, table_f, precision=highest)
        spectral = rounded(spectral * in_triangle[:, :, :, None, None])
        modal = jnp.einsum('spjcl,kl->spjck', spectral, inward, precision=highest)
        modal = rounded(modal * factor[:, :, :, None, :])
        solved = rounded(jnp.einsum('spjck,lk->spjcl', modal, outward, precision=highest))
        grid_coeffs = rounded(jnp.einsum('spjcl,sprj->lprcs', solved, table_f, precision=highest))
        hemi_grid = jnp.stack([0.5 * (grid_coeffs[:, 0] + grid_coeffs[:, 1]), 0.5 * (grid_coeffs[:, 0] - grid_coeffs[:, 1])], axis=1)
        flat_coeffs = rounded(hemi_grid).reshape(LEV, 2, LATH, 2 * M)
        current = jnp.einsum('lhrk,gk->lhrg', flat_coeffs, wave_table, precision=highest).astype(jnp.bfloat16)
    return current
```

```python
import functools
import math

import jax
import jax.numpy as jnp
from jax import lax
from jax.experimental import pallas as pl
from jax.experimental.pallas import tpu as pltpu
from jax.sharding import PartitionSpec as P

tau_scale = 2.0
LANES = 128


def partner(value, axis):
    pairs = [(source, source ^ 1) for source in range(lax.axis_size(axis))]
    return lax.ppermute(value, axis, pairs)


def phase_of(product, period):
    return (product % period).astype(jnp.float32) * (2.0 * math.pi / period)


def table_kernel(scale, high_cos, high_sin, low_cos, low_sin, out):
    for block in range(out.shape[1] // LANES):
        spot = slice(block * LANES, (block + 1) * LANES)
        values = (
            high_cos[:, block : block + 1] * low_cos[...]
            - high_sin[:, block : block + 1] * low_sin[...]
        )
        out[:, spot] = (values * scale).astype(out.dtype)


def fourier_rows_table(ids, quarter, lon_count, chunks):
    rows = ids.shape[0]
    blocks = lon_count // LANES
    high = phase_of(
        ids[:, None] * LANES * jnp.arange(blocks, dtype=jnp.int32)[None, :] + quarter[:, None],
        lon_count,
    )
    low = phase_of(ids[:, None] * jnp.arange(LANES, dtype=jnp.int32)[None, :], lon_count)
    step = rows // chunks
    high_spec = pl.BlockSpec((step, blocks), lambda i: (i, 0))
    low_spec = pl.BlockSpec((step, LANES), lambda i: (i, 0))
    return pl.pallas_call(
        functools.partial(table_kernel, math.sqrt(2.0 / lon_count)),
        out_shape=jax.ShapeDtypeStruct((rows, lon_count), jnp.bfloat16),
        grid=(chunks,),
        in_specs=[high_spec, high_spec, low_spec, low_spec],
        out_specs=pl.BlockSpec((step, lon_count), lambda i: (i, 0)),
        cost_estimate=pl.CostEstimate(
            flops=4 * rows * lon_count, bytes_accessed=2 * rows * lon_count, transcendentals=0
        ),
    )(jnp.cos(high), jnp.sin(high), jnp.cos(low), jnp.sin(low))


def column_kernel(
    sizes, waves, sign_ref, eig_ref, modes_in, modes_out, own, other, table, out, rows_in, rows_out
):
    wave_size, level_size, group, tiles, half_count, wave_count, first = sizes
    places = wave_size * level_size
    eights = group // 8
    sign = sign_ref[0, 0]
    parity = sign_ref[0, 1]
    low_half = lax.broadcasted_iota(jnp.int32, (tiles, LANES), 1) < LANES // 2

    def spread(index, carry):
        place, part = index // 2, index % 2
        for tile in range(tiles):
            lanes = slice(tile * LANES, (tile + 1) * LANES)
            value = other[place, part, :, lanes].astype(jnp.float32) + sign * own[
                place, part, :, lanes
            ].astype(jnp.float32)
            value = value.astype(jnp.bfloat16).astype(jnp.float32)
            for eight in range(eights):
                start = pl.multiple_of(((index * eights + eight) * tiles + tile) * 8, 8)
                rows_in[pl.ds(start, 8), :] = value[eight * 8 : (eight + 1) * 8]
        return carry

    lax.fori_loop(0, places * 2, spread, 0)

    def where_rows(place, part, slot):
        eight, within = slot // 8, slot % 8
        return pl.ds((((place * 2 + part) * eights + eight) * tiles) * 8 + within, tiles, 8)

    def one_slot(slot, carry):
        legendre = table[slot]
        stacked = []
        for part in range(2):
            low_rows, high_rows = [], []
            for level in range(level_size):
                low_pieces, high_pieces = [], []
                for pair in range(wave_size // 2):
                    a = rows_in[where_rows(2 * pair * level_size + level, part, slot), :]
                    b = rows_in[where_rows((2 * pair + 1) * level_size + level, part, slot), :]
                    low_pieces.append(jnp.where(low_half, a, pltpu.roll(b, LANES // 2, 1)))
                    high_pieces.append(jnp.where(low_half, pltpu.roll(a, LANES // 2, 1), b))
                low_rows.append(jnp.concatenate(low_pieces, axis=1))
                high_rows.append(jnp.concatenate(high_pieces, axis=1))
            stacked += low_rows + high_rows
        field = jnp.concatenate(stacked, axis=0).astype(jnp.bfloat16)
        degree = (
            waves[first + pl.program_id(0) * group + slot]
            + 2 * lax.broadcasted_iota(jnp.int32, (1, half_count), 1)
        ).astype(jnp.float32) + parity
        inside = (degree <= float(wave_count - 1)).astype(jnp.float32)
        ratio = tau_scale * degree * (degree + 1.0) / float(wave_count * (wave_count - 1))
        factor = 1.0 / (1.0 + eig_ref[...] * ratio)
        spectral = jnp.dot(field, legendre, preferred_element_type=jnp.float32)
        spectral = (spectral * inside).astype(jnp.bfloat16)
        levels = modes_in.shape[0]
        solved = []
        for part in range(2):
            column = spectral[part * levels : (part + 1) * levels]
            modal = jnp.dot(modes_in[...], column, preferred_element_type=jnp.float32)
            modal = (modal * factor).astype(jnp.bfloat16)
            solved.append(
                jnp.dot(modes_out[...], modal, preferred_element_type=jnp.float32).astype(
                    jnp.bfloat16
                )
            )
        grid = lax.dot_general(
            jnp.concatenate(solved, axis=0),
            legendre,
            (((1,), (1,)), ((), ())),
            preferred_element_type=jnp.float32,
        )
        for part in range(2):
            for level in range(level_size):
                low_start = part * levels + level * tiles
                high_start = low_start + level_size * tiles
                for pair in range(wave_size // 2):
                    lanes = slice(pair * LANES, (pair + 1) * LANES)
                    low = grid[low_start : low_start + tiles, lanes]
                    high = grid[high_start : high_start + tiles, lanes]
                    a = jnp.where(low_half, low, pltpu.roll(high, LANES // 2, 1))
                    b = jnp.where(low_half, pltpu.roll(low, LANES // 2, 1), high)
                    rows_out[where_rows(2 * pair * level_size + level, part, slot), :] = a
                    rows_out[where_rows((2 * pair + 1) * level_size + level, part, slot), :] = b
        return carry

    lax.fori_loop(0, group, one_slot, 0)

    def gather(index, carry):
        place, part = index // 2, index % 2
        for tile in range(tiles):
            parts = []
            for eight in range(eights):
                start = pl.multiple_of(((index * eights + eight) * tiles + tile) * 8, 8)
                parts.append(rows_out[pl.ds(start, 8), :])
            out[place, part, :, tile * LANES : (tile + 1) * LANES] = jnp.concatenate(
                parts, axis=0
            ).astype(out.dtype)
        return carry

    lax.fori_loop(0, places * 2, gather, 0)


def columns(own, other, legendre, waves, eig_rates, modes_in, modes_out, hemi_sign, wave_size, chunk):
    places, _, count, width = own.shape
    level_size = places // wave_size
    levels = modes_in.shape[0]
    half_rows, half_count = legendre.shape[1:]
    local_levels = levels // level_size
    rows_here = width // local_levels
    wave_count = wave_size * level_size * legendre.shape[0]
    first = chunk * count
    parity = 0.5 - 0.5 * hemi_sign
    if rows_here * 2 == LANES and wave_size % 2 == 0 and count % 16 == 0:
        tiles = width // LANES
        order = jnp.arange(levels).reshape(level_size, tiles, 2).transpose(2, 0, 1).reshape(-1)
        group = 16
        sizes = (wave_size, level_size, group, tiles, half_count, wave_count, first)
        data_spec = pl.BlockSpec((places, 2, group, width), lambda i: (0, 0, i, 0))
        whole = lambda shape: pl.BlockSpec(shape, lambda i: (0,) * len(shape))
        slots = places * count * 2 * width
        return pl.pallas_call(
            functools.partial(column_kernel, sizes),
            out_shape=jax.ShapeDtypeStruct(own.shape, jnp.bfloat16),
            grid=(count // group,),
            in_specs=[
                pl.BlockSpec(memory_space=pltpu.SMEM),
                pl.BlockSpec(memory_space=pltpu.SMEM),
                whole((levels, 1)),
                whole((levels, levels)),
                whole((levels, levels)),
                data_spec,
                data_spec,
                pl.BlockSpec(
                    (group, half_rows, half_count), lambda i: (first // group + i, 0, 0)
                ),
            ],
            out_specs=data_spec,
            scratch_shapes=[
                pltpu.VMEM((places * 2 * group * tiles, LANES), jnp.float32),
                pltpu.VMEM((places * 2 * group * tiles, LANES), jnp.float32),
            ],
            compiler_params=pltpu.CompilerParams(vmem_limit_bytes=48 * 2**20),
            cost_estimate=pl.CostEstimate(
                flops=slots * half_rows * 6,
                bytes_accessed=8 * slots,
                transcendentals=0,
            ),
        )(
            waves,
            jnp.stack([hemi_sign, parity])[None, :],
            eig_rates[:, None],
            modes_in[:, order],
            modes_out[order, :],
            own,
            other,
            legendre,
        )
    mirrored = (other.astype(jnp.float32) + hemi_sign * own.astype(jnp.float32)).astype(
        jnp.bfloat16
    )
    mirrored = mirrored.reshape(wave_size, level_size, 2, count, local_levels, rows_here)
    field = mirrored.transpose(3, 2, 1, 4, 0, 5).reshape(count, 2, levels, half_rows)
    table = legendre[first : first + count]
    degree = (
        waves[first : first + count, None] + 2 * jnp.arange(half_count, dtype=jnp.int32)[None, :]
    ).astype(jnp.float32) + parity
    inside = (degree <= float(wave_count - 1)).astype(jnp.float32)
    ratio = tau_scale * degree * (degree + 1.0) / float(wave_count * (wave_count - 1))
    factor = 1.0 / (1.0 + ratio[:, None, :] * eig_rates[None, :, None])
    spectral = jnp.einsum("sclr,srj->sclj", field, table, preferred_element_type=jnp.float32)
    spectral = (spectral * inside[:, None, None, :]).astype(jnp.bfloat16)
    modal = jnp.einsum("kl,sclj->sckj", modes_in, spectral, preferred_element_type=jnp.float32)
    modal = (modal * factor[:, None, :, :]).astype(jnp.bfloat16)
    solved = jnp.einsum(
        "lk,sckj->sclj", modes_out, modal, preferred_element_type=jnp.float32
    ).astype(jnp.bfloat16)
    grid = jnp.einsum("sclj,srj->sclr", solved, table, preferred_element_type=jnp.float32)
    grid = grid.astype(jnp.bfloat16)
    grid = grid.reshape(count, 2, level_size, local_levels, wave_size, rows_here)
    return grid.transpose(4, 2, 1, 0, 3, 5).reshape(own.shape)


def shards(grid_state, legendre, wave_order, lat_order, eig_rates, modes_in, modes_out):
    local_levels, _, rows_here, lon_count = grid_state.shape
    wave_size = lax.axis_size("wave")
    level_size = lax.axis_size("level")
    places = wave_size * level_size
    half_rows = lat_order.shape[0]
    narrow = legendre.shape[0]
    chunks = min(4, narrow)
    count = narrow // chunks
    width = local_levels * rows_here
    parity = lax.axis_index("fld")
    wave_place = lax.axis_index("wave")
    place = wave_place * level_size + lax.axis_index("level")
    legendre = legendre.reshape(narrow, legendre.shape[2], legendre.shape[3])
    hemi_sign = 1.0 - 2.0 * parity.astype(jnp.float32)
    lat_rows = lax.dynamic_slice_in_dim(lat_order, wave_place * rows_here, rows_here)
    sine = jnp.sin((lat_rows.astype(jnp.float32) + 0.5) * (math.pi / (2.0 * half_rows)))
    coupling = (0.5 * hemi_sign * sine)[None, :, None]
    waves = lax.dynamic_slice_in_dim(wave_order, place * narrow, narrow)

    ids = wave_order.reshape(places, chunks, count).transpose(1, 0, 2)
    ids = jnp.broadcast_to(ids[:, :, None, :], (chunks, places, 2, count)).reshape(-1)
    quarter = jnp.broadcast_to(
        (jnp.arange(2, dtype=jnp.int32) * (lon_count // 4))[None, None, :, None],
        (chunks, places, 2, count),
    ).reshape(-1)
    table = fourier_rows_table(ids, quarter, lon_count, chunks)
    table = table.reshape(chunks, places * 2 * count, lon_count)

    field = grid_state.reshape(local_levels, rows_here, lon_count).astype(jnp.float32)
    forcing = (field + coupling * jnp.tanh(field)).astype(jnp.bfloat16)
    forcing = forcing.reshape(width, lon_count)

    def exchange(value):
        return lax.all_to_all(
            value, ("wave", "level"), split_axis=0, concat_axis=0, tiled=True
        )

    returned = []
    for chunk in range(chunks):
        fourier = lax.dot_general(
            table[chunk], forcing, (((1,), (1,)), ((), ())), preferred_element_type=jnp.float32
        ).astype(jnp.bfloat16)
        own = exchange(fourier.reshape(places, 2, count, width))
        other = partner(own, "fld")
        grid = columns(
            own, other, legendre, waves, eig_rates, modes_in, modes_out, hemi_sign, wave_size, chunk
        )
        back = partner(grid, "fld")
        hemi = (
            0.5 * (back.astype(jnp.float32) + hemi_sign * grid.astype(jnp.float32))
        ).astype(jnp.bfloat16)
        returned.append(exchange(hemi).reshape(places * 2 * count, width))
    coeffs = jnp.concatenate(returned, axis=0)
    current = lax.dot_general(
        coeffs,
        table.reshape(-1, lon_count),
        (((0,), (0,)), ((), ())),
        preferred_element_type=jnp.float32,
    ).astype(jnp.bfloat16)
    return current.reshape(grid_state.shape)


def solution(mesh):
    placed = (
        P(("member", "level"), "fld", "wave", None),
        P(("wave", "level"), "fld", None, None),
        P(),
        P(),
        P(),
        P(),
        P(),
    )
    return jax.shard_map(
        shards,
        mesh=mesh,
        in_specs=placed,
        out_specs=P(("member", "level"), "fld", "wave", None),
        check_vma=False,
    )
```

```python
import functools
import math

import jax
import jax.numpy as jnp
from jax import lax
from jax.experimental import pallas as pl
from jax.experimental.pallas import tpu as pltpu
from jax.sharding import PartitionSpec as P


tau_scale = 2.0
LANES = 128
DIRECT_LIMIT = 16
CHUNKS = 4
SPLITS = 4
EXCHANGE_AXES = ("wave", "level")


def partner(value, axis):
    pairs = [(source, source ^ 1) for source in range(lax.axis_size(axis))]
    return lax.ppermute(value, axis, pairs)


def shift_places(value, wave_shift, level_shift):
    if wave_shift == 0 and level_shift == 0:
        return value
    waves, levels = lax.axis_size("wave"), lax.axis_size("level")
    pairs = []
    for wave in range(waves):
        for level in range(levels):
            target = (wave + wave_shift) % waves * levels + (level + level_shift) % levels
            pairs.append((wave * levels + level, target))
    return lax.ppermute(value, EXCHANGE_AXES, pairs)


def rolled(value, start):
    return lax.dynamic_slice_in_dim(
        jnp.concatenate([value, value], axis=0), start, value.shape[0], axis=0
    )


def phase_of(product, period):
    return (product % period).astype(jnp.float32) * (2.0 * math.pi / period)


def table_kernel(scale, high_cos, high_sin, low_cos, low_sin, out):
    for block in range(out.shape[1] // LANES):
        spot = slice(block * LANES, (block + 1) * LANES)
        values = (
            high_cos[:, block : block + 1] * low_cos[...]
            - high_sin[:, block : block + 1] * low_sin[...]
        )
        out[:, spot] = (values * scale).astype(out.dtype)


def fourier_table(ids, quarter, lon_count, chunks):
    rows = ids.shape[0]
    blocks = lon_count // LANES
    high = phase_of(
        ids[:, None] * LANES * jnp.arange(blocks, dtype=jnp.int32)[None, :] + quarter[:, None],
        lon_count,
    )
    low = phase_of(ids[:, None] * jnp.arange(LANES, dtype=jnp.int32)[None, :], lon_count)
    step = rows // chunks
    high_spec = pl.BlockSpec((step, blocks), lambda i: (i, 0))
    low_spec = pl.BlockSpec((step, LANES), lambda i: (i, 0))
    return pl.pallas_call(
        functools.partial(table_kernel, math.sqrt(2.0 / lon_count)),
        out_shape=jax.ShapeDtypeStruct((rows, lon_count), jnp.bfloat16),
        grid=(chunks,),
        in_specs=[high_spec, high_spec, low_spec, low_spec],
        out_specs=pl.BlockSpec((step, lon_count), lambda i: (i, 0)),
        cost_estimate=pl.CostEstimate(
            flops=4 * rows * lon_count, bytes_accessed=2 * rows * lon_count, transcendentals=0
        ),
    )(jnp.cos(high), jnp.sin(high), jnp.cos(low), jnp.sin(low))


def level_block(levels, rows_here):
    return 8 if levels % 8 == 0 and 8 * rows_here % LANES == 0 else levels


def fourier_kernel(grid_ref, coupling, table, *outs):
    levels, rows, lon_count = grid_ref.shape
    field = grid_ref[...].astype(jnp.float32)
    forcing = (field + coupling[...][None] * jnp.tanh(field)).astype(jnp.bfloat16)
    forcing = forcing.reshape(levels * rows, lon_count)
    height = outs[0].shape[0]
    for index, out in enumerate(outs):
        out[...] = lax.dot_general(
            table[index * height : (index + 1) * height],
            forcing,
            (((1,), (1,)), ((), ())),
            preferred_element_type=jnp.float32,
        ).astype(out.dtype)


def fourier(grid_state, coupling, table, pieces, start, levels):
    _, rows_here, lon_count = grid_state.shape
    height = table.shape[0] // pieces
    block = level_block(levels, rows_here)
    first = start // block
    width = levels * rows_here
    return pl.pallas_call(
        fourier_kernel,
        out_shape=[jax.ShapeDtypeStruct((height, width), jnp.bfloat16)] * pieces,
        grid=(levels // block,),
        in_specs=[
            pl.BlockSpec((block, rows_here, lon_count), lambda i: (first + i, 0, 0)),
            pl.BlockSpec((rows_here, 1), lambda i: (0, 0)),
            pl.BlockSpec(table.shape, lambda i: (0, 0), pipeline_mode=pl.Buffered(1)),
        ],
        out_specs=[pl.BlockSpec((height, block * rows_here), lambda i: (0, i))] * pieces,
        compiler_params=pltpu.CompilerParams(vmem_limit_bytes=40 * 2**20),
        cost_estimate=pl.CostEstimate(
            flops=2 * table.shape[0] * width * lon_count,
            bytes_accessed=2 * (width * lon_count + table.shape[0] * (width + lon_count)),
            transcendentals=width * lon_count,
        ),
    )(grid_state, coupling, table)


def column_kernel(sizes, waves, scalars, eig_ref, modes_in, modes_out, table, *refs):
    wave_size, level_size, splits, group, tiles, half_count, wave_count, first = sizes
    places = wave_size * level_size
    pieces, (out, rows_in, rows_out) = refs[: places * splits], refs[places * splits :]
    eights = group // 8
    some = tiles // splits
    rows_here = LANES // 2
    parity = scalars[wave_size].astype(jnp.float32)
    low_half = lax.broadcasted_iota(jnp.int32, (tiles, LANES), 1) < LANES // 2

    for place in range(places):
        for split in range(splits):
            piece = pieces[place * splits + split]

            def spread(part, carry, place=place, split=split, piece=piece):
                for tile in range(some):
                    value = piece[part, :, tile * LANES : (tile + 1) * LANES].astype(jnp.float32)
                    for eight in range(eights):
                        row = ((place * 2 + part) * eights + eight) * tiles + split * some + tile
                        rows_in[pl.ds(pl.multiple_of(row * 8, 8), 8), :] = value[
                            eight * 8 : (eight + 1) * 8
                        ]
                return carry

            lax.fori_loop(0, 2, spread, 0)

    def where_rows(place, part, slot):
        eight, within = slot // 8, slot % 8
        return pl.ds((((place * 2 + part) * eights + eight) * tiles) * 8 + within, tiles, 8)

    def one_slot(slot, carry):
        legendre = jnp.concatenate(
            [
                table[slot, pl.ds(pl.multiple_of(scalars[wave] * rows_here, rows_here), rows_here), :]
                for wave in range(wave_size)
            ],
            axis=0,
        )
        stacked = []
        for part in range(2):
            low_rows, high_rows = [], []
            for level in range(level_size):
                low_pieces, high_pieces = [], []
                for pair in range(wave_size // 2):
                    a = rows_in[where_rows(2 * pair * level_size + level, part, slot), :]
                    b = rows_in[where_rows((2 * pair + 1) * level_size + level, part, slot), :]
                    low_pieces.append(jnp.where(low_half, a, pltpu.roll(b, LANES // 2, 1)))
                    high_pieces.append(jnp.where(low_half, pltpu.roll(a, LANES // 2, 1), b))
                low_rows.append(jnp.concatenate(low_pieces, axis=1))
                high_rows.append(jnp.concatenate(high_pieces, axis=1))
            stacked += low_rows + high_rows
        field = jnp.concatenate(stacked, axis=0).astype(jnp.bfloat16)
        degree = (
            waves[first + slot] + 2 * lax.broadcasted_iota(jnp.int32, (1, half_count), 1)
        ).astype(jnp.float32) + parity
        inside = (degree <= float(wave_count - 1)).astype(jnp.float32)
        ratio = tau_scale * degree * (degree + 1.0) / float(wave_count * (wave_count - 1))
        factor = 1.0 / (1.0 + eig_ref[...] * ratio)
        spectral = jnp.dot(field, legendre, preferred_element_type=jnp.float32)
        spectral = (spectral * inside).astype(jnp.bfloat16)
        levels = modes_in.shape[0]
        solved = []
        for part in range(2):
            column = spectral[part * levels : (part + 1) * levels]
            modal = jnp.dot(modes_in[...], column, preferred_element_type=jnp.float32)
            modal = (modal * factor).astype(jnp.bfloat16)
            solved.append(
                jnp.dot(modes_out[...], modal, preferred_element_type=jnp.float32).astype(
                    jnp.bfloat16
                )
            )
        grid = lax.dot_general(
            jnp.concatenate(solved, axis=0),
            legendre,
            (((1,), (1,)), ((), ())),
            preferred_element_type=jnp.float32,
        )
        for part in range(2):
            for level in range(level_size):
                low_start = part * levels + level * tiles
                high_start = low_start + level_size * tiles
                for pair in range(wave_size // 2):
                    lanes = slice(pair * LANES, (pair + 1) * LANES)
                    low = grid[low_start : low_start + tiles, lanes]
                    high = grid[high_start : high_start + tiles, lanes]
                    a = jnp.where(low_half, low, pltpu.roll(high, LANES // 2, 1))
                    b = jnp.where(low_half, pltpu.roll(low, LANES // 2, 1), high)
                    rows_out[where_rows(2 * pair * level_size + level, part, slot), :] = a
                    rows_out[where_rows((2 * pair + 1) * level_size + level, part, slot), :] = b
        return carry

    lax.fori_loop(0, group, one_slot, 0)

    def gather(index, carry):
        place, part = index // 2, index % 2
        for tile in range(tiles):
            parts = []
            for eight in range(eights):
                start = pl.multiple_of(((index * eights + eight) * tiles + tile) * 8, 8)
                parts.append(rows_out[pl.ds(start, 8), :])
            out[place, part, :, tile * LANES : (tile + 1) * LANES] = jnp.concatenate(
                parts, axis=0
            ).astype(out.dtype)
        return carry

    lax.fori_loop(0, places * 2, gather, 0)


def columns_fused(pieces, legendre, waves, scalars, eig_rates, modes, sizes):
    wave_size, level_size, _, group, tiles, half_count, _, first = sizes
    places = wave_size * level_size
    half_rows = legendre.shape[1]
    width = tiles * LANES
    levels = modes[0].shape[0]
    flat = [piece for place in pieces for piece in place]
    whole = lambda shape: pl.BlockSpec(shape, lambda i: (0,) * len(shape))
    scratch = pltpu.VMEM((places * 2 * group * tiles, LANES), jnp.float32)
    values = places * 2 * group * width
    return pl.pallas_call(
        functools.partial(column_kernel, sizes),
        out_shape=jax.ShapeDtypeStruct((places, 2, group, width), jnp.bfloat16),
        grid=(1,),
        in_specs=[
            pl.BlockSpec(memory_space=pltpu.SMEM),
            pl.BlockSpec(memory_space=pltpu.SMEM),
            whole((levels, 1)),
            whole((levels, levels)),
            whole((levels, levels)),
            pl.BlockSpec((group, half_rows, half_count), lambda i: (first // group, 0, 0)),
        ]
        + [whole(piece.shape) for piece in flat],
        out_specs=whole((places, 2, group, width)),
        scratch_shapes=[scratch, scratch],
        compiler_params=pltpu.CompilerParams(vmem_limit_bytes=40 * 2**20),
        cost_estimate=pl.CostEstimate(
            flops=values * half_rows * 6, bytes_accessed=6 * values, transcendentals=0
        ),
    )(waves, scalars, eig_rates[:, None], *modes, legendre, *flat)


def columns_plain(mirrored, legendre, waves, parity, eig_rates, modes_in, modes_out, sizes):
    wave_size, level_size, count, first, wave_count = sizes
    levels = modes_in.shape[0]
    half_rows, half_count = legendre.shape[1:]
    local_levels, rows_here = levels // level_size, half_rows // wave_size
    shape = mirrored.shape
    mirrored = mirrored.reshape(wave_size, level_size, 2, count, local_levels, rows_here)
    field = mirrored.transpose(3, 2, 1, 4, 0, 5).reshape(count, 2, levels, half_rows)
    table = legendre[first : first + count]
    degree = (
        waves[first : first + count, None] + 2 * jnp.arange(half_count, dtype=jnp.int32)[None, :]
    ).astype(jnp.float32) + parity
    inside = (degree <= float(wave_count - 1)).astype(jnp.float32)
    ratio = tau_scale * degree * (degree + 1.0) / float(wave_count * (wave_count - 1))
    factor = 1.0 / (1.0 + ratio[:, None, :] * eig_rates[None, :, None])
    spectral = jnp.einsum("sclr,srj->sclj", field, table, preferred_element_type=jnp.float32)
    spectral = (spectral * inside[:, None, None, :]).astype(jnp.bfloat16)
    modal = jnp.einsum("kl,sclj->sckj", modes_in, spectral, preferred_element_type=jnp.float32)
    modal = (modal * factor[:, None, :, :]).astype(jnp.bfloat16)
    solved = jnp.einsum(
        "lk,sckj->sclj", modes_out, modal, preferred_element_type=jnp.float32
    ).astype(jnp.bfloat16)
    grid = jnp.einsum("sclj,srj->sclr", solved, table, preferred_element_type=jnp.float32)
    grid = grid.astype(jnp.bfloat16)
    grid = grid.reshape(count, 2, level_size, local_levels, wave_size, rows_here)
    return grid.transpose(4, 2, 1, 0, 3, 5).reshape(shape)


def inverse_kernel(pieces, *refs):
    table, out = refs[pieces], refs[-1]
    coeffs = jnp.concatenate([ref[...] for ref in refs[:pieces]], axis=0)
    current = lax.dot_general(
        coeffs, table[...], (((0,), (0,)), ((), ())), preferred_element_type=jnp.float32
    )
    out[...] = current.astype(out.dtype).reshape(out.shape)


def inverse_fourier(pieces, table, current, shape, start, levels):
    _, rows_here, lon_count = shape
    block = level_block(levels, rows_here)
    width = block * rows_here
    full = shape[0] * rows_here
    first = start // block
    specs = [
        pl.BlockSpec(
            (piece.shape[0], width),
            (lambda i: (0, first + i)) if piece.shape[1] == full else (lambda i: (0, i)),
        )
        for piece in pieces
    ]
    table_spec = pl.BlockSpec(table.shape, lambda i: (0, 0), pipeline_mode=pl.Buffered(1))
    operands = list(pieces) + [table]
    specs.append(table_spec)
    aliases = {}
    if current is not None:
        aliases = {len(operands): 0}
        operands.append(current)
        specs.append(pl.BlockSpec(memory_space=pl.ANY))
    return pl.pallas_call(
        functools.partial(inverse_kernel, len(pieces)),
        out_shape=jax.ShapeDtypeStruct(shape, jnp.bfloat16),
        grid=(levels // block,),
        in_specs=specs,
        out_specs=pl.BlockSpec((block, rows_here, lon_count), lambda i: (first + i, 0, 0)),
        input_output_aliases=aliases,
        compiler_params=pltpu.CompilerParams(vmem_limit_bytes=40 * 2**20),
        cost_estimate=pl.CostEstimate(
            flops=2 * table.shape[0] * levels * rows_here * lon_count,
            bytes_accessed=2 * levels * rows_here * (table.shape[0] + lon_count),
            transcendentals=0,
        ),
    )(*operands)


def shards(grid_state, legendre, wave_order, lat_order, eig_rates, modes_in, modes_out):
    out_shape = grid_state.shape
    local_levels, _, rows_here, lon_count = out_shape
    wave_size = lax.axis_size("wave")
    level_size = lax.axis_size("level")
    places = wave_size * level_size
    half_rows = lat_order.shape[0]
    wave_count = wave_order.shape[0]
    narrow, half_count = legendre.shape[0], legendre.shape[3]
    chunks = min(CHUNKS, narrow)
    count = narrow // chunks
    width = local_levels * rows_here
    fused = (
        places <= DIRECT_LIMIT
        and rows_here * 2 == LANES
        and wave_size % 2 == 0
        and count % 16 == 0
        and local_levels % 8 == 0
    )
    splits = SPLITS if fused else 1
    parity = lax.axis_index("fld")
    wave_place = lax.axis_index("wave")
    level_place = lax.axis_index("level")
    legendre = legendre.reshape(narrow, half_rows, half_count)
    grid_state = grid_state.reshape(local_levels, rows_here, lon_count)
    hemi_sign = 1.0 - 2.0 * parity.astype(jnp.float32)
    lat_rows = lax.dynamic_slice_in_dim(lat_order, wave_place * rows_here, rows_here)
    sine = jnp.sin((lat_rows.astype(jnp.float32) + 0.5) * (math.pi / (2.0 * half_rows)))
    coupling = (0.5 * hemi_sign * sine)[:, None]
    place = wave_place * level_size + level_place
    waves = lax.dynamic_slice_in_dim(wave_order, place * narrow, narrow)

    ids = wave_order.reshape(wave_size, level_size, chunks, count)
    if fused:
        ids = rolled(ids, wave_place)
        ids = jnp.swapaxes(rolled(jnp.swapaxes(ids, 0, 1), level_place), 0, 1)
    ids = ids.reshape(places, chunks, count).transpose(1, 0, 2)
    ids = jnp.broadcast_to(ids[:, :, None, :], (chunks, places, 2, count)).reshape(chunks, -1)
    quarter = jnp.broadcast_to(
        (jnp.arange(2, dtype=jnp.int32) * (lon_count // 4))[None, :, None], (places, 2, count)
    ).reshape(-1)
    tables = [fourier_table(ids[0], quarter, lon_count, 1)]
    if chunks > 1:
        tables.append(
            fourier_table(
                ids[1:].reshape(-1), jnp.tile(quarter, chunks - 1), lon_count, chunks - 1
            )
        )
    table = jnp.concatenate(tables, axis=0)
    places_list = [(wave, level) for wave in range(wave_size) for level in range(level_size)]
    height = 2 * count

    if not fused:
        parts = fourier(grid_state, coupling, table, chunks, 0, local_levels)
        returned = []
        for chunk in range(chunks):
            value = parts[chunk]
            mirrored = (
                partner(value, "fld").astype(jnp.float32) + hemi_sign * value.astype(jnp.float32)
            ).astype(jnp.bfloat16)
            mirrored = lax.all_to_all(
                mirrored.reshape(places, height, width), EXCHANGE_AXES, 0, 0, tiled=True
            )
            grid = columns_plain(
                mirrored.reshape(wave_size, level_size, 2, count, width),
                legendre,
                waves,
                parity.astype(jnp.float32),
                eig_rates,
                modes_in,
                modes_out,
                (wave_size, level_size, count, chunk * count, wave_count),
            ).reshape(places, height, width)
            hemi = (
                0.5
                * (partner(grid, "fld").astype(jnp.float32) + hemi_sign * grid.astype(jnp.float32))
            ).astype(jnp.bfloat16)
            hemi = lax.all_to_all(hemi, EXCHANGE_AXES, 0, 0, tiled=True)
            returned.append(hemi.reshape(places * height, width))
        coeffs = [jnp.concatenate(returned, axis=0)]
        current = inverse_fourier(coeffs, table, None, grid_state.shape, 0, local_levels)
        return current.reshape(out_shape)

    tiles = width // LANES
    level_index = jnp.arange(local_levels, dtype=jnp.int32).reshape(tiles, 2).T
    from_level = (level_place - jnp.arange(level_size, dtype=jnp.int32)) % level_size
    order = (from_level[None, :, None] * local_levels + level_index[:, None, :]).reshape(-1)
    modes = (jnp.take(modes_in, order, axis=1), jnp.take(modes_out, order, axis=0))
    scalars = jnp.concatenate(
        [(wave_place - jnp.arange(wave_size, dtype=jnp.int32)) % wave_size, parity[None]]
    )

    def send(value):
        other = partner(value, "fld")
        arrived = []
        for index, (wave, level) in enumerate(places_list):
            rows = slice(index * height, (index + 1) * height)
            mirrored = (
                other[rows].astype(jnp.float32) + hemi_sign * value[rows].astype(jnp.float32)
            ).astype(jnp.bfloat16)
            moved = shift_places(mirrored, wave, level)
            arrived.append(moved.reshape(2, count, -1))
        return arrived

    some = local_levels // splits
    forward = [[] for _ in range(chunks)]
    for split in range(splits):
        (value,) = fourier(grid_state, coupling, tables[0], 1, split * some, some)
        forward[0].append(send(value))
    rest = fourier(grid_state, coupling, tables[1], chunks - 1, 0, local_levels)
    for chunk in range(1, chunks):
        forward[chunk].append(send(rest[chunk - 1]))

    returned, last = [], []
    for chunk in range(chunks):
        pieces = [list(piece) for piece in zip(*forward[chunk])]
        sizes = (
            wave_size,
            level_size,
            len(pieces[0]),
            count,
            tiles,
            half_count,
            wave_count,
            chunk * count,
        )
        grid = columns_fused(pieces, legendre, waves, scalars, eig_rates, modes, sizes)
        grid = grid.reshape(places, height, width)
        other = partner(grid, "fld")
        cuts = splits if chunk == chunks - 1 else 1
        for cut in range(cuts):
            lanes = slice(cut * (width // cuts), (cut + 1) * (width // cuts))
            back = []
            for index, (wave, level) in enumerate(places_list):
                hemi = (
                    0.5
                    * (
                        other[index, :, lanes].astype(jnp.float32)
                        + hemi_sign * grid[index, :, lanes].astype(jnp.float32)
                    )
                ).astype(jnp.bfloat16)
                back.append(
                    shift_places(
                        hemi, (wave_size - wave) % wave_size, (level_size - level) % level_size
                    )
                )
            (returned if cuts == 1 else last).append(back)
    earlier = [piece for back in returned for piece in back]
    current = None
    for split in range(splits):
        current = inverse_fourier(
            earlier + last[split], table, current, grid_state.shape, split * some, some
        )
    return current.reshape(out_shape)


def solution(mesh):
    placed = (
        P(("member", "level"), "fld", "wave", None),
        P(("wave", "level"), "fld", None, None),
        P(),
        P(),
        P(),
        P(),
        P(),
    )
    return jax.shard_map(
        shards,
        mesh=mesh,
        in_specs=placed,
        out_specs=P(("member", "level"), "fld", "wave", None),
        check_vma=False,
    )
```

```python
import functools
import math

import jax
import jax.numpy as jnp
from jax import lax
from jax.experimental import pallas as pl
from jax.experimental.pallas import tpu as pltpu
from jax.sharding import PartitionSpec as P


tau_scale = 2.0
LANES = 128
CHUNKS = 4
WHOLE_SENDS = (0, 2)
WHOLE_BACKS = (0, 2)
DIRECT_LIMIT = 16
EXCHANGE_AXES = ("wave", "level")


def partner(value, axis):
    pairs = [(source, source ^ 1) for source in range(lax.axis_size(axis))]
    return lax.ppermute(value, axis, pairs)


def shift_places(value, wave_shift, level_shift):
    if wave_shift == 0 and level_shift == 0:
        return value
    waves, levels = lax.axis_size("wave"), lax.axis_size("level")
    pairs = []
    for wave in range(waves):
        for level in range(levels):
            target = (wave + wave_shift) % waves * levels + (level + level_shift) % levels
            pairs.append((wave * levels + level, target))
    return lax.ppermute(value, EXCHANGE_AXES, pairs)


def rolled(value, start):
    return lax.dynamic_slice_in_dim(
        jnp.concatenate([value, value], axis=0), start, value.shape[0], axis=0
    )


def phase_of(product, period):
    return (product % period).astype(jnp.float32) * (2.0 * math.pi / period)


def level_block(levels, rows_here):
    return 8 if levels % 8 == 0 and 8 * rows_here % LANES == 0 else levels


def fourier_kernel(scale, grid_ref, coupling, high_cos, high_sin, low_cos, low_sin, out, table):
    levels, rows, lon_count = grid_ref.shape

    @pl.when(pl.program_id(0) == 0)
    def _():
        for block in range(lon_count // LANES):
            values = (
                high_cos[:, block : block + 1] * low_cos[...]
                - high_sin[:, block : block + 1] * low_sin[...]
            )
            table[:, block * LANES : (block + 1) * LANES] = (values * scale).astype(table.dtype)

    field = grid_ref[...].astype(jnp.float32)
    forcing = (field + coupling[...][None] * jnp.tanh(field)).astype(jnp.bfloat16)
    forcing = forcing.reshape(levels * rows, lon_count)
    out[...] = lax.dot_general(
        table[...], forcing, (((1,), (1,)), ((), ())), preferred_element_type=jnp.float32
    ).astype(out.dtype)


def fourier(grid_state, coupling, ids, quarter):
    levels, rows_here, lon_count = grid_state.shape
    height = ids.shape[0]
    blocks = lon_count // LANES
    high = phase_of(
        ids[:, None] * LANES * jnp.arange(blocks, dtype=jnp.int32)[None, :] + quarter[:, None],
        lon_count,
    )
    low = phase_of(ids[:, None] * jnp.arange(LANES, dtype=jnp.int32)[None, :], lon_count)
    block = level_block(levels, rows_here)
    width = levels * rows_here
    whole = lambda *shape: pl.BlockSpec(shape, lambda i: (0,) * len(shape))
    return pl.pallas_call(
        functools.partial(fourier_kernel, math.sqrt(2.0 / lon_count)),
        out_shape=[
            jax.ShapeDtypeStruct((height, width), jnp.bfloat16),
            jax.ShapeDtypeStruct((height, lon_count), jnp.bfloat16),
        ],
        grid=(levels // block,),
        in_specs=[
            pl.BlockSpec((block, rows_here, lon_count), lambda i: (i, 0, 0)),
            whole(rows_here, 1),
            whole(height, blocks),
            whole(height, blocks),
            whole(height, LANES),
            whole(height, LANES),
        ],
        out_specs=[
            pl.BlockSpec((height, block * rows_here), lambda i: (0, i)),
            whole(height, lon_count),
        ],
        compiler_params=pltpu.CompilerParams(vmem_limit_bytes=56 * 2**20),
        cost_estimate=pl.CostEstimate(
            flops=2 * height * width * lon_count,
            bytes_accessed=2 * (width * lon_count + height * (width + lon_count)),
            transcendentals=width * lon_count,
        ),
    )(grid_state, coupling, jnp.cos(high), jnp.sin(high), jnp.cos(low), jnp.sin(low))


def inverse_kernel(pieces, tables, *refs):
    out = refs[-1]
    coeffs = jnp.concatenate([ref[...] for ref in refs[:pieces]], axis=0)
    table = jnp.concatenate([ref[...] for ref in refs[pieces : pieces + tables]], axis=0)
    current = lax.dot_general(
        coeffs, table, (((0,), (0,)), ((), ())), preferred_element_type=jnp.float32
    ).reshape(out.shape)
    if len(refs) > pieces + tables + 1:
        current = current + refs[pieces + tables][...]
    out[...] = current.astype(out.dtype)


def inverse_fourier(pieces, tables, shape, dtype, partial=None):
    levels, rows_here, lon_count = shape
    block = level_block(levels, rows_here)
    height = sum(piece.shape[0] for piece in pieces)
    grid_spec = pl.BlockSpec((block, rows_here, lon_count), lambda i: (i, 0, 0))
    partials = [] if partial is None else [partial]
    return pl.pallas_call(
        functools.partial(inverse_kernel, len(pieces), len(tables)),
        out_shape=jax.ShapeDtypeStruct(shape, dtype),
        grid=(levels // block,),
        in_specs=[
            pl.BlockSpec((piece.shape[0], block * rows_here), lambda i: (0, i)) for piece in pieces
        ]
        + [
            pl.BlockSpec(table.shape, lambda i: (0, 0), pipeline_mode=pl.Buffered(1))
            for table in tables
        ]
        + [grid_spec] * len(partials),
        out_specs=grid_spec,
        compiler_params=pltpu.CompilerParams(vmem_limit_bytes=40 * 2**20),
        cost_estimate=pl.CostEstimate(
            flops=2 * height * levels * rows_here * lon_count,
            bytes_accessed=levels * rows_here * (2 * height + 6 * lon_count),
            transcendentals=0,
        ),
    )(*pieces, *tables, *partials)


def column_kernel(sizes, waves, scalars, eig_ref, modes_in, modes_out, table, *refs):
    wave_size, level_size, group, tiles, half_count, wave_count, first = sizes
    places = wave_size * level_size
    pieces, (out, rows_in, rows_out) = refs[:-3], refs[-3:]
    eights = group // 8
    rows_here = LANES // 2
    parity = scalars[wave_size].astype(jnp.float32)
    low_half = lax.broadcasted_iota(jnp.int32, (tiles, LANES), 1) < LANES // 2

    def spread(start, part, value):
        for tile in range(tiles):
            for eight in range(eights):
                row = ((start * 2 + part) * eights + eight) * tiles + tile
                rows_in[pl.ds(pl.multiple_of(row * 8, 8), 8), :] = value(tile)[
                    eight * 8 : (eight + 1) * 8
                ]

    if len(pieces) == 2:
        own, other = pieces
        sign = 1.0 - 2.0 * parity

        def combined(index, carry):
            place, part = index // 2, index % 2

            def value(tile):
                lanes = slice(tile * LANES, (tile + 1) * LANES)
                both = other[place, part, :, lanes].astype(jnp.float32) + sign * own[
                    place, part, :, lanes
                ].astype(jnp.float32)
                return both.astype(jnp.bfloat16).astype(jnp.float32)

            spread(place, part, value)
            return carry

        lax.fori_loop(0, places * 2, combined, 0)
    else:
        for place, piece in enumerate(pieces):

            def arrived(part, carry, place=place, piece=piece):
                def value(tile):
                    return piece[part, :, tile * LANES : (tile + 1) * LANES].astype(jnp.float32)

                spread(place, part, value)
                return carry

            lax.fori_loop(0, 2, arrived, 0)

    def where_rows(place, part, slot):
        eight, within = slot // 8, slot % 8
        return pl.ds((((place * 2 + part) * eights + eight) * tiles) * 8 + within, tiles, 8)

    def one_slot(slot, carry):
        legendre = jnp.concatenate(
            [
                table[slot, pl.ds(pl.multiple_of(scalars[wave] * rows_here, rows_here), rows_here), :]
                for wave in range(wave_size)
            ],
            axis=0,
        )
        stacked = []
        for part in range(2):
            low_rows, high_rows = [], []
            for level in range(level_size):
                low_pieces, high_pieces = [], []
                for pair in range(wave_size // 2):
                    a = rows_in[where_rows(2 * pair * level_size + level, part, slot), :]
                    b = rows_in[where_rows((2 * pair + 1) * level_size + level, part, slot), :]
                    low_pieces.append(jnp.where(low_half, a, pltpu.roll(b, LANES // 2, 1)))
                    high_pieces.append(jnp.where(low_half, pltpu.roll(a, LANES // 2, 1), b))
                low_rows.append(jnp.concatenate(low_pieces, axis=1))
                high_rows.append(jnp.concatenate(high_pieces, axis=1))
            stacked += low_rows + high_rows
        field = jnp.concatenate(stacked, axis=0).astype(jnp.bfloat16)
        degree = (
            waves[first + slot] + 2 * lax.broadcasted_iota(jnp.int32, (1, half_count), 1)
        ).astype(jnp.float32) + parity
        inside = (degree <= float(wave_count - 1)).astype(jnp.float32)
        ratio = tau_scale * degree * (degree + 1.0) / float(wave_count * (wave_count - 1))
        factor = 1.0 / (1.0 + eig_ref[...] * ratio)
        spectral = jnp.dot(field, legendre, preferred_element_type=jnp.float32)
        spectral = (spectral * inside).astype(jnp.bfloat16)
        levels = modes_in.shape[0]
        solved = []
        for part in range(2):
            column = spectral[part * levels : (part + 1) * levels]
            modal = jnp.dot(modes_in[...], column, preferred_element_type=jnp.float32)
            modal = (modal * factor).astype(jnp.bfloat16)
            solved.append(
                jnp.dot(modes_out[...], modal, preferred_element_type=jnp.float32).astype(
                    jnp.bfloat16
                )
            )
        grid = lax.dot_general(
            jnp.concatenate(solved, axis=0),
            legendre,
            (((1,), (1,)), ((), ())),
            preferred_element_type=jnp.float32,
        )
        for part in range(2):
            for level in range(level_size):
                low_start = part * levels + level * tiles
                high_start = low_start + level_size * tiles
                for pair in range(wave_size // 2):
                    lanes = slice(pair * LANES, (pair + 1) * LANES)
                    low = grid[low_start : low_start + tiles, lanes]
                    high = grid[high_start : high_start + tiles, lanes]
                    a = jnp.where(low_half, low, pltpu.roll(high, LANES // 2, 1))
                    b = jnp.where(low_half, pltpu.roll(low, LANES // 2, 1), high)
                    rows_out[where_rows(2 * pair * level_size + level, part, slot), :] = a
                    rows_out[where_rows((2 * pair + 1) * level_size + level, part, slot), :] = b
        return carry

    lax.fori_loop(0, group, one_slot, 0)

    def gather(index, carry):
        place, part = index // 2, index % 2
        for tile in range(tiles):
            parts = []
            for eight in range(eights):
                start = pl.multiple_of(((index * eights + eight) * tiles + tile) * 8, 8)
                parts.append(rows_out[pl.ds(start, 8), :])
            out[place, part, :, tile * LANES : (tile + 1) * LANES] = jnp.concatenate(
                parts, axis=0
            ).astype(out.dtype)
        return carry

    lax.fori_loop(0, places * 2, gather, 0)


def columns_fused(pieces, legendre, waves, scalars, eig_rates, modes, sizes):
    wave_size, level_size, group, tiles, half_count, _, first = sizes
    places = wave_size * level_size
    half_rows = legendre.shape[1]
    width = tiles * LANES
    levels = modes[0].shape[0]
    whole = lambda shape: pl.BlockSpec(shape, lambda i: (0,) * len(shape))
    scratch = pltpu.VMEM((places * 2 * group * tiles, LANES), jnp.float32)
    values = places * 2 * group * width
    return pl.pallas_call(
        functools.partial(column_kernel, sizes),
        out_shape=jax.ShapeDtypeStruct((places, 2, group, width), jnp.bfloat16),
        grid=(1,),
        in_specs=[
            pl.BlockSpec(memory_space=pltpu.SMEM),
            pl.BlockSpec(memory_space=pltpu.SMEM),
            whole((levels, 1)),
            whole((levels, levels)),
            whole((levels, levels)),
            pl.BlockSpec((group, half_rows, half_count), lambda i: (first // group, 0, 0)),
        ]
        + [whole(piece.shape) for piece in pieces],
        out_specs=whole((places, 2, group, width)),
        scratch_shapes=[scratch, scratch],
        compiler_params=pltpu.CompilerParams(vmem_limit_bytes=40 * 2**20),
        cost_estimate=pl.CostEstimate(
            flops=values * half_rows * 6, bytes_accessed=6 * values, transcendentals=0
        ),
    )(waves, scalars, eig_rates[:, None], *modes, legendre, *pieces)


def columns_plain(mirrored, legendre, waves, parity, eig_rates, modes_in, modes_out, sizes):
    wave_size, level_size, count, first, wave_count = sizes
    levels = modes_in.shape[0]
    half_rows, half_count = legendre.shape[1:]
    local_levels, rows_here = levels // level_size, half_rows // wave_size
    shape = mirrored.shape
    mirrored = mirrored.reshape(wave_size, level_size, 2, count, local_levels, rows_here)
    field = mirrored.transpose(3, 2, 1, 4, 0, 5).reshape(count, 2, levels, half_rows)
    table = legendre[first : first + count]
    degree = (
        waves[first : first + count, None] + 2 * jnp.arange(half_count, dtype=jnp.int32)[None, :]
    ).astype(jnp.float32) + parity
    inside = (degree <= float(wave_count - 1)).astype(jnp.float32)
    ratio = tau_scale * degree * (degree + 1.0) / float(wave_count * (wave_count - 1))
    factor = 1.0 / (1.0 + ratio[:, None, :] * eig_rates[None, :, None])
    spectral = jnp.einsum("sclr,srj->sclj", field, table, preferred_element_type=jnp.float32)
    spectral = (spectral * inside[:, None, None, :]).astype(jnp.bfloat16)
    modal = jnp.einsum("kl,sclj->sckj", modes_in, spectral, preferred_element_type=jnp.float32)
    modal = (modal * factor[:, None, :, :]).astype(jnp.bfloat16)
    solved = jnp.einsum(
        "lk,sckj->sclj", modes_out, modal, preferred_element_type=jnp.float32
    ).astype(jnp.bfloat16)
    grid = jnp.einsum("sclj,srj->sclr", solved, table, preferred_element_type=jnp.float32)
    grid = grid.astype(jnp.bfloat16)
    grid = grid.reshape(count, 2, level_size, local_levels, wave_size, rows_here)
    return grid.transpose(4, 2, 1, 0, 3, 5).reshape(shape)


def shards(grid_state, legendre, wave_order, lat_order, eig_rates, modes_in, modes_out):
    out_shape = grid_state.shape
    local_levels, _, rows_here, lon_count = out_shape
    wave_size = lax.axis_size("wave")
    level_size = lax.axis_size("level")
    places = wave_size * level_size
    half_rows = lat_order.shape[0]
    wave_count = wave_order.shape[0]
    narrow, half_count = legendre.shape[0], legendre.shape[3]
    chunks = min(CHUNKS, narrow)
    count = narrow // chunks
    height = 2 * count
    width = local_levels * rows_here
    direct = (
        places <= DIRECT_LIMIT
        and rows_here * 2 == LANES
        and wave_size % 2 == 0
        and count % 16 == 0
    )
    parity = lax.axis_index("fld")
    wave_place = lax.axis_index("wave")
    level_place = lax.axis_index("level")
    place = wave_place * level_size + level_place
    legendre = legendre.reshape(narrow, half_rows, half_count)
    grid_state = grid_state.reshape(local_levels, rows_here, lon_count)
    hemi_sign = 1.0 - 2.0 * parity.astype(jnp.float32)
    lat_rows = lax.dynamic_slice_in_dim(lat_order, wave_place * rows_here, rows_here)
    sine = jnp.sin((lat_rows.astype(jnp.float32) + 0.5) * (math.pi / (2.0 * half_rows)))
    coupling = (0.5 * hemi_sign * sine)[:, None]
    waves = lax.dynamic_slice_in_dim(wave_order, place * narrow, narrow)
    quarter = jnp.broadcast_to(
        (jnp.arange(2, dtype=jnp.int32) * (lon_count // 4))[None, :, None], (places, 2, count)
    ).reshape(-1)
    fixed = wave_order.reshape(wave_size, level_size, chunks, count)
    turned = rolled(fixed, wave_place)
    turned = jnp.swapaxes(rolled(jnp.swapaxes(turned, 0, 1), level_place), 0, 1)

    def slot_ids(order, chunk):
        ids = order[:, :, chunk].reshape(places, 1, count)
        return jnp.broadcast_to(ids, (places, 2, count)).reshape(-1)

    def exchange(value):
        return lax.all_to_all(value, EXCHANGE_AXES, split_axis=0, concat_axis=0, tiled=True)

    def joined(other, own, scale):
        both = scale * (other.astype(jnp.float32) + hemi_sign * own.astype(jnp.float32))
        return both.astype(jnp.bfloat16)

    if not direct:
        returned, tables = [], []
        for chunk in range(chunks):
            value, table = fourier(grid_state, coupling, slot_ids(fixed, chunk), quarter)
            tables.append(table)
            own = exchange(value.reshape(places, height, width))
            mirrored = joined(partner(own, "fld"), own, 1.0)
            grid = columns_plain(
                mirrored.reshape(wave_size, level_size, 2, count, width),
                legendre,
                waves,
                parity.astype(jnp.float32),
                eig_rates,
                modes_in,
                modes_out,
                (wave_size, level_size, count, chunk * count, wave_count),
            ).reshape(places, height, width)
            hemi = exchange(joined(partner(grid, "fld"), grid, 0.5))
            returned.append(hemi.reshape(places * height, width))
        current = inverse_fourier(returned, tables, grid_state.shape, jnp.bfloat16)
        return current.reshape(out_shape)

    tiles = width // LANES
    level_index = jnp.arange(local_levels, dtype=jnp.int32).reshape(tiles, 2).T
    sources = []
    for is_turned in (0, 1):
        shift = jnp.arange(level_size, dtype=jnp.int32)
        from_level = (level_place - shift) % level_size if is_turned else shift
        order = (from_level[None, :, None] * local_levels + level_index[:, None, :]).reshape(-1)
        shift = jnp.arange(wave_size, dtype=jnp.int32)
        from_wave = (wave_place - shift) % wave_size if is_turned else shift
        sources.append(
            (
                jnp.concatenate([from_wave, parity[None]]),
                (jnp.take(modes_in, order, axis=1), jnp.take(modes_out, order, axis=0)),
            )
        )
    shifts = [(wave, level) for wave in range(wave_size) for level in range(level_size)]

    arrived, tables = [], []
    for chunk in range(chunks):
        is_whole = chunk in WHOLE_SENDS
        value, table = fourier(
            grid_state, coupling, slot_ids(fixed if is_whole else turned, chunk), quarter
        )
        tables.append(table)
        if is_whole:
            arrived.append([exchange(value.reshape(places, 2, count, width))])
            continue
        other = partner(value, "fld")
        pieces = []
        for index, (wave, level) in enumerate(shifts):
            rows = slice(index * height, (index + 1) * height)
            mirrored = joined(other[rows], value[rows], 1.0)
            piece = shift_places(mirrored, wave, level)
            pieces.append(piece.reshape(2, count, width))
        arrived.append(pieces)

    returned = []
    for chunk in range(chunks):
        is_whole = chunk in WHOLE_SENDS
        pieces = arrived[chunk]
        if is_whole:
            pieces = [pieces[0], partner(pieces[0], "fld")]
        scalars, modes = sources[0 if is_whole else 1]
        sizes = (wave_size, level_size, count, tiles, half_count, wave_count, chunk * count)
        grid = columns_fused(pieces, legendre, waves, scalars, eig_rates, modes, sizes)
        grid = grid.reshape(places, height, width)
        other = partner(grid, "fld")
        if chunk in WHOLE_BACKS:
            hemi = exchange(joined(other, grid, 0.5))
            returned.append([hemi.reshape(places * height, width)])
            continue
        pieces = []
        for index, (wave, level) in enumerate(shifts):
            hemi = joined(other[index], grid[index], 0.5)
            pieces.append(
                shift_places(hemi, (wave_size - wave) % wave_size, (level_size - level) % level_size)
            )
        returned.append(pieces)
    half = chunks // 2
    flat = lambda groups: [piece for group in groups for piece in group]
    partial = inverse_fourier(flat(returned[:half]), tables[:half], grid_state.shape, jnp.float32)
    current = inverse_fourier(
        flat(returned[half:]), tables[half:], grid_state.shape, jnp.bfloat16, partial
    )
    return current.reshape(out_shape)


def solution(mesh):
    placed = (
        P(("member", "level"), "fld", "wave", None),
        P(("wave", "level"), "fld", None, None),
        P(),
        P(),
        P(),
        P(),
        P(),
    )
    return jax.shard_map(
        shards,
        mesh=mesh,
        in_specs=placed,
        out_specs=P(("member", "level"), "fld", "wave", None),
        check_vma=False,
    )
```

```python
import functools
import math

import jax
import jax.numpy as jnp
from jax import lax
from jax.experimental import pallas as pl
from jax.experimental.pallas import tpu as pltpu
from jax.sharding import PartitionSpec as P


tau_scale = 2.0
LANES = 128
CHUNKS = 4
WHOLE_CHUNKS = (0, 2)
DIRECT_LIMIT = 16
EXCHANGE_AXES = ("wave", "level")


def partner(value, axis):
    pairs = [(source, source ^ 1) for source in range(lax.axis_size(axis))]
    return lax.ppermute(value, axis, pairs)


def shift_places(value, wave_shift, level_shift):
    if wave_shift == 0 and level_shift == 0:
        return value
    waves, levels = lax.axis_size("wave"), lax.axis_size("level")
    pairs = []
    for wave in range(waves):
        for level in range(levels):
            target = (wave + wave_shift) % waves * levels + (level + level_shift) % levels
            pairs.append((wave * levels + level, target))
    return lax.ppermute(value, EXCHANGE_AXES, pairs)


def rolled(value, start):
    return lax.dynamic_slice_in_dim(
        jnp.concatenate([value, value], axis=0), start, value.shape[0], axis=0
    )


def level_block(levels, rows_here, most):
    whole = levels % most == 0 and most * rows_here % LANES == 0
    return most if whole else levels


def write_table(ids, quarter, table):
    rows, lon_count = table.shape
    scale = math.sqrt(2.0 / lon_count)
    wave = ids[...].astype(jnp.float32)
    lane = lax.broadcasted_iota(jnp.int32, (rows, LANES), 1).astype(jnp.float32)

    def angle(steps):
        steps = steps - lon_count * jnp.floor(steps * (1.0 / lon_count))
        return steps * (2.0 * math.pi / lon_count)

    low = angle(wave * lane)
    high = angle(wave * lane * float(LANES) + quarter[...].astype(jnp.float32))
    low_cos, low_sin = jnp.cos(low) * scale, jnp.sin(low) * scale
    high_cos, high_sin = jnp.cos(high), jnp.sin(high)
    for block in range(lon_count // LANES):
        values = (
            high_cos[:, block : block + 1] * low_cos - high_sin[:, block : block + 1] * low_sin
        )
        table[:, block * LANES : (block + 1) * LANES] = values.astype(table.dtype)


def fourier_kernel(half_rows, sign_ref, grid_ref, lat_rows, ids, quarter, out, table):
    levels, rows, lon_count = grid_ref.shape

    @pl.when(pl.program_id(0) == 0)
    def _():
        write_table(ids, quarter, table)

    latitude = (lat_rows[...].astype(jnp.float32) + 0.5) * (math.pi / (2.0 * half_rows))
    coupling = 0.5 * sign_ref[0] * jnp.sin(latitude)
    field = grid_ref[...].astype(jnp.float32)
    forcing = (field + coupling[None] * jnp.tanh(field)).astype(jnp.bfloat16)
    forcing = forcing.reshape(levels * rows, lon_count)
    out[...] = lax.dot_general(
        table[...], forcing, (((1,), (1,)), ((), ())), preferred_element_type=jnp.float32
    ).astype(out.dtype)


def fourier(grid_state, sign, lat_rows, half_rows, ids, quarter):
    levels, rows_here, lon_count = grid_state.shape
    height = ids.shape[0]
    block = level_block(levels, rows_here, 16)
    width = levels * rows_here
    whole = lambda *shape: pl.BlockSpec(shape, lambda i: (0,) * len(shape))
    return pl.pallas_call(
        functools.partial(fourier_kernel, half_rows),
        out_shape=[
            jax.ShapeDtypeStruct((height, width), jnp.bfloat16),
            jax.ShapeDtypeStruct((height, lon_count), jnp.bfloat16),
        ],
        grid=(levels // block,),
        in_specs=[
            pl.BlockSpec(memory_space=pltpu.SMEM),
            pl.BlockSpec((block, rows_here, lon_count), lambda i: (i, 0, 0)),
            whole(rows_here, 1),
            whole(height, 1),
            whole(height, 1),
        ],
        out_specs=[
            pl.BlockSpec((height, block * rows_here), lambda i: (0, i)),
            whole(height, lon_count),
        ],
        compiler_params=pltpu.CompilerParams(vmem_limit_bytes=56 * 2**20),
        cost_estimate=pl.CostEstimate(
            flops=2 * height * width * lon_count,
            bytes_accessed=2 * (width * lon_count + height * (width + lon_count)),
            transcendentals=width * lon_count,
        ),
    )(sign[None], grid_state, lat_rows[:, None], ids[:, None], quarter[:, None])


def inverse_kernel(pieces, tables, *refs):
    out = refs[-1]
    coeffs = jnp.concatenate([ref[...] for ref in refs[:pieces]], axis=0)
    table = jnp.concatenate([ref[...] for ref in refs[pieces : pieces + tables]], axis=0)
    current = lax.dot_general(
        coeffs, table, (((0,), (0,)), ((), ())), preferred_element_type=jnp.float32
    )
    out[...] = current.astype(out.dtype).reshape(out.shape)


def inverse_fourier(pieces, tables, current, shape, start, levels):
    _, rows_here, lon_count = shape
    block = level_block(levels, rows_here, 8)
    width = block * rows_here
    full = shape[0] * rows_here
    first = start // block
    height = sum(piece.shape[0] for piece in pieces)
    specs = [
        pl.BlockSpec(
            (piece.shape[0], width),
            (lambda i: (0, first + i)) if piece.shape[1] == full else (lambda i: (0, i)),
        )
        for piece in pieces
    ] + [
        pl.BlockSpec(table.shape, lambda i: (0, 0), pipeline_mode=pl.Buffered(1))
        for table in tables
    ]
    operands = list(pieces) + list(tables)
    aliases = {}
    if current is not None:
        aliases = {len(operands): 0}
        operands.append(current)
        specs.append(pl.BlockSpec(memory_space=pl.ANY))
    return pl.pallas_call(
        functools.partial(inverse_kernel, len(pieces), len(tables)),
        out_shape=jax.ShapeDtypeStruct(shape, jnp.bfloat16),
        grid=(levels // block,),
        in_specs=specs,
        out_specs=pl.BlockSpec((block, rows_here, lon_count), lambda i: (first + i, 0, 0)),
        input_output_aliases=aliases,
        compiler_params=pltpu.CompilerParams(vmem_limit_bytes=40 * 2**20),
        cost_estimate=pl.CostEstimate(
            flops=2 * height * levels * rows_here * lon_count,
            bytes_accessed=2 * levels * rows_here * (height + lon_count),
            transcendentals=0,
        ),
    )(*operands)


def column_kernel(sizes, waves, scalars, eig_ref, modes_in, modes_out, table, *refs):
    wave_size, level_size, group, tiles, half_count, wave_count, first = sizes
    places = wave_size * level_size
    pieces, (out, rows_in, rows_out) = refs[:-3], refs[-3:]
    eights = group // 8
    rows_here = LANES // 2
    parity = scalars[wave_size].astype(jnp.float32)
    low_half = lax.broadcasted_iota(jnp.int32, (tiles, LANES), 1) < LANES // 2

    def spread(start, part, value):
        for tile in range(tiles):
            for eight in range(eights):
                row = ((start * 2 + part) * eights + eight) * tiles + tile
                rows_in[pl.ds(pl.multiple_of(row * 8, 8), 8), :] = value(tile)[
                    eight * 8 : (eight + 1) * 8
                ]

    if len(pieces) == 2:
        own, other = pieces
        sign = 1.0 - 2.0 * parity

        def combined(index, carry):
            place, part = index // 2, index % 2

            def value(tile):
                lanes = slice(tile * LANES, (tile + 1) * LANES)
                both = other[place, part, :, lanes].astype(jnp.float32) + sign * own[
                    place, part, :, lanes
                ].astype(jnp.float32)
                return both.astype(jnp.bfloat16).astype(jnp.float32)

            spread(place, part, value)
            return carry

        lax.fori_loop(0, places * 2, combined, 0)
    else:
        for place, piece in enumerate(pieces):

            def arrived(part, carry, place=place, piece=piece):
                def value(tile):
                    return piece[part, :, tile * LANES : (tile + 1) * LANES].astype(jnp.float32)

                spread(place, part, value)
                return carry

            lax.fori_loop(0, 2, arrived, 0)

    def where_rows(place, part, slot):
        eight, within = slot // 8, slot % 8
        return pl.ds((((place * 2 + part) * eights + eight) * tiles) * 8 + within, tiles, 8)

    def one_slot(slot, carry):
        legendre = jnp.concatenate(
            [
                table[slot, pl.ds(pl.multiple_of(scalars[wave] * rows_here, rows_here), rows_here), :]
                for wave in range(wave_size)
            ],
            axis=0,
        )
        stacked = []
        for part in range(2):
            low_rows, high_rows = [], []
            for level in range(level_size):
                low_pieces, high_pieces = [], []
                for pair in range(wave_size // 2):
                    a = rows_in[where_rows(2 * pair * level_size + level, part, slot), :]
                    b = rows_in[where_rows((2 * pair + 1) * level_size + level, part, slot), :]
                    low_pieces.append(jnp.where(low_half, a, pltpu.roll(b, LANES // 2, 1)))
                    high_pieces.append(jnp.where(low_half, pltpu.roll(a, LANES // 2, 1), b))
                low_rows.append(jnp.concatenate(low_pieces, axis=1))
                high_rows.append(jnp.concatenate(high_pieces, axis=1))
            stacked += low_rows + high_rows
        field = jnp.concatenate(stacked, axis=0).astype(jnp.bfloat16)
        degree = (
            waves[first + slot] + 2 * lax.broadcasted_iota(jnp.int32, (1, half_count), 1)
        ).astype(jnp.float32) + parity
        inside = (degree <= float(wave_count - 1)).astype(jnp.float32)
        ratio = tau_scale * degree * (degree + 1.0) / float(wave_count * (wave_count - 1))
        factor = 1.0 / (1.0 + eig_ref[...] * ratio)
        spectral = jnp.dot(field, legendre, preferred_element_type=jnp.float32)
        spectral = (spectral * inside).astype(jnp.bfloat16)
        levels = modes_in.shape[0]
        solved = []
        for part in range(2):
            column = spectral[part * levels : (part + 1) * levels]
            modal = jnp.dot(modes_in[...], column, preferred_element_type=jnp.float32)
            modal = (modal * factor).astype(jnp.bfloat16)
            solved.append(
                jnp.dot(modes_out[...], modal, preferred_element_type=jnp.float32).astype(
                    jnp.bfloat16
                )
            )
        grid = lax.dot_general(
            jnp.concatenate(solved, axis=0),
            legendre,
            (((1,), (1,)), ((), ())),
            preferred_element_type=jnp.float32,
        )
        for part in range(2):
            for level in range(level_size):
                low_start = part * levels + level * tiles
                high_start = low_start + level_size * tiles
                for pair in range(wave_size // 2):
                    lanes = slice(pair * LANES, (pair + 1) * LANES)
                    low = grid[low_start : low_start + tiles, lanes]
                    high = grid[high_start : high_start + tiles, lanes]
                    a = jnp.where(low_half, low, pltpu.roll(high, LANES // 2, 1))
                    b = jnp.where(low_half, pltpu.roll(low, LANES // 2, 1), high)
                    rows_out[where_rows(2 * pair * level_size + level, part, slot), :] = a
                    rows_out[where_rows((2 * pair + 1) * level_size + level, part, slot), :] = b
        return carry

    lax.fori_loop(0, group, one_slot, 0)

    def gather(index, carry):
        place, part = index // 2, index % 2
        for tile in range(tiles):
            parts = []
            for eight in range(eights):
                start = pl.multiple_of(((index * eights + eight) * tiles + tile) * 8, 8)
                parts.append(rows_out[pl.ds(start, 8), :])
            out[place, part, :, tile * LANES : (tile + 1) * LANES] = jnp.concatenate(
                parts, axis=0
            ).astype(out.dtype)
        return carry

    lax.fori_loop(0, places * 2, gather, 0)


def columns_fused(pieces, legendre, waves, scalars, eig_rates, modes, sizes):
    wave_size, level_size, group, tiles, half_count, _, first = sizes
    places = wave_size * level_size
    half_rows = legendre.shape[1]
    width = tiles * LANES
    levels = modes[0].shape[0]
    whole = lambda shape: pl.BlockSpec(shape, lambda i: (0,) * len(shape))
    scratch = pltpu.VMEM((places * 2 * group * tiles, LANES), jnp.float32)
    values = places * 2 * group * width
    return pl.pallas_call(
        functools.partial(column_kernel, sizes),
        out_shape=jax.ShapeDtypeStruct((places, 2, group, width), jnp.bfloat16),
        grid=(1,),
        in_specs=[
            pl.BlockSpec(memory_space=pltpu.SMEM),
            pl.BlockSpec(memory_space=pltpu.SMEM),
            whole((levels, 1)),
            whole((levels, levels)),
            whole((levels, levels)),
            pl.BlockSpec((group, half_rows, half_count), lambda i: (first // group, 0, 0)),
        ]
        + [whole(piece.shape) for piece in pieces],
        out_specs=whole((places, 2, group, width)),
        scratch_shapes=[scratch, scratch],
        compiler_params=pltpu.CompilerParams(vmem_limit_bytes=40 * 2**20),
        cost_estimate=pl.CostEstimate(
            flops=values * half_rows * 6, bytes_accessed=6 * values, transcendentals=0
        ),
    )(waves, scalars, eig_rates[:, None], *modes, legendre, *pieces)


def columns_plain(mirrored, legendre, waves, parity, eig_rates, modes_in, modes_out, sizes):
    wave_size, level_size, count, first, wave_count = sizes
    levels = modes_in.shape[0]
    half_rows, half_count = legendre.shape[1:]
    local_levels, rows_here = levels // level_size, half_rows // wave_size
    shape = mirrored.shape
    mirrored = mirrored.reshape(wave_size, level_size, 2, count, local_levels, rows_here)
    field = mirrored.transpose(3, 2, 1, 4, 0, 5).reshape(count, 2, levels, half_rows)
    table = legendre[first : first + count]
    degree = (
        waves[first : first + count, None] + 2 * jnp.arange(half_count, dtype=jnp.int32)[None, :]
    ).astype(jnp.float32) + parity
    inside = (degree <= float(wave_count - 1)).astype(jnp.float32)
    ratio = tau_scale * degree * (degree + 1.0) / float(wave_count * (wave_count - 1))
    factor = 1.0 / (1.0 + ratio[:, None, :] * eig_rates[None, :, None])
    spectral = jnp.einsum("sclr,srj->sclj", field, table, preferred_element_type=jnp.float32)
    spectral = (spectral * inside[:, None, None, :]).astype(jnp.bfloat16)
    modal = jnp.einsum("kl,sclj->sckj", modes_in, spectral, preferred_element_type=jnp.float32)
    modal = (modal * factor[:, None, :, :]).astype(jnp.bfloat16)
    solved = jnp.einsum(
        "lk,sckj->sclj", modes_out, modal, preferred_element_type=jnp.float32
    ).astype(jnp.bfloat16)
    grid = jnp.einsum("sclj,srj->sclr", solved, table, preferred_element_type=jnp.float32)
    grid = grid.astype(jnp.bfloat16)
    grid = grid.reshape(count, 2, level_size, local_levels, wave_size, rows_here)
    return grid.transpose(4, 2, 1, 0, 3, 5).reshape(shape)


def shards(grid_state, legendre, wave_order, lat_order, eig_rates, modes_in, modes_out):
    out_shape = grid_state.shape
    local_levels, _, rows_here, lon_count = out_shape
    wave_size = lax.axis_size("wave")
    level_size = lax.axis_size("level")
    places = wave_size * level_size
    half_rows = lat_order.shape[0]
    wave_count = wave_order.shape[0]
    narrow, half_count = legendre.shape[0], legendre.shape[3]
    chunks = min(CHUNKS, narrow)
    count = narrow // chunks
    height = 2 * count
    width = local_levels * rows_here
    direct = (
        places <= DIRECT_LIMIT
        and rows_here * 2 == LANES
        and wave_size % 2 == 0
        and count % 16 == 0
        and local_levels % 32 == 0
    )
    parity = lax.axis_index("fld")
    wave_place = lax.axis_index("wave")
    level_place = lax.axis_index("level")
    place = wave_place * level_size + level_place
    legendre = legendre.reshape(narrow, half_rows, half_count)
    grid_state = grid_state.reshape(local_levels, rows_here, lon_count)
    hemi_sign = 1.0 - 2.0 * parity.astype(jnp.float32)
    lat_rows = lax.dynamic_slice_in_dim(lat_order, wave_place * rows_here, rows_here)
    waves = lax.dynamic_slice_in_dim(wave_order, place * narrow, narrow)
    quarter = jnp.broadcast_to(
        (jnp.arange(2, dtype=jnp.int32) * (lon_count // 4))[None, :, None], (places, 2, count)
    ).reshape(-1)
    fixed = wave_order.reshape(wave_size, level_size, chunks, count)
    turned = rolled(fixed, wave_place)
    turned = jnp.swapaxes(rolled(jnp.swapaxes(turned, 0, 1), level_place), 0, 1)

    def slot_ids(order, chunk):
        ids = order[:, :, chunk].reshape(places, 1, count)
        return jnp.broadcast_to(ids, (places, 2, count)).reshape(-1)

    def exchange(value):
        return lax.all_to_all(value, EXCHANGE_AXES, split_axis=0, concat_axis=0, tiled=True)

    def joined(other, own, scale):
        both = scale * (other.astype(jnp.float32) + hemi_sign * own.astype(jnp.float32))
        return both.astype(jnp.bfloat16)

    if not direct:
        returned, tables = [], []
        for chunk in range(chunks):
            value, table = fourier(
                grid_state, hemi_sign, lat_rows, half_rows, slot_ids(fixed, chunk), quarter
            )
            tables.append(table)
            own = exchange(value.reshape(places, height, width))
            mirrored = joined(partner(own, "fld"), own, 1.0)
            grid = columns_plain(
                mirrored.reshape(wave_size, level_size, 2, count, width),
                legendre,
                waves,
                parity.astype(jnp.float32),
                eig_rates,
                modes_in,
                modes_out,
                (wave_size, level_size, count, chunk * count, wave_count),
            ).reshape(places, height, width)
            hemi = exchange(joined(partner(grid, "fld"), grid, 0.5))
            returned.append(hemi.reshape(places * height, width))
        current = inverse_fourier(returned, tables, None, grid_state.shape, 0, local_levels)
        return current.reshape(out_shape)

    tiles = width // LANES
    level_index = jnp.arange(local_levels, dtype=jnp.int32).reshape(tiles, 2).T
    sources = []
    for is_turned in (0, 1):
        shift = jnp.arange(level_size, dtype=jnp.int32)
        from_level = (level_place - shift) % level_size if is_turned else shift
        order = (from_level[None, :, None] * local_levels + level_index[:, None, :]).reshape(-1)
        shift = jnp.arange(wave_size, dtype=jnp.int32)
        from_wave = (wave_place - shift) % wave_size if is_turned else shift
        sources.append(
            (
                jnp.concatenate([from_wave, parity[None]]),
                (jnp.take(modes_in, order, axis=1), jnp.take(modes_out, order, axis=0)),
            )
        )
    shifts = [(wave, level) for wave in range(wave_size) for level in range(level_size)]

    arrived, tables = [], []
    for chunk in range(chunks):
        is_whole = chunk in WHOLE_CHUNKS
        ids = slot_ids(fixed if is_whole else turned, chunk)
        value, table = fourier(grid_state, hemi_sign, lat_rows, half_rows, ids, quarter)
        tables.append(table)
        if is_whole:
            arrived.append([exchange(value.reshape(places, 2, count, width))])
            continue
        other = partner(value, "fld")
        pieces = []
        for index, (wave, level) in enumerate(shifts):
            rows = slice(index * height, (index + 1) * height)
            mirrored = joined(other[rows], value[rows], 1.0)
            piece = shift_places(mirrored, wave, level)
            pieces.append(piece.reshape(2, count, width))
        arrived.append(pieces)

    cuts = [(0, local_levels // 2)]
    cuts += [(local_levels // 4 * part, local_levels // 4) for part in (2, 3)]
    returned, last = [], []
    for chunk in range(chunks):
        is_whole = chunk in WHOLE_CHUNKS
        pieces = arrived[chunk]
        if is_whole:
            pieces = [pieces[0], partner(pieces[0], "fld")]
        scalars, modes = sources[0 if is_whole else 1]
        sizes = (wave_size, level_size, count, tiles, half_count, wave_count, chunk * count)
        grid = columns_fused(pieces, legendre, waves, scalars, eig_rates, modes, sizes)
        grid = grid.reshape(places, height, width)
        other = partner(grid, "fld")
        if is_whole:
            hemi = exchange(joined(other, grid, 0.5))
            returned.append(hemi.reshape(places * height, width))
            continue
        is_last = chunk == chunks - 1
        for start, levels in cuts if is_last else [(0, local_levels)]:
            lanes = slice(start * rows_here, (start + levels) * rows_here)
            pieces = []
            for index, (wave, level) in enumerate(shifts):
                hemi = joined(other[index, :, lanes], grid[index, :, lanes], 0.5)
                wave, level = (wave_size - wave) % wave_size, (level_size - level) % level_size
                pieces.append(shift_places(hemi, wave, level))
            if is_last:
                last.append(pieces)
            else:
                returned += pieces
    current = None
    for cut, (start, levels) in enumerate(cuts):
        current = inverse_fourier(
            returned + last[cut], tables, current, grid_state.shape, start, levels
        )
    return current.reshape(out_shape)


def solution(mesh):
    placed = (
        P(("member", "level"), "fld", "wave", None),
        P(("wave", "level"), "fld", None, None),
        P(),
        P(),
        P(),
        P(),
        P(),
    )
    return jax.shard_map(
        shards,
        mesh=mesh,
        in_specs=placed,
        out_specs=P(("member", "level"), "fld", "wave", None),
        check_vma=False,
    )
```

```python
import functools
import math

import jax
import jax.numpy as jnp
from jax import lax
from jax.experimental import pallas as pl
from jax.experimental.pallas import tpu as pltpu
from jax.sharding import PartitionSpec as P


tau_scale = 2.0
LANES = 128
CHUNKS = 4
WHOLE_CHUNKS = (0, 2)
DIRECT_LIMIT = 16
EXCHANGE_AXES = ("wave", "level")


def partner(value, axis):
    pairs = [(source, source ^ 1) for source in range(lax.axis_size(axis))]
    return lax.ppermute(value, axis, pairs)


def shift_places(value, wave_shift, level_shift):
    if wave_shift == 0 and level_shift == 0:
        return value
    waves, levels = lax.axis_size("wave"), lax.axis_size("level")
    pairs = []
    for wave in range(waves):
        for level in range(levels):
            target = (wave + wave_shift) % waves * levels + (level + level_shift) % levels
            pairs.append((wave * levels + level, target))
    return lax.ppermute(value, EXCHANGE_AXES, pairs)


def level_block(levels, rows_here, most):
    whole = levels % most == 0 and most * rows_here % LANES == 0
    return most if whole else levels


def pick(values, index):
    rows, many = index.shape[0], values.shape[1]
    hit = lax.broadcasted_iota(jnp.int32, (rows, many), 1) == index
    return jnp.sum(jnp.where(hit, values, 0.0), axis=1, keepdims=True)


def write_table(sizes, place_ref, wave_order, table):
    wave_size, level_size, chunks, chunk, turned, _ = sizes
    rows, lon_count = table.shape
    places = wave_size * level_size
    count = rows // (2 * places)
    scale = math.sqrt(2.0 / lon_count)
    row = lax.broadcasted_iota(jnp.int32, (rows, 1), 0)
    slot, place = row % count, row // (2 * count)
    part = (row // count) % 2
    if turned:
        wave = (place // level_size + place_ref[0]) % wave_size
        place = wave * level_size + (place % level_size + place_ref[1]) % level_size
    wave = pick(wave_order[...].astype(jnp.float32), (place * chunks + chunk) * count + slot)
    lane = lax.broadcasted_iota(jnp.int32, (rows, LANES), 1).astype(jnp.float32)

    def angle(steps):
        steps = steps - lon_count * jnp.floor(steps * (1.0 / lon_count))
        return steps * (2.0 * math.pi / lon_count)

    low = angle(wave * lane)
    high = angle(wave * lane * float(LANES) + part.astype(jnp.float32) * (lon_count / 4))
    low_cos, low_sin = jnp.cos(low) * scale, jnp.sin(low) * scale
    high_cos, high_sin = jnp.cos(high), jnp.sin(high)
    for block in range(lon_count // LANES):
        values = (
            high_cos[:, block : block + 1] * low_cos - high_sin[:, block : block + 1] * low_sin
        )
        table[:, block * LANES : (block + 1) * LANES] = values.astype(table.dtype)


def fourier_kernel(sizes, place_ref, grid_ref, wave_order, lat_order, out, table, coupling):
    levels, rows, lon_count = grid_ref.shape

    @pl.when(pl.program_id(0) == 0)
    def _():
        write_table(sizes, place_ref, wave_order, table)
        row = lax.broadcasted_iota(jnp.int32, (rows, 1), 0) + place_ref[0] * rows
        latitude = pick(lat_order[...].astype(jnp.float32), row) + 0.5
        sine = jnp.sin(latitude * (math.pi / (2.0 * lat_order.shape[1])))
        sign = 1.0 - 2.0 * place_ref[2].astype(jnp.float32)
        coupling[...] = jnp.broadcast_to(0.5 * sign * sine, coupling.shape)

    field = grid_ref[...].astype(jnp.float32)
    forcing = (field + coupling[:, :1][None] * jnp.tanh(field)).astype(jnp.bfloat16)
    forcing = forcing.reshape(levels * rows, lon_count)
    out[...] = lax.dot_general(
        table[...], forcing, (((1,), (1,)), ((), ())), preferred_element_type=jnp.float32
    ).astype(out.dtype)


def fourier(grid_state, place, wave_order, lat_order, sizes):
    levels, rows_here, lon_count = grid_state.shape
    _, _, _, _, _, height = sizes
    block = level_block(levels, rows_here, 16)
    width = levels * rows_here
    whole = lambda *shape: pl.BlockSpec(shape, lambda i: (0,) * len(shape))
    return pl.pallas_call(
        functools.partial(fourier_kernel, sizes),
        out_shape=[
            jax.ShapeDtypeStruct((height, width), jnp.bfloat16),
            jax.ShapeDtypeStruct((height, lon_count), jnp.bfloat16),
        ],
        grid=(levels // block,),
        in_specs=[
            pl.BlockSpec(memory_space=pltpu.SMEM),
            pl.BlockSpec((block, rows_here, lon_count), lambda i: (i, 0, 0)),
            whole(1, wave_order.shape[0]),
            whole(1, lat_order.shape[0]),
        ],
        out_specs=[
            pl.BlockSpec((height, block * rows_here), lambda i: (0, i)),
            whole(height, lon_count),
        ],
        scratch_shapes=[pltpu.VMEM((rows_here, LANES), jnp.float32)],
        compiler_params=pltpu.CompilerParams(vmem_limit_bytes=56 * 2**20),
        cost_estimate=pl.CostEstimate(
            flops=2 * height * width * lon_count,
            bytes_accessed=2 * (width * lon_count + height * (width + lon_count)),
            transcendentals=width * lon_count,
        ),
    )(place, grid_state, wave_order[None], lat_order[None])


def inverse_kernel(pieces, tables, has_partial, *refs):
    out = refs[-1]
    coeffs = jnp.concatenate([ref[...] for ref in refs[:pieces]], axis=0)
    table = jnp.concatenate([ref[...] for ref in refs[pieces : pieces + tables]], axis=0)
    current = lax.dot_general(
        coeffs, table, (((0,), (0,)), ((), ())), preferred_element_type=jnp.float32
    ).reshape(out.shape)
    if has_partial:
        current = current + refs[pieces + tables][...]
    out[...] = current.astype(out.dtype)


def inverse_fourier(pieces, tables, shape, start, levels, current=None, partial=None, dtype=None):
    _, rows_here, lon_count = shape
    block = level_block(levels, rows_here, 8)
    width = block * rows_here
    first = start // block
    height = sum(table.shape[0] for table in tables)
    grid_block = (block, rows_here, lon_count)

    def cut(begin):
        return first - begin // block

    specs, operands, aliases = [], [], {}
    for piece, begin in pieces:
        operands.append(piece)
        specs.append(pl.BlockSpec((piece.shape[0], width), lambda i, skip=cut(begin): (0, skip + i)))
    for table in tables:
        operands.append(table)
        specs.append(
            pl.BlockSpec(table.shape, lambda i: (0, 0), pipeline_mode=pl.Buffered(1))
        )
    if partial is not None:
        operands.append(partial[0])
        specs.append(pl.BlockSpec(grid_block, lambda i, skip=cut(partial[1]): (skip + i, 0, 0)))
    if current is not None:
        aliases = {len(operands): 0}
        operands.append(current)
        specs.append(pl.BlockSpec(memory_space=pl.ANY))
    out_first = 0 if dtype is not None else first
    out_shape = (levels, rows_here, lon_count) if dtype is not None else shape
    return pl.pallas_call(
        functools.partial(inverse_kernel, len(pieces), len(tables), partial is not None),
        out_shape=jax.ShapeDtypeStruct(out_shape, dtype or jnp.bfloat16),
        grid=(levels // block,),
        in_specs=specs,
        out_specs=pl.BlockSpec(grid_block, lambda i: (out_first + i, 0, 0)),
        input_output_aliases=aliases,
        compiler_params=pltpu.CompilerParams(vmem_limit_bytes=56 * 2**20),
        cost_estimate=pl.CostEstimate(
            flops=2 * height * levels * rows_here * lon_count,
            bytes_accessed=2 * levels * rows_here * (height + lon_count),
            transcendentals=0,
        ),
    )(*operands)


def column_kernel(sizes, waves, scalars, eig_ref, modes_in, modes_out, table, *refs):
    wave_size, level_size, group, tiles, half_count, wave_count, first = sizes
    places = wave_size * level_size
    pieces, (out, rows_in, rows_out) = refs[:-3], refs[-3:]
    eights = group // 8
    rows_here = LANES // 2
    parity = scalars[wave_size].astype(jnp.float32)
    low_half = lax.broadcasted_iota(jnp.int32, (tiles, LANES), 1) < LANES // 2

    def spread(start, part, value):
        for tile in range(tiles):
            for eight in range(eights):
                row = ((start * 2 + part) * eights + eight) * tiles + tile
                rows_in[pl.ds(pl.multiple_of(row * 8, 8), 8), :] = value(tile)[
                    eight * 8 : (eight + 1) * 8
                ]

    if len(pieces) == 2:
        own, other = pieces
        sign = 1.0 - 2.0 * parity

        def combined(index, carry):
            place, part = index // 2, index % 2

            def value(tile):
                lanes = slice(tile * LANES, (tile + 1) * LANES)
                both = other[place, part, :, lanes].astype(jnp.float32) + sign * own[
                    place, part, :, lanes
                ].astype(jnp.float32)
                return both.astype(jnp.bfloat16).astype(jnp.float32)

            spread(place, part, value)
            return carry

        lax.fori_loop(0, places * 2, combined, 0)
    else:
        for place, piece in enumerate(pieces):

            def arrived(part, carry, place=place, piece=piece):
                def value(tile):
                    return piece[part, :, tile * LANES : (tile + 1) * LANES].astype(jnp.float32)

                spread(place, part, value)
                return carry

            lax.fori_loop(0, 2, arrived, 0)

    def where_rows(place, part, slot):
        eight, within = slot // 8, slot % 8
        return pl.ds((((place * 2 + part) * eights + eight) * tiles) * 8 + within, tiles, 8)

    def one_slot(slot, carry):
        legendre = jnp.concatenate(
            [
                table[slot, pl.ds(pl.multiple_of(scalars[wave] * rows_here, rows_here), rows_here), :]
                for wave in range(wave_size)
            ],
            axis=0,
        )
        stacked = []
        for part in range(2):
            low_rows, high_rows = [], []
            for level in range(level_size):
                low_pieces, high_pieces = [], []
                for pair in range(wave_size // 2):
                    a = rows_in[where_rows(2 * pair * level_size + level, part, slot), :]
                    b = rows_in[where_rows((2 * pair + 1) * level_size + level, part, slot), :]
                    low_pieces.append(jnp.where(low_half, a, pltpu.roll(b, LANES // 2, 1)))
                    high_pieces.append(jnp.where(low_half, pltpu.roll(a, LANES // 2, 1), b))
                low_rows.append(jnp.concatenate(low_pieces, axis=1))
                high_rows.append(jnp.concatenate(high_pieces, axis=1))
            stacked += low_rows + high_rows
        field = jnp.concatenate(stacked, axis=0).astype(jnp.bfloat16)
        degree = (
            waves[first + slot] + 2 * lax.broadcasted_iota(jnp.int32, (1, half_count), 1)
        ).astype(jnp.float32) + parity
        inside = (degree <= float(wave_count - 1)).astype(jnp.float32)
        ratio = tau_scale * degree * (degree + 1.0) / float(wave_count * (wave_count - 1))
        factor = 1.0 / (1.0 + eig_ref[...] * ratio)
        spectral = jnp.dot(field, legendre, preferred_element_type=jnp.float32)
        spectral = (spectral * inside).astype(jnp.bfloat16)
        levels = modes_in.shape[0]
        solved = []
        for part in range(2):
            column = spectral[part * levels : (part + 1) * levels]
            modal = jnp.dot(modes_in[...], column, preferred_element_type=jnp.float32)
            modal = (modal * factor).astype(jnp.bfloat16)
            solved.append(
                jnp.dot(modes_out[...], modal, preferred_element_type=jnp.float32).astype(
                    jnp.bfloat16
                )
            )
        grid = lax.dot_general(
            jnp.concatenate(solved, axis=0),
            legendre,
            (((1,), (1,)), ((), ())),
            preferred_element_type=jnp.float32,
        )
        for part in range(2):
            for level in range(level_size):
                low_start = part * levels + level * tiles
                high_start = low_start + level_size * tiles
                for pair in range(wave_size // 2):
                    lanes = slice(pair * LANES, (pair + 1) * LANES)
                    low = grid[low_start : low_start + tiles, lanes]
                    high = grid[high_start : high_start + tiles, lanes]
                    a = jnp.where(low_half, low, pltpu.roll(high, LANES // 2, 1))
                    b = jnp.where(low_half, pltpu.roll(low, LANES // 2, 1), high)
                    rows_out[where_rows(2 * pair * level_size + level, part, slot), :] = a
                    rows_out[where_rows((2 * pair + 1) * level_size + level, part, slot), :] = b
        return carry

    lax.fori_loop(0, group, one_slot, 0)

    def gather(index, carry):
        place, part = index // 2, index % 2
        for tile in range(tiles):
            parts = []
            for eight in range(eights):
                start = pl.multiple_of(((index * eights + eight) * tiles + tile) * 8, 8)
                parts.append(rows_out[pl.ds(start, 8), :])
            out[place, part, :, tile * LANES : (tile + 1) * LANES] = jnp.concatenate(
                parts, axis=0
            ).astype(out.dtype)
        return carry

    lax.fori_loop(0, places * 2, gather, 0)


def columns_fused(pieces, legendre, waves, scalars, eig_rates, modes, sizes):
    wave_size, level_size, group, tiles, half_count, _, first = sizes
    places = wave_size * level_size
    half_rows = legendre.shape[1]
    width = tiles * LANES
    levels = modes[0].shape[0]
    whole = lambda shape: pl.BlockSpec(shape, lambda i: (0,) * len(shape))
    scratch = pltpu.VMEM((places * 2 * group * tiles, LANES), jnp.float32)
    values = places * 2 * group * width
    return pl.pallas_call(
        functools.partial(column_kernel, sizes),
        out_shape=jax.ShapeDtypeStruct((places, 2, group, width), jnp.bfloat16),
        grid=(1,),
        in_specs=[
            pl.BlockSpec(memory_space=pltpu.SMEM),
            pl.BlockSpec(memory_space=pltpu.SMEM),
            whole((levels, 1)),
            whole((levels, levels)),
            whole((levels, levels)),
            pl.BlockSpec((group, half_rows, half_count), lambda i: (first // group, 0, 0)),
        ]
        + [whole(piece.shape) for piece in pieces],
        out_specs=whole((places, 2, group, width)),
        scratch_shapes=[scratch, scratch],
        compiler_params=pltpu.CompilerParams(vmem_limit_bytes=56 * 2**20),
        cost_estimate=pl.CostEstimate(
            flops=values * half_rows * 6, bytes_accessed=6 * values, transcendentals=0
        ),
    )(waves, scalars, eig_rates[:, None], *modes, legendre, *pieces)


def columns_plain(mirrored, legendre, waves, parity, eig_rates, modes_in, modes_out, sizes):
    wave_size, level_size, count, first, wave_count = sizes
    levels = modes_in.shape[0]
    half_rows, half_count = legendre.shape[1:]
    local_levels, rows_here = levels // level_size, half_rows // wave_size
    shape = mirrored.shape
    mirrored = mirrored.reshape(wave_size, level_size, 2, count, local_levels, rows_here)
    field = mirrored.transpose(3, 2, 1, 4, 0, 5).reshape(count, 2, levels, half_rows)
    table = legendre[first : first + count]
    degree = (
        waves[first : first + count, None] + 2 * jnp.arange(half_count, dtype=jnp.int32)[None, :]
    ).astype(jnp.float32) + parity
    inside = (degree <= float(wave_count - 1)).astype(jnp.float32)
    ratio = tau_scale * degree * (degree + 1.0) / float(wave_count * (wave_count - 1))
    factor = 1.0 / (1.0 + ratio[:, None, :] * eig_rates[None, :, None])
    spectral = jnp.einsum("sclr,srj->sclj", field, table, preferred_element_type=jnp.float32)
    spectral = (spectral * inside[:, None, None, :]).astype(jnp.bfloat16)
    modal = jnp.einsum("kl,sclj->sckj", modes_in, spectral, preferred_element_type=jnp.float32)
    modal = (modal * factor[:, None, :, :]).astype(jnp.bfloat16)
    solved = jnp.einsum(
        "lk,sckj->sclj", modes_out, modal, preferred_element_type=jnp.float32
    ).astype(jnp.bfloat16)
    grid = jnp.einsum("sclj,srj->sclr", solved, table, preferred_element_type=jnp.float32)
    grid = grid.astype(jnp.bfloat16)
    grid = grid.reshape(count, 2, level_size, local_levels, wave_size, rows_here)
    return grid.transpose(4, 2, 1, 0, 3, 5).reshape(shape)


def shards(grid_state, legendre, wave_order, lat_order, eig_rates, modes_in, modes_out):
    out_shape = grid_state.shape
    local_levels, _, rows_here, lon_count = out_shape
    wave_size = lax.axis_size("wave")
    level_size = lax.axis_size("level")
    places = wave_size * level_size
    half_rows = lat_order.shape[0]
    wave_count = wave_order.shape[0]
    narrow, half_count = legendre.shape[0], legendre.shape[3]
    chunks = min(CHUNKS, narrow)
    count = narrow // chunks
    height = 2 * count
    width = local_levels * rows_here
    direct = (
        places <= DIRECT_LIMIT
        and rows_here * 2 == LANES
        and wave_size % 2 == 0
        and count % 16 == 0
        and local_levels % 32 == 0
    )
    parity = lax.axis_index("fld")
    wave_place = lax.axis_index("wave")
    level_place = lax.axis_index("level")
    place = wave_place * level_size + level_place
    legendre = legendre.reshape(narrow, half_rows, half_count)
    grid_state = grid_state.reshape(local_levels, rows_here, lon_count)
    hemi_sign = 1.0 - 2.0 * parity.astype(jnp.float32)
    waves = lax.dynamic_slice_in_dim(wave_order, place * narrow, narrow)
    where = jnp.stack([wave_place, level_place, parity]).astype(jnp.int32)

    def exchange(value):
        return lax.all_to_all(value, EXCHANGE_AXES, split_axis=0, concat_axis=0, tiled=True)

    def joined(other, own, scale):
        both = scale * (other.astype(jnp.float32) + hemi_sign * own.astype(jnp.float32))
        return both.astype(jnp.bfloat16)

    if not direct:
        returned, tables = [], []
        for chunk in range(chunks):
            sizes = (wave_size, level_size, chunks, chunk, False, places * height)
            value, table = fourier(grid_state, where, wave_order, lat_order, sizes)
            tables.append(table)
            own = exchange(value.reshape(places, height, width))
            mirrored = joined(partner(own, "fld"), own, 1.0)
            grid = columns_plain(
                mirrored.reshape(wave_size, level_size, 2, count, width),
                legendre,
                waves,
                parity.astype(jnp.float32),
                eig_rates,
                modes_in,
                modes_out,
                (wave_size, level_size, count, chunk * count, wave_count),
            ).reshape(places, height, width)
            hemi = exchange(joined(partner(grid, "fld"), grid, 0.5))
            returned.append((hemi.reshape(places * height, width), 0))
        current = inverse_fourier(returned, tables, grid_state.shape, 0, local_levels)
        return current.reshape(out_shape)

    tiles = width // LANES
    level_index = jnp.arange(local_levels, dtype=jnp.int32).reshape(tiles, 2).T
    sources = []
    for is_turned in (0, 1):
        shift = jnp.arange(level_size, dtype=jnp.int32)
        from_level = (level_place - shift) % level_size if is_turned else shift
        order = (from_level[None, :, None] * local_levels + level_index[:, None, :]).reshape(-1)
        shift = jnp.arange(wave_size, dtype=jnp.int32)
        from_wave = (wave_place - shift) % wave_size if is_turned else shift
        sources.append(
            (
                jnp.concatenate([from_wave, parity[None]]),
                (jnp.take(modes_in, order, axis=1), jnp.take(modes_out, order, axis=0)),
            )
        )
    shifts = [(wave, level) for wave in range(wave_size) for level in range(level_size)]

    arrived, tables = [], []
    for chunk in range(chunks):
        is_whole = chunk in WHOLE_CHUNKS
        sizes = (wave_size, level_size, chunks, chunk, not is_whole, places * height)
        value, table = fourier(grid_state, where, wave_order, lat_order, sizes)
        tables.append(table)
        if is_whole:
            arrived.append([exchange(value.reshape(places, 2, count, width))])
            continue
        other = partner(value, "fld")
        pieces = []
        for index, (wave, level) in enumerate(shifts):
            rows = slice(index * height, (index + 1) * height)
            mirrored = joined(other[rows], value[rows], 1.0)
            piece = shift_places(mirrored, wave, level)
            pieces.append(piece.reshape(2, count, width))
        arrived.append(pieces)

    half, fourth = local_levels // 2, local_levels // 4
    cuts = {chunk: [(0, local_levels)] for chunk in range(chunks)}
    cuts[1] = [(0, half), (half, half)]
    cuts[chunks - 1] = [(0, half), (half, fourth), (half + fourth, fourth)]
    returned = []
    for chunk in range(chunks):
        is_whole = chunk in WHOLE_CHUNKS
        pieces = arrived[chunk]
        if is_whole:
            pieces = [pieces[0], partner(pieces[0], "fld")]
        scalars, modes = sources[0 if is_whole else 1]
        sizes = (wave_size, level_size, count, tiles, half_count, wave_count, chunk * count)
        grid = columns_fused(pieces, legendre, waves, scalars, eig_rates, modes, sizes)
        grid = grid.reshape(places, height, width)
        other = partner(grid, "fld")
        if is_whole:
            hemi = exchange(joined(other, grid, 0.5))
            returned.append([(0, local_levels, [hemi.reshape(places * height, width)])])
            continue
        groups = []
        for start, levels in cuts[chunk]:
            lanes = slice(start * rows_here, (start + levels) * rows_here)
            pieces = []
            for index, (wave, level) in enumerate(shifts):
                hemi = joined(other[index, :, lanes], grid[index, :, lanes], 0.5)
                wave, level = (wave_size - wave) % wave_size, (level_size - level) % level_size
                pieces.append(shift_places(hemi, wave, level))
            groups.append((start, levels, pieces))
        returned.append(groups)

    def pieces_at(chunk_list, start):
        return [
            (piece, begin)
            for chunk in chunk_list
            for begin, levels, pieces in returned[chunk]
            if begin <= start < begin + levels
            for piece in pieces
        ]

    shape = grid_state.shape
    everything = list(range(chunks))
    partial = inverse_fourier(
        pieces_at(everything[:2], half), tables[:2], shape, half, half, dtype=jnp.float32
    )
    current = inverse_fourier(pieces_at(everything, 0), tables, shape, 0, half)
    for cut in (1, 2):
        start = half + (cut - 1) * fourth
        current = inverse_fourier(
            pieces_at(everything[2:], start),
            tables[2:],
            shape,
            start,
            fourth,
            current=current,
            partial=(partial, half),
        )
    return current.reshape(out_shape)


def solution(mesh):
    placed = (
        P(("member", "level"), "fld", "wave", None),
        P(("wave", "level"), "fld", None, None),
        P(),
        P(),
        P(),
        P(),
        P(),
    )
    return jax.shard_map(
        shards,
        mesh=mesh,
        in_specs=placed,
        out_specs=P(("member", "level"), "fld", "wave", None),
        check_vma=False,
    )
```

```python
import functools
import math

import jax
import jax.numpy as jnp
from jax import lax
from jax.experimental import pallas as pl
from jax.experimental.pallas import tpu as pltpu
from jax.sharding import PartitionSpec as P


tau_scale = 2.0
LANES = 128
CHUNKS = 4
WHOLE_CHUNKS = (0, 2)
DIRECT_LIMIT = 16
EXCHANGE_AXES = ("wave", "level")


def partner(value, axis):
    pairs = [(source, source ^ 1) for source in range(lax.axis_size(axis))]
    return lax.ppermute(value, axis, pairs)


def shift_places(value, wave_shift, level_shift):
    if wave_shift == 0 and level_shift == 0:
        return value
    waves, levels = lax.axis_size("wave"), lax.axis_size("level")
    pairs = []
    for wave in range(waves):
        for level in range(levels):
            target = (wave + wave_shift) % waves * levels + (level + level_shift) % levels
            pairs.append((wave * levels + level, target))
    return lax.ppermute(value, EXCHANGE_AXES, pairs)


def level_block(levels, rows_here, most):
    whole = levels % most == 0 and most * rows_here % LANES == 0
    return most if whole else levels


def pick(values, index):
    rows, many = index.shape[0], values.shape[1]
    hit = lax.broadcasted_iota(jnp.int32, (rows, many), 1) == index
    return jnp.sum(jnp.where(hit, values, 0.0), axis=1, keepdims=True)


def write_table(sizes, place_ref, wave_order, table):
    wave_size, level_size, chunks, chunk, turned, _ = sizes
    rows, lon_count = table.shape
    places = wave_size * level_size
    count = rows // (2 * places)
    scale = math.sqrt(2.0 / lon_count)
    row = lax.broadcasted_iota(jnp.int32, (rows, 1), 0)
    slot, place = row % count, row // (2 * count)
    part = (row // count) % 2
    if turned:
        wave = (place // level_size + place_ref[0]) % wave_size
        place = wave * level_size + (place % level_size + place_ref[1]) % level_size
    wave = pick(wave_order[...].astype(jnp.float32), (place * chunks + chunk) * count + slot)
    lane = lax.broadcasted_iota(jnp.int32, (rows, LANES), 1).astype(jnp.float32)

    def angle(steps):
        steps = steps - lon_count * jnp.floor(steps * (1.0 / lon_count))
        return steps * (2.0 * math.pi / lon_count)

    low = angle(wave * lane)
    high = angle(wave * lane * float(LANES) + part.astype(jnp.float32) * (lon_count / 4))
    low_cos, low_sin = jnp.cos(low) * scale, jnp.sin(low) * scale
    high_cos, high_sin = jnp.cos(high), jnp.sin(high)
    for block in range(lon_count // LANES):
        values = (
            high_cos[:, block : block + 1] * low_cos - high_sin[:, block : block + 1] * low_sin
        )
        table[:, block * LANES : (block + 1) * LANES] = values.astype(table.dtype)


def fourier_kernel(sizes, place_ref, grid_ref, wave_order, lat_order, out, table, coupling):
    levels, rows, lon_count = grid_ref.shape

    @pl.when(pl.program_id(0) == 0)
    def _():
        write_table(sizes, place_ref, wave_order, table)
        row = lax.broadcasted_iota(jnp.int32, (rows, 1), 0) + place_ref[0] * rows
        latitude = pick(lat_order[...].astype(jnp.float32), row) + 0.5
        sine = jnp.sin(latitude * (math.pi / (2.0 * lat_order.shape[1])))
        sign = 1.0 - 2.0 * place_ref[2].astype(jnp.float32)
        coupling[...] = jnp.broadcast_to(0.5 * sign * sine, coupling.shape)

    field = grid_ref[...].astype(jnp.float32)
    forcing = (field + coupling[:, :1][None] * jnp.tanh(field)).astype(jnp.bfloat16)
    forcing = forcing.reshape(levels * rows, lon_count)
    out[...] = lax.dot_general(
        table[...], forcing, (((1,), (1,)), ((), ())), preferred_element_type=jnp.float32
    ).astype(out.dtype)


def fourier(grid_state, place, wave_order, lat_order, sizes):
    levels, rows_here, lon_count = grid_state.shape
    _, _, _, _, _, height = sizes
    block = level_block(levels, rows_here, 16)
    width = levels * rows_here
    whole = lambda *shape: pl.BlockSpec(shape, lambda i: (0,) * len(shape))
    return pl.pallas_call(
        functools.partial(fourier_kernel, sizes),
        out_shape=[
            jax.ShapeDtypeStruct((height, width), jnp.bfloat16),
            jax.ShapeDtypeStruct((height, lon_count), jnp.bfloat16),
        ],
        grid=(levels // block,),
        in_specs=[
            pl.BlockSpec(memory_space=pltpu.SMEM),
            pl.BlockSpec((block, rows_here, lon_count), lambda i: (i, 0, 0)),
            whole(1, wave_order.shape[0]),
            whole(1, lat_order.shape[0]),
        ],
        out_specs=[
            pl.BlockSpec((height, block * rows_here), lambda i: (0, i)),
            whole(height, lon_count),
        ],
        scratch_shapes=[pltpu.VMEM((rows_here, LANES), jnp.float32)],
        compiler_params=pltpu.CompilerParams(vmem_limit_bytes=56 * 2**20),
        cost_estimate=pl.CostEstimate(
            flops=2 * height * width * lon_count,
            bytes_accessed=2 * (width * lon_count + height * (width + lon_count)),
            transcendentals=width * lon_count,
        ),
    )(place, grid_state, wave_order[None], lat_order[None])


def inverse_kernel(pieces, tables, has_partial, *refs):
    out = refs[-1]
    coeffs = jnp.concatenate([ref[...] for ref in refs[:pieces]], axis=0)
    table = jnp.concatenate([ref[...] for ref in refs[pieces : pieces + tables]], axis=0)
    current = lax.dot_general(
        coeffs, table, (((0,), (0,)), ((), ())), preferred_element_type=jnp.float32
    ).reshape(out.shape)
    if has_partial:
        current = current + refs[pieces + tables][...]
    out[...] = current.astype(out.dtype)


def inverse_fourier(pieces, tables, shape, start, levels, current=None, partial=None, dtype=None):
    _, rows_here, lon_count = shape
    block = level_block(levels, rows_here, 8)
    width = block * rows_here
    first = start // block
    height = sum(table.shape[0] for table in tables)
    grid_block = (block, rows_here, lon_count)

    def cut(begin):
        return first - begin // block

    specs, operands, aliases = [], [], {}
    for piece, begin in pieces:
        operands.append(piece)
        specs.append(pl.BlockSpec((piece.shape[0], width), lambda i, skip=cut(begin): (0, skip + i)))
    for table in tables:
        operands.append(table)
        specs.append(
            pl.BlockSpec(table.shape, lambda i: (0, 0), pipeline_mode=pl.Buffered(1))
        )
    if partial is not None:
        operands.append(partial[0])
        specs.append(pl.BlockSpec(grid_block, lambda i, skip=cut(partial[1]): (skip + i, 0, 0)))
    if current is not None:
        aliases = {len(operands): 0}
        operands.append(current)
        specs.append(pl.BlockSpec(memory_space=pl.ANY))
    out_first = 0 if dtype is not None else first
    out_shape = (levels, rows_here, lon_count) if dtype is not None else shape
    return pl.pallas_call(
        functools.partial(inverse_kernel, len(pieces), len(tables), partial is not None),
        out_shape=jax.ShapeDtypeStruct(out_shape, dtype or jnp.bfloat16),
        grid=(levels // block,),
        in_specs=specs,
        out_specs=pl.BlockSpec(grid_block, lambda i: (out_first + i, 0, 0)),
        input_output_aliases=aliases,
        compiler_params=pltpu.CompilerParams(vmem_limit_bytes=56 * 2**20),
        cost_estimate=pl.CostEstimate(
            flops=2 * height * levels * rows_here * lon_count,
            bytes_accessed=2 * levels * rows_here * (height + lon_count),
            transcendentals=0,
        ),
    )(*operands)


def column_kernel(sizes, waves, scalars, eig_ref, modes_in, modes_out, table, *refs):
    wave_size, level_size, group, tiles, half_count, wave_count, first = sizes
    places = wave_size * level_size
    pieces, (out, rows_in, rows_out) = refs[:-3], refs[-3:]
    eights = group // 8
    rows_here = LANES // 2
    parity = scalars[wave_size].astype(jnp.float32)
    low_half = lax.broadcasted_iota(jnp.int32, (tiles, LANES), 1) < LANES // 2

    def spread(start, part, value):
        for tile in range(tiles):
            for eight in range(eights):
                row = ((start * 2 + part) * eights + eight) * tiles + tile
                rows_in[pl.ds(pl.multiple_of(row * 8, 8), 8), :] = value(tile)[
                    eight * 8 : (eight + 1) * 8
                ]

    if len(pieces) == 2:
        own, other = pieces
        sign = 1.0 - 2.0 * parity

        def combined(index, carry):
            place, part = index // 2, index % 2

            def value(tile):
                lanes = slice(tile * LANES, (tile + 1) * LANES)
                both = other[place, part, :, lanes].astype(jnp.float32) + sign * own[
                    place, part, :, lanes
                ].astype(jnp.float32)
                return both.astype(jnp.bfloat16).astype(jnp.float32)

            spread(place, part, value)
            return carry

        lax.fori_loop(0, places * 2, combined, 0)
    else:
        for place, piece in enumerate(pieces):

            def arrived(part, carry, place=place, piece=piece):
                def value(tile):
                    return piece[part, :, tile * LANES : (tile + 1) * LANES].astype(jnp.float32)

                spread(place, part, value)
                return carry

            lax.fori_loop(0, 2, arrived, 0)

    def where_rows(place, part, slot):
        eight, within = slot // 8, slot % 8
        return pl.ds((((place * 2 + part) * eights + eight) * tiles) * 8 + within, tiles, 8)

    def one_slot(slot, carry):
        legendre = jnp.concatenate(
            [
                table[slot, pl.ds(pl.multiple_of(scalars[wave] * rows_here, rows_here), rows_here), :]
                for wave in range(wave_size)
            ],
            axis=0,
        )
        stacked = []
        for part in range(2):
            low_rows, high_rows = [], []
            for level in range(level_size):
                low_pieces, high_pieces = [], []
                for pair in range(wave_size // 2):
                    a = rows_in[where_rows(2 * pair * level_size + level, part, slot), :]
                    b = rows_in[where_rows((2 * pair + 1) * level_size + level, part, slot), :]
                    low_pieces.append(jnp.where(low_half, a, pltpu.roll(b, LANES // 2, 1)))
                    high_pieces.append(jnp.where(low_half, pltpu.roll(a, LANES // 2, 1), b))
                low_rows.append(jnp.concatenate(low_pieces, axis=1))
                high_rows.append(jnp.concatenate(high_pieces, axis=1))
            stacked += low_rows + high_rows
        field = jnp.concatenate(stacked, axis=0).astype(jnp.bfloat16)
        degree = (
            waves[first + slot] + 2 * lax.broadcasted_iota(jnp.int32, (1, half_count), 1)
        ).astype(jnp.float32) + parity
        inside = (degree <= float(wave_count - 1)).astype(jnp.float32)
        ratio = tau_scale * degree * (degree + 1.0) / float(wave_count * (wave_count - 1))
        factor = 1.0 / (1.0 + eig_ref[...] * ratio)
        spectral = jnp.dot(field, legendre, preferred_element_type=jnp.float32)
        spectral = (spectral * inside).astype(jnp.bfloat16)
        levels = modes_in.shape[0]
        solved = []
        for part in range(2):
            column = spectral[part * levels : (part + 1) * levels]
            modal = jnp.dot(modes_in[...], column, preferred_element_type=jnp.float32)
            modal = (modal * factor).astype(jnp.bfloat16)
            solved.append(
                jnp.dot(modes_out[...], modal, preferred_element_type=jnp.float32).astype(
                    jnp.bfloat16
                )
            )
        grid = lax.dot_general(
            jnp.concatenate(solved, axis=0),
            legendre,
            (((1,), (1,)), ((), ())),
            preferred_element_type=jnp.float32,
        )
        for part in range(2):
            for level in range(level_size):
                low_start = part * levels + level * tiles
                high_start = low_start + level_size * tiles
                for pair in range(wave_size // 2):
                    lanes = slice(pair * LANES, (pair + 1) * LANES)
                    low = grid[low_start : low_start + tiles, lanes]
                    high = grid[high_start : high_start + tiles, lanes]
                    a = jnp.where(low_half, low, pltpu.roll(high, LANES // 2, 1))
                    b = jnp.where(low_half, pltpu.roll(low, LANES // 2, 1), high)
                    rows_out[where_rows(2 * pair * level_size + level, part, slot), :] = a
                    rows_out[where_rows((2 * pair + 1) * level_size + level, part, slot), :] = b
        return carry

    lax.fori_loop(0, group, one_slot, 0)

    def gather(index, carry):
        place, part = index // 2, index % 2
        for tile in range(tiles):
            parts = []
            for eight in range(eights):
                start = pl.multiple_of(((index * eights + eight) * tiles + tile) * 8, 8)
                parts.append(rows_out[pl.ds(start, 8), :])
            out[place, part, :, tile * LANES : (tile + 1) * LANES] = jnp.concatenate(
                parts, axis=0
            ).astype(out.dtype)
        return carry

    lax.fori_loop(0, places * 2, gather, 0)


def columns_fused(pieces, legendre, waves, scalars, eig_rates, modes, sizes):
    wave_size, level_size, group, tiles, half_count, _, first = sizes
    places = wave_size * level_size
    half_rows = legendre.shape[1]
    width = tiles * LANES
    levels = modes[0].shape[0]
    whole = lambda shape: pl.BlockSpec(shape, lambda i: (0,) * len(shape))
    scratch = pltpu.VMEM((places * 2 * group * tiles, LANES), jnp.float32)
    values = places * 2 * group * width
    return pl.pallas_call(
        functools.partial(column_kernel, sizes),
        out_shape=jax.ShapeDtypeStruct((places, 2, group, width), jnp.bfloat16),
        grid=(1,),
        in_specs=[
            pl.BlockSpec(memory_space=pltpu.SMEM),
            pl.BlockSpec(memory_space=pltpu.SMEM),
            whole((levels, 1)),
            whole((levels, levels)),
            whole((levels, levels)),
            pl.BlockSpec((group, half_rows, half_count), lambda i: (first // group, 0, 0)),
        ]
        + [whole(piece.shape) for piece in pieces],
        out_specs=whole((places, 2, group, width)),
        scratch_shapes=[scratch, scratch],
        compiler_params=pltpu.CompilerParams(vmem_limit_bytes=56 * 2**20),
        cost_estimate=pl.CostEstimate(
            flops=values * half_rows * 6, bytes_accessed=6 * values, transcendentals=0
        ),
    )(waves, scalars, eig_rates[:, None], *modes, legendre, *pieces)


def columns_plain(mirrored, legendre, waves, parity, eig_rates, modes_in, modes_out, sizes):
    wave_size, level_size, count, first, wave_count = sizes
    levels = modes_in.shape[0]
    half_rows, half_count = legendre.shape[1:]
    local_levels, rows_here = levels // level_size, half_rows // wave_size
    shape = mirrored.shape
    mirrored = mirrored.reshape(wave_size, level_size, 2, count, local_levels, rows_here)
    field = mirrored.transpose(3, 2, 1, 4, 0, 5).reshape(count, 2, levels, half_rows)
    table = legendre[first : first + count]
    degree = (
        waves[first : first + count, None] + 2 * jnp.arange(half_count, dtype=jnp.int32)[None, :]
    ).astype(jnp.float32) + parity
    inside = (degree <= float(wave_count - 1)).astype(jnp.float32)
    ratio = tau_scale * degree * (degree + 1.0) / float(wave_count * (wave_count - 1))
    factor = 1.0 / (1.0 + ratio[:, None, :] * eig_rates[None, :, None])
    spectral = jnp.einsum("sclr,srj->sclj", field, table, preferred_element_type=jnp.float32)
    spectral = (spectral * inside[:, None, None, :]).astype(jnp.bfloat16)
    modal = jnp.einsum("kl,sclj->sckj", modes_in, spectral, preferred_element_type=jnp.float32)
    modal = (modal * factor[:, None, :, :]).astype(jnp.bfloat16)
    solved = jnp.einsum(
        "lk,sckj->sclj", modes_out, modal, preferred_element_type=jnp.float32
    ).astype(jnp.bfloat16)
    grid = jnp.einsum("sclj,srj->sclr", solved, table, preferred_element_type=jnp.float32)
    grid = grid.astype(jnp.bfloat16)
    grid = grid.reshape(count, 2, level_size, local_levels, wave_size, rows_here)
    return grid.transpose(4, 2, 1, 0, 3, 5).reshape(shape)


def shards(grid_state, legendre, wave_order, lat_order, eig_rates, modes_in, modes_out):
    out_shape = grid_state.shape
    local_levels, _, rows_here, lon_count = out_shape
    wave_size = lax.axis_size("wave")
    level_size = lax.axis_size("level")
    places = wave_size * level_size
    half_rows = lat_order.shape[0]
    wave_count = wave_order.shape[0]
    narrow, half_count = legendre.shape[0], legendre.shape[3]
    chunks = min(CHUNKS, narrow)
    count = narrow // chunks
    height = 2 * count
    width = local_levels * rows_here
    direct = (
        places <= DIRECT_LIMIT
        and rows_here * 2 == LANES
        and wave_size % 2 == 0
        and count % 16 == 0
        and local_levels % 32 == 0
    )
    parity = lax.axis_index("fld")
    wave_place = lax.axis_index("wave")
    level_place = lax.axis_index("level")
    place = wave_place * level_size + level_place
    legendre = legendre.reshape(narrow, half_rows, half_count)
    grid_state = grid_state.reshape(local_levels, rows_here, lon_count)
    hemi_sign = 1.0 - 2.0 * parity.astype(jnp.float32)
    waves = lax.dynamic_slice_in_dim(wave_order, place * narrow, narrow)
    where = jnp.stack([wave_place, level_place, parity]).astype(jnp.int32)

    def exchange(value):
        return lax.all_to_all(value, EXCHANGE_AXES, split_axis=0, concat_axis=0, tiled=True)

    def joined(other, own, scale):
        both = scale * (other.astype(jnp.float32) + hemi_sign * own.astype(jnp.float32))
        return both.astype(jnp.bfloat16)

    if not direct:
        returned, tables = [], []
        for chunk in range(chunks):
            sizes = (wave_size, level_size, chunks, chunk, False, places * height)
            value, table = fourier(grid_state, where, wave_order, lat_order, sizes)
            tables.append(table)
            own = exchange(value.reshape(places, height, width))
            mirrored = joined(partner(own, "fld"), own, 1.0)
            grid = columns_plain(
                mirrored.reshape(wave_size, level_size, 2, count, width),
                legendre,
                waves,
                parity.astype(jnp.float32),
                eig_rates,
                modes_in,
                modes_out,
                (wave_size, level_size, count, chunk * count, wave_count),
            ).reshape(places, height, width)
            hemi = exchange(joined(partner(grid, "fld"), grid, 0.5))
            returned.append((hemi.reshape(places * height, width), 0))
        current = inverse_fourier(returned, tables, grid_state.shape, 0, local_levels)
        return current.reshape(out_shape)

    tiles = width // LANES
    level_index = jnp.arange(local_levels, dtype=jnp.int32).reshape(tiles, 2).T
    sources = []
    for is_turned in (0, 1):
        shift = jnp.arange(level_size, dtype=jnp.int32)
        from_level = (level_place - shift) % level_size if is_turned else shift
        order = (from_level[None, :, None] * local_levels + level_index[:, None, :]).reshape(-1)
        shift = jnp.arange(wave_size, dtype=jnp.int32)
        from_wave = (wave_place - shift) % wave_size if is_turned else shift
        sources.append(
            (
                jnp.concatenate([from_wave, parity[None]]),
                (jnp.take(modes_in, order, axis=1), jnp.take(modes_out, order, axis=0)),
            )
        )
    shifts = [(wave, level) for wave in range(wave_size) for level in range(level_size)]

    arrived, tables = [], []
    for chunk in range(chunks):
        is_whole = chunk in WHOLE_CHUNKS
        sizes = (wave_size, level_size, chunks, chunk, not is_whole, places * height)
        value, table = fourier(grid_state, where, wave_order, lat_order, sizes)
        tables.append(table)
        if is_whole:
            arrived.append([exchange(value.reshape(places, 2, count, width))])
            continue
        other = partner(value, "fld")
        pieces = []
        for index, (wave, level) in enumerate(shifts):
            rows = slice(index * height, (index + 1) * height)
            mirrored = joined(other[rows], value[rows], 1.0)
            piece = shift_places(mirrored, wave, level)
            pieces.append(piece.reshape(2, count, width))
        arrived.append(pieces)

    half, fourth = local_levels // 2, local_levels // 4
    cuts = {chunk: [(0, local_levels)] for chunk in range(chunks)}
    cuts[1] = [(0, half), (half, half)]
    cuts[chunks - 1] = [(0, half), (half, fourth), (half + fourth, fourth)]
    returned = []
    for chunk in range(chunks):
        is_whole = chunk in WHOLE_CHUNKS
        pieces = arrived[chunk]
        if is_whole:
            pieces = [pieces[0], partner(pieces[0], "fld")]
        scalars, modes = sources[0 if is_whole else 1]
        sizes = (wave_size, level_size, count, tiles, half_count, wave_count, chunk * count)
        grid = columns_fused(pieces, legendre, waves, scalars, eig_rates, modes, sizes)
        grid = grid.reshape(places, height, width)
        other = partner(grid, "fld")
        if is_whole:
            hemi = exchange(joined(other, grid, 0.5))
            returned.append([(0, local_levels, [hemi.reshape(places * height, width)])])
            continue
        groups = []
        for start, levels in cuts[chunk]:
            lanes = slice(start * rows_here, (start + levels) * rows_here)
            pieces = []
            for index, (wave, level) in enumerate(shifts):
                hemi = joined(other[index, :, lanes], grid[index, :, lanes], 0.5)
                wave, level = (wave_size - wave) % wave_size, (level_size - level) % level_size
                pieces.append(shift_places(hemi, wave, level))
            groups.append((start, levels, pieces))
        returned.append(groups)

    def pieces_at(chunk_list, start):
        return [
            (piece, begin)
            for chunk in chunk_list
            for begin, levels, pieces in returned[chunk]
            if begin <= start < begin + levels
            for piece in pieces
        ]

    shape = grid_state.shape
    everything = list(range(chunks))
    partials = []
    for start in (0, half):
        partials.append(
            inverse_fourier(
                pieces_at(everything[:2], start),
                tables[:2],
                shape,
                start,
                half,
                dtype=jnp.bfloat16,
            )
        )
    current = None
    for start, levels in cuts[chunks - 1]:
        base = 0 if start < half else half
        current = inverse_fourier(
            pieces_at(everything[2:], start),
            tables[2:],
            shape,
            start,
            levels,
            current=current,
            partial=(partials[0 if base == 0 else 1], base),
        )
    return current.reshape(out_shape)


def solution(mesh):
    placed = (
        P(("member", "level"), "fld", "wave", None),
        P(("wave", "level"), "fld", None, None),
        P(),
        P(),
        P(),
        P(),
        P(),
    )
    return jax.shard_map(
        shards,
        mesh=mesh,
        in_specs=placed,
        out_specs=P(("member", "level"), "fld", "wave", None),
        check_vma=False,
    )
```

```python
import functools
import math

import jax
import jax.numpy as jnp
from jax import lax
from jax.experimental import pallas as pl
from jax.experimental.pallas import tpu as pltpu
from jax.sharding import PartitionSpec as P


tau_scale = 2.0
LANES = 128
CHUNKS = 4
WHOLE_CHUNKS = (0, 2)
DIRECT_LIMIT = 16
EXCHANGE_AXES = ("wave", "level")


def partner(value, axis):
    pairs = [(source, source ^ 1) for source in range(lax.axis_size(axis))]
    return lax.ppermute(value, axis, pairs)


def shift_places(value, wave_shift, level_shift):
    if wave_shift == 0 and level_shift == 0:
        return value
    waves, levels = lax.axis_size("wave"), lax.axis_size("level")
    pairs = []
    for wave in range(waves):
        for level in range(levels):
            target = (wave + wave_shift) % waves * levels + (level + level_shift) % levels
            pairs.append((wave * levels + level, target))
    return lax.ppermute(value, EXCHANGE_AXES, pairs)


def level_block(levels, rows_here, most):
    whole = levels % most == 0 and most * rows_here % LANES == 0
    return most if whole else levels


def pick(values, index):
    rows, many = index.shape[0], values.shape[1]
    hit = lax.broadcasted_iota(jnp.int32, (rows, many), 1) == index
    return jnp.sum(jnp.where(hit, values, 0.0), axis=1, keepdims=True)


def write_table(sizes, place_ref, wave_order, table):
    wave_size, level_size, chunks, chunk, turned, _ = sizes
    rows, lon_count = table.shape
    places = wave_size * level_size
    count = rows // (2 * places)
    scale = math.sqrt(2.0 / lon_count)
    row = lax.broadcasted_iota(jnp.int32, (rows, 1), 0)
    slot, place = row % count, row // (2 * count)
    part = (row // count) % 2
    if turned:
        wave = (place // level_size + place_ref[0]) % wave_size
        place = wave * level_size + (place % level_size + place_ref[1]) % level_size
    wave = pick(wave_order[...].astype(jnp.float32), (place * chunks + chunk) * count + slot)
    lane = lax.broadcasted_iota(jnp.int32, (rows, LANES), 1).astype(jnp.float32)

    def angle(steps):
        steps = steps - lon_count * jnp.floor(steps * (1.0 / lon_count))
        return steps * (2.0 * math.pi / lon_count)

    low = angle(wave * lane)
    high = angle(wave * lane * float(LANES) + part.astype(jnp.float32) * (lon_count / 4))
    low_cos, low_sin = jnp.cos(low) * scale, jnp.sin(low) * scale
    high_cos, high_sin = jnp.cos(high), jnp.sin(high)
    for block in range(lon_count // LANES):
        values = (
            high_cos[:, block : block + 1] * low_cos - high_sin[:, block : block + 1] * low_sin
        )
        table[:, block * LANES : (block + 1) * LANES] = values.astype(table.dtype)


def fourier_kernel(
    sizes, place_ref, grid_ref, wave_order, lat_order, out, table, coupling, held, arrived
):
    _, levels, rows, lon_count = held.shape
    step, steps = pl.program_id(0), pl.num_programs(0)

    def fetch(index):
        slot = index % 2
        source = grid_ref.at[pl.ds(index * levels, levels)]
        return pltpu.make_async_copy(source, held.at[slot], arrived.at[slot])

    @pl.when(step == 0)
    def _():
        fetch(step).start()
        write_table(sizes, place_ref, wave_order, table)
        row = lax.broadcasted_iota(jnp.int32, (rows, 1), 0) + place_ref[0] * rows
        latitude = pick(lat_order[...].astype(jnp.float32), row) + 0.5
        sine = jnp.sin(latitude * (math.pi / (2.0 * lat_order.shape[1])))
        sign = 1.0 - 2.0 * place_ref[2].astype(jnp.float32)
        coupling[...] = jnp.broadcast_to(0.5 * sign * sine, coupling.shape)

    @pl.when(step + 1 < steps)
    def _():
        fetch(step + 1).start()

    fetch(step).wait()
    field = held[step % 2].astype(jnp.float32)
    forcing = (field + coupling[:, :1][None] * jnp.tanh(field)).astype(jnp.bfloat16)
    forcing = forcing.reshape(levels * rows, lon_count)
    out[...] = lax.dot_general(
        table[...], forcing, (((1,), (1,)), ((), ())), preferred_element_type=jnp.float32
    ).astype(out.dtype)


def fourier(grid_state, place, wave_order, lat_order, sizes):
    levels, rows_here, lon_count = grid_state.shape
    _, _, _, _, _, height = sizes
    block = level_block(levels, rows_here, 16)
    width = levels * rows_here
    whole = lambda *shape: pl.BlockSpec(shape, lambda i: (0,) * len(shape))
    return pl.pallas_call(
        functools.partial(fourier_kernel, sizes),
        out_shape=[
            jax.ShapeDtypeStruct((height, width), jnp.bfloat16),
            jax.ShapeDtypeStruct((height, lon_count), jnp.bfloat16),
        ],
        grid=(levels // block,),
        in_specs=[
            pl.BlockSpec(memory_space=pltpu.SMEM),
            pl.BlockSpec(memory_space=pl.ANY),
            whole(1, wave_order.shape[0]),
            whole(1, lat_order.shape[0]),
        ],
        out_specs=[
            pl.BlockSpec((height, block * rows_here), lambda i: (0, i)),
            whole(height, lon_count),
        ],
        scratch_shapes=[
            pltpu.VMEM((rows_here, LANES), jnp.float32),
            pltpu.VMEM((2, block, rows_here, lon_count), jnp.bfloat16),
            pltpu.SemaphoreType.DMA((2,)),
        ],
        compiler_params=pltpu.CompilerParams(vmem_limit_bytes=56 * 2**20),
        cost_estimate=pl.CostEstimate(
            flops=2 * height * width * lon_count,
            bytes_accessed=2 * (width * lon_count + height * (width + lon_count)),
            transcendentals=width * lon_count,
        ),
    )(place, grid_state, wave_order[None], lat_order[None])


def inverse_kernel(pieces, tables, has_partial, *refs):
    out = refs[-1]
    coeffs = jnp.concatenate([ref[...] for ref in refs[:pieces]], axis=0)
    levels, rows, lon_count = out.shape
    loops = 3 if not has_partial and lon_count % (3 * LANES) == 0 else 1
    some = lon_count // loops

    def longitudes(index, carry):
        lanes = pl.ds(pl.multiple_of(index * some, some), some)
        table = jnp.concatenate([ref[:, lanes] for ref in refs[pieces : pieces + tables]], axis=0)
        current = lax.dot_general(
            coeffs, table, (((0,), (0,)), ((), ())), preferred_element_type=jnp.float32
        ).reshape(levels, rows, some)
        if has_partial:
            current = current + refs[pieces + tables][:, :, lanes]
        out[:, :, lanes] = current.astype(out.dtype)
        return carry

    if loops == 1:
        longitudes(0, 0)
    else:
        lax.fori_loop(0, loops, longitudes, 0)


def inverse_fourier(pieces, tables, shape, start, levels, current=None, partial=None, dtype=None):
    _, rows_here, lon_count = shape
    block = level_block(levels, rows_here, 8 if partial is None else levels // 2)
    width = block * rows_here
    first = start // block
    height = sum(table.shape[0] for table in tables)
    grid_block = (block, rows_here, lon_count)

    def cut(begin):
        return first - begin // block

    specs, operands, aliases = [], [], {}
    for piece, begin in pieces:
        operands.append(piece)
        specs.append(pl.BlockSpec((piece.shape[0], width), lambda i, skip=cut(begin): (0, skip + i)))
    for table in tables:
        operands.append(table)
        specs.append(
            pl.BlockSpec(table.shape, lambda i: (0, 0), pipeline_mode=pl.Buffered(1))
        )
    if partial is not None:
        operands.append(partial[0])
        specs.append(pl.BlockSpec(grid_block, lambda i, skip=cut(partial[1]): (skip + i, 0, 0)))
    if current is not None:
        aliases = {len(operands): 0}
        operands.append(current)
        specs.append(pl.BlockSpec(memory_space=pl.ANY))
    out_first = 0 if dtype is not None else first
    out_shape = (levels, rows_here, lon_count) if dtype is not None else shape
    return pl.pallas_call(
        functools.partial(inverse_kernel, len(pieces), len(tables), partial is not None),
        out_shape=jax.ShapeDtypeStruct(out_shape, dtype or jnp.bfloat16),
        grid=(levels // block,),
        in_specs=specs,
        out_specs=pl.BlockSpec(grid_block, lambda i: (out_first + i, 0, 0)),
        input_output_aliases=aliases,
        compiler_params=pltpu.CompilerParams(vmem_limit_bytes=56 * 2**20),
        cost_estimate=pl.CostEstimate(
            flops=2 * height * levels * rows_here * lon_count,
            bytes_accessed=2 * levels * rows_here * (height + lon_count),
            transcendentals=0,
        ),
    )(*operands)


def column_kernel(sizes, waves, scalars, eig_ref, modes_in, modes_out, table, *refs):
    wave_size, level_size, group, tiles, half_count, wave_count, first = sizes
    places = wave_size * level_size
    pieces, (out, rows_in, rows_out) = refs[:-3], refs[-3:]
    eights = group // 8
    rows_here = LANES // 2
    parity = scalars[wave_size].astype(jnp.float32)
    low_half = lax.broadcasted_iota(jnp.int32, (tiles, LANES), 1) < LANES // 2

    def spread(start, part, value):
        for tile in range(tiles):
            for eight in range(eights):
                row = ((start * 2 + part) * eights + eight) * tiles + tile
                rows_in[pl.ds(pl.multiple_of(row * 8, 8), 8), :] = value(tile)[
                    eight * 8 : (eight + 1) * 8
                ]

    if len(pieces) == 2:
        own, other = pieces
        sign = 1.0 - 2.0 * parity

        def combined(index, carry):
            place, part = index // 2, index % 2

            def value(tile):
                lanes = slice(tile * LANES, (tile + 1) * LANES)
                both = other[place, part, :, lanes].astype(jnp.float32) + sign * own[
                    place, part, :, lanes
                ].astype(jnp.float32)
                return both.astype(jnp.bfloat16).astype(jnp.float32)

            spread(place, part, value)
            return carry

        lax.fori_loop(0, places * 2, combined, 0)
    else:
        for place, piece in enumerate(pieces):

            def arrived(part, carry, place=place, piece=piece):
                def value(tile):
                    return piece[part, :, tile * LANES : (tile + 1) * LANES].astype(jnp.float32)

                spread(place, part, value)
                return carry

            lax.fori_loop(0, 2, arrived, 0)

    def where_rows(place, part, slot):
        eight, within = slot // 8, slot % 8
        return pl.ds((((place * 2 + part) * eights + eight) * tiles) * 8 + within, tiles, 8)

    def one_slot(slot, carry):
        legendre = jnp.concatenate(
            [
                table[slot, pl.ds(pl.multiple_of(scalars[wave] * rows_here, rows_here), rows_here), :]
                for wave in range(wave_size)
            ],
            axis=0,
        )
        stacked = []
        for part in range(2):
            low_rows, high_rows = [], []
            for level in range(level_size):
                low_pieces, high_pieces = [], []
                for pair in range(wave_size // 2):
                    a = rows_in[where_rows(2 * pair * level_size + level, part, slot), :]
                    b = rows_in[where_rows((2 * pair + 1) * level_size + level, part, slot), :]
                    low_pieces.append(jnp.where(low_half, a, pltpu.roll(b, LANES // 2, 1)))
                    high_pieces.append(jnp.where(low_half, pltpu.roll(a, LANES // 2, 1), b))
                low_rows.append(jnp.concatenate(low_pieces, axis=1))
                high_rows.append(jnp.concatenate(high_pieces, axis=1))
            stacked += low_rows + high_rows
        field = jnp.concatenate(stacked, axis=0).astype(jnp.bfloat16)
        degree = (
            waves[first + slot] + 2 * lax.broadcasted_iota(jnp.int32, (1, half_count), 1)
        ).astype(jnp.float32) + parity
        inside = (degree <= float(wave_count - 1)).astype(jnp.float32)
        ratio = tau_scale * degree * (degree + 1.0) / float(wave_count * (wave_count - 1))
        factor = 1.0 / (1.0 + eig_ref[...] * ratio)
        spectral = jnp.dot(field, legendre, preferred_element_type=jnp.float32)
        spectral = (spectral * inside).astype(jnp.bfloat16)
        levels = modes_in.shape[0]
        solved = []
        for part in range(2):
            column = spectral[part * levels : (part + 1) * levels]
            modal = jnp.dot(modes_in[...], column, preferred_element_type=jnp.float32)
            modal = (modal * factor).astype(jnp.bfloat16)
            solved.append(
                jnp.dot(modes_out[...], modal, preferred_element_type=jnp.float32).astype(
                    jnp.bfloat16
                )
            )
        grid = lax.dot_general(
            jnp.concatenate(solved, axis=0),
            legendre,
            (((1,), (1,)), ((), ())),
            preferred_element_type=jnp.float32,
        )
        for part in range(2):
            for level in range(level_size):
                low_start = part * levels + level * tiles
                high_start = low_start + level_size * tiles
                for pair in range(wave_size // 2):
                    lanes = slice(pair * LANES, (pair + 1) * LANES)
                    low = grid[low_start : low_start + tiles, lanes]
                    high = grid[high_start : high_start + tiles, lanes]
                    a = jnp.where(low_half, low, pltpu.roll(high, LANES // 2, 1))
                    b = jnp.where(low_half, pltpu.roll(low, LANES // 2, 1), high)
                    rows_out[where_rows(2 * pair * level_size + level, part, slot), :] = a
                    rows_out[where_rows((2 * pair + 1) * level_size + level, part, slot), :] = b
        return carry

    lax.fori_loop(0, group, one_slot, 0)

    def gather(index, carry):
        place, part = index // 2, index % 2
        for tile in range(tiles):
            parts = []
            for eight in range(eights):
                start = pl.multiple_of(((index * eights + eight) * tiles + tile) * 8, 8)
                parts.append(rows_out[pl.ds(start, 8), :])
            out[place, part, :, tile * LANES : (tile + 1) * LANES] = jnp.concatenate(
                parts, axis=0
            ).astype(out.dtype)
        return carry

    lax.fori_loop(0, places * 2, gather, 0)


def columns_fused(pieces, legendre, waves, scalars, eig_rates, modes, sizes):
    wave_size, level_size, group, tiles, half_count, _, first = sizes
    places = wave_size * level_size
    half_rows = legendre.shape[1]
    width = tiles * LANES
    levels = modes[0].shape[0]
    whole = lambda shape: pl.BlockSpec(shape, lambda i: (0,) * len(shape))
    scratch = pltpu.VMEM((places * 2 * group * tiles, LANES), jnp.float32)
    values = places * 2 * group * width
    return pl.pallas_call(
        functools.partial(column_kernel, sizes),
        out_shape=jax.ShapeDtypeStruct((places, 2, group, width), jnp.bfloat16),
        grid=(1,),
        in_specs=[
            pl.BlockSpec(memory_space=pltpu.SMEM),
            pl.BlockSpec(memory_space=pltpu.SMEM),
            whole((levels, 1)),
            whole((levels, levels)),
            whole((levels, levels)),
            pl.BlockSpec((group, half_rows, half_count), lambda i: (first // group, 0, 0)),
        ]
        + [whole(piece.shape) for piece in pieces],
        out_specs=whole((places, 2, group, width)),
        scratch_shapes=[scratch, scratch],
        compiler_params=pltpu.CompilerParams(vmem_limit_bytes=56 * 2**20),
        cost_estimate=pl.CostEstimate(
            flops=values * half_rows * 6, bytes_accessed=6 * values, transcendentals=0
        ),
    )(waves, scalars, eig_rates[:, None], *modes, legendre, *pieces)


def columns_plain(mirrored, legendre, waves, parity, eig_rates, modes_in, modes_out, sizes):
    wave_size, level_size, count, first, wave_count = sizes
    levels = modes_in.shape[0]
    half_rows, half_count = legendre.shape[1:]
    local_levels, rows_here = levels // level_size, half_rows // wave_size
    shape = mirrored.shape
    mirrored = mirrored.reshape(wave_size, level_size, 2, count, local_levels, rows_here)
    field = mirrored.transpose(3, 2, 1, 4, 0, 5).reshape(count, 2, levels, half_rows)
    table = legendre[first : first + count]
    degree = (
        waves[first : first + count, None] + 2 * jnp.arange(half_count, dtype=jnp.int32)[None, :]
    ).astype(jnp.float32) + parity
    inside = (degree <= float(wave_count - 1)).astype(jnp.float32)
    ratio = tau_scale * degree * (degree + 1.0) / float(wave_count * (wave_count - 1))
    factor = 1.0 / (1.0 + ratio[:, None, :] * eig_rates[None, :, None])
    spectral = jnp.einsum("sclr,srj->sclj", field, table, preferred_element_type=jnp.float32)
    spectral = (spectral * inside[:, None, None, :]).astype(jnp.bfloat16)
    modal = jnp.einsum("kl,sclj->sckj", modes_in, spectral, preferred_element_type=jnp.float32)
    modal = (modal * factor[:, None, :, :]).astype(jnp.bfloat16)
    solved = jnp.einsum(
        "lk,sckj->sclj", modes_out, modal, preferred_element_type=jnp.float32
    ).astype(jnp.bfloat16)
    grid = jnp.einsum("sclj,srj->sclr", solved, table, preferred_element_type=jnp.float32)
    grid = grid.astype(jnp.bfloat16)
    grid = grid.reshape(count, 2, level_size, local_levels, wave_size, rows_here)
    return grid.transpose(4, 2, 1, 0, 3, 5).reshape(shape)


def shards(grid_state, legendre, wave_order, lat_order, eig_rates, modes_in, modes_out):
    out_shape = grid_state.shape
    local_levels, _, rows_here, lon_count = out_shape
    wave_size = lax.axis_size("wave")
    level_size = lax.axis_size("level")
    places = wave_size * level_size
    half_rows = lat_order.shape[0]
    wave_count = wave_order.shape[0]
    narrow, half_count = legendre.shape[0], legendre.shape[3]
    chunks = min(CHUNKS, narrow)
    count = narrow // chunks
    height = 2 * count
    width = local_levels * rows_here
    direct = (
        places <= DIRECT_LIMIT
        and rows_here * 2 == LANES
        and wave_size % 2 == 0
        and count % 16 == 0
        and local_levels % 32 == 0
    )
    parity = lax.axis_index("fld")
    wave_place = lax.axis_index("wave")
    level_place = lax.axis_index("level")
    place = wave_place * level_size + level_place
    legendre = legendre.reshape(narrow, half_rows, half_count)
    grid_state = grid_state.reshape(local_levels, rows_here, lon_count)
    hemi_sign = 1.0 - 2.0 * parity.astype(jnp.float32)
    waves = lax.dynamic_slice_in_dim(wave_order, place * narrow, narrow)
    where = jnp.stack([wave_place, level_place, parity]).astype(jnp.int32)

    def exchange(value):
        return lax.all_to_all(value, EXCHANGE_AXES, split_axis=0, concat_axis=0, tiled=True)

    def joined(other, own, scale):
        both = scale * (other.astype(jnp.float32) + hemi_sign * own.astype(jnp.float32))
        return both.astype(jnp.bfloat16)

    if not direct:
        returned, tables = [], []
        for chunk in range(chunks):
            sizes = (wave_size, level_size, chunks, chunk, False, places * height)
            value, table = fourier(grid_state, where, wave_order, lat_order, sizes)
            tables.append(table)
            own = exchange(value.reshape(places, height, width))
            mirrored = joined(partner(own, "fld"), own, 1.0)
            grid = columns_plain(
                mirrored.reshape(wave_size, level_size, 2, count, width),
                legendre,
                waves,
                parity.astype(jnp.float32),
                eig_rates,
                modes_in,
                modes_out,
                (wave_size, level_size, count, chunk * count, wave_count),
            ).reshape(places, height, width)
            hemi = exchange(joined(partner(grid, "fld"), grid, 0.5))
            returned.append((hemi.reshape(places * height, width), 0))
        current = inverse_fourier(returned, tables, grid_state.shape, 0, local_levels)
        return current.reshape(out_shape)

    tiles = width // LANES
    level_index = jnp.arange(local_levels, dtype=jnp.int32).reshape(tiles, 2).T
    sources = []
    for is_turned in (0, 1):
        shift = jnp.arange(level_size, dtype=jnp.int32)
        from_level = (level_place - shift) % level_size if is_turned else shift
        order = (from_level[None, :, None] * local_levels + level_index[:, None, :]).reshape(-1)
        shift = jnp.arange(wave_size, dtype=jnp.int32)
        from_wave = (wave_place - shift) % wave_size if is_turned else shift
        sources.append(
            (
                jnp.concatenate([from_wave, parity[None]]),
                (jnp.take(modes_in, order, axis=1), jnp.take(modes_out, order, axis=0)),
            )
        )
    shifts = [(wave, level) for wave in range(wave_size) for level in range(level_size)]

    arrived, tables = [], []
    for chunk in range(chunks):
        is_whole = chunk in WHOLE_CHUNKS
        sizes = (wave_size, level_size, chunks, chunk, not is_whole, places * height)
        value, table = fourier(grid_state, where, wave_order, lat_order, sizes)
        tables.append(table)
        if is_whole:
            arrived.append([exchange(value.reshape(places, 2, count, width))])
            continue
        other = partner(value, "fld")
        pieces = []
        for index, (wave, level) in enumerate(shifts):
            rows = slice(index * height, (index + 1) * height)
            mirrored = joined(other[rows], value[rows], 1.0)
            piece = shift_places(mirrored, wave, level)
            pieces.append(piece.reshape(2, count, width))
        arrived.append(pieces)

    half, fourth = local_levels // 2, local_levels // 4
    groups = [(0, half), (half, fourth), (half + fourth, fourth)]
    cuts = {chunk: groups if chunk in (1, chunks - 1) else [(0, local_levels)] for chunk in range(chunks)}
    returned = []
    for chunk in range(chunks):
        is_whole = chunk in WHOLE_CHUNKS
        pieces = arrived[chunk]
        if is_whole:
            pieces = [pieces[0], partner(pieces[0], "fld")]
        scalars, modes = sources[0 if is_whole else 1]
        sizes = (wave_size, level_size, count, tiles, half_count, wave_count, chunk * count)
        grid = columns_fused(pieces, legendre, waves, scalars, eig_rates, modes, sizes)
        grid = grid.reshape(places, height, width)
        other = partner(grid, "fld")
        if is_whole:
            hemi = exchange(joined(other, grid, 0.5))
            returned.append([(0, local_levels, [hemi.reshape(places * height, width)])])
            continue
        sent = []
        for start, levels in cuts[chunk]:
            lanes = slice(start * rows_here, (start + levels) * rows_here)
            pieces = []
            for index, (wave, level) in enumerate(shifts):
                hemi = joined(other[index, :, lanes], grid[index, :, lanes], 0.5)
                wave, level = (wave_size - wave) % wave_size, (level_size - level) % level_size
                pieces.append(shift_places(hemi, wave, level))
            sent.append((start, levels, pieces))
        returned.append(sent)

    def pieces_at(chunk_list, start):
        return [
            (piece, begin)
            for chunk in chunk_list
            for begin, levels, pieces in returned[chunk]
            if begin <= start < begin + levels
            for piece in pieces
        ]

    shape = grid_state.shape
    everything = list(range(chunks))
    partials = []
    for start, levels in groups:
        partials.append(
            inverse_fourier(
                pieces_at(everything[:2], start),
                tables[:2],
                shape,
                start,
                levels,
                dtype=jnp.bfloat16,
            )
        )
    current = None
    for cut, (start, levels) in enumerate(groups):
        current = inverse_fourier(
            pieces_at(everything[2:], start),
            tables[2:],
            shape,
            start,
            levels,
            current=current,
            partial=(partials[cut], start),
        )
    return current.reshape(out_shape)


def solution(mesh):
    placed = (
        P(("member", "level"), "fld", "wave", None),
        P(("wave", "level"), "fld", None, None),
        P(),
        P(),
        P(),
        P(),
        P(),
    )
    return jax.shard_map(
        shards,
        mesh=mesh,
        in_specs=placed,
        out_specs=P(("member", "level"), "fld", "wave", None),
        check_vma=False,
    )
```

```python
import functools
import math

import jax
import jax.numpy as jnp
from jax import lax
from jax.experimental import pallas as pl
from jax.experimental.pallas import tpu as pltpu
from jax.sharding import PartitionSpec as P


tau_scale = 2.0
LANES = 128
CHUNKS = 4
WHOLE_CHUNKS = (0, 2)
DIRECT_LIMIT = 16
EXCHANGE_AXES = ("wave", "level")


def partner(value, axis):
    pairs = [(source, source ^ 1) for source in range(lax.axis_size(axis))]
    return lax.ppermute(value, axis, pairs)


def shift_places(value, wave_shift, level_shift):
    if wave_shift == 0 and level_shift == 0:
        return value
    waves, levels = lax.axis_size("wave"), lax.axis_size("level")
    pairs = []
    for wave in range(waves):
        for level in range(levels):
            target = (wave + wave_shift) % waves * levels + (level + level_shift) % levels
            pairs.append((wave * levels + level, target))
    return lax.ppermute(value, EXCHANGE_AXES, pairs)


def level_block(levels, rows_here, most):
    whole = levels % most == 0 and most * rows_here % LANES == 0
    return most if whole else levels


def pick(values, index):
    rows, many = index.shape[0], values.shape[1]
    hit = lax.broadcasted_iota(jnp.int32, (rows, many), 1) == index
    return jnp.sum(jnp.where(hit, values, 0.0), axis=1, keepdims=True)


def write_table(sizes, place_ref, wave_order, table):
    wave_size, level_size, chunks, chunk, turned, _ = sizes
    rows, lon_count = table.shape
    places = wave_size * level_size
    count = rows // (2 * places)
    scale = math.sqrt(2.0 / lon_count)
    row = lax.broadcasted_iota(jnp.int32, (rows, 1), 0)
    slot, place = row % count, row // (2 * count)
    part = (row // count) % 2
    if turned:
        wave = (place // level_size + place_ref[0]) % wave_size
        place = wave * level_size + (place % level_size + place_ref[1]) % level_size
    wave = pick(wave_order[...].astype(jnp.float32), (place * chunks + chunk) * count + slot)
    lane = lax.broadcasted_iota(jnp.int32, (rows, LANES), 1).astype(jnp.float32)

    def angle(steps):
        steps = steps - lon_count * jnp.floor(steps * (1.0 / lon_count))
        return steps * (2.0 * math.pi / lon_count)

    low = angle(wave * lane)
    high = angle(wave * lane * float(LANES) + part.astype(jnp.float32) * (lon_count / 4))
    low_cos, low_sin = jnp.cos(low) * scale, jnp.sin(low) * scale
    high_cos, high_sin = jnp.cos(high), jnp.sin(high)
    for block in range(lon_count // LANES):
        values = (
            high_cos[:, block : block + 1] * low_cos - high_sin[:, block : block + 1] * low_sin
        )
        table[:, block * LANES : (block + 1) * LANES] = values.astype(table.dtype)


def fourier_kernel(
    sizes, place_ref, grid_ref, wave_order, lat_order, out, table, coupling, held, arrived
):
    _, levels, rows, lon_count = held.shape
    step, steps = pl.program_id(0), pl.num_programs(0)

    def fetch(index):
        slot = index % 2
        source = grid_ref.at[pl.ds(index * levels, levels)]
        return pltpu.make_async_copy(source, held.at[slot], arrived.at[slot])

    @pl.when(step == 0)
    def _():
        fetch(step).start()
        write_table(sizes, place_ref, wave_order, table)
        row = lax.broadcasted_iota(jnp.int32, (rows, 1), 0) + place_ref[0] * rows
        latitude = pick(lat_order[...].astype(jnp.float32), row) + 0.5
        sine = jnp.sin(latitude * (math.pi / (2.0 * lat_order.shape[1])))
        sign = 1.0 - 2.0 * place_ref[2].astype(jnp.float32)
        coupling[...] = jnp.broadcast_to(0.5 * sign * sine, coupling.shape)

    @pl.when(step + 1 < steps)
    def _():
        fetch(step + 1).start()

    fetch(step).wait()
    field = held[step % 2].astype(jnp.float32)
    forcing = (field + coupling[:, :1][None] * jnp.tanh(field)).astype(jnp.bfloat16)
    forcing = forcing.reshape(levels * rows, lon_count)
    out[...] = lax.dot_general(
        table[...], forcing, (((1,), (1,)), ((), ())), preferred_element_type=jnp.float32
    ).astype(out.dtype)


def fourier(grid_state, place, wave_order, lat_order, sizes):
    levels, rows_here, lon_count = grid_state.shape
    _, _, _, _, _, height = sizes
    block = level_block(levels, rows_here, 16)
    width = levels * rows_here
    whole = lambda *shape: pl.BlockSpec(shape, lambda i: (0,) * len(shape))
    return pl.pallas_call(
        functools.partial(fourier_kernel, sizes),
        out_shape=[
            jax.ShapeDtypeStruct((height, width), jnp.bfloat16),
            jax.ShapeDtypeStruct((height, lon_count), jnp.bfloat16),
        ],
        grid=(levels // block,),
        in_specs=[
            pl.BlockSpec(memory_space=pltpu.SMEM),
            pl.BlockSpec(memory_space=pl.ANY),
            whole(1, wave_order.shape[0]),
            whole(1, lat_order.shape[0]),
        ],
        out_specs=[
            pl.BlockSpec((height, block * rows_here), lambda i: (0, i)),
            whole(height, lon_count),
        ],
        scratch_shapes=[
            pltpu.VMEM((rows_here, LANES), jnp.float32),
            pltpu.VMEM((2, block, rows_here, lon_count), jnp.bfloat16),
            pltpu.SemaphoreType.DMA((2,)),
        ],
        compiler_params=pltpu.CompilerParams(vmem_limit_bytes=56 * 2**20),
        cost_estimate=pl.CostEstimate(
            flops=2 * height * width * lon_count,
            bytes_accessed=2 * (width * lon_count + height * (width + lon_count)),
            transcendentals=width * lon_count,
        ),
    )(place, grid_state, wave_order[None], lat_order[None])


def inverse_kernel(pieces, tables, has_partial, *refs):
    out = refs[-1]
    coeffs = jnp.concatenate([ref[...] for ref in refs[:pieces]], axis=0)
    levels, rows, lon_count = out.shape
    loops = 3 if not has_partial and lon_count % (3 * LANES) == 0 else 1
    some = lon_count // loops

    def longitudes(index, carry):
        lanes = pl.ds(pl.multiple_of(index * some, some), some)
        table = jnp.concatenate([ref[:, lanes] for ref in refs[pieces : pieces + tables]], axis=0)
        current = lax.dot_general(
            coeffs, table, (((0,), (0,)), ((), ())), preferred_element_type=jnp.float32
        ).reshape(levels, rows, some)
        if has_partial:
            current = current + refs[pieces + tables][:, :, lanes]
        out[:, :, lanes] = current.astype(out.dtype)
        return carry

    if loops == 1:
        longitudes(0, 0)
    else:
        lax.fori_loop(0, loops, longitudes, 0)


def inverse_fourier(pieces, tables, shape, start, levels, current=None, partial=None, dtype=None):
    _, rows_here, lon_count = shape
    block = level_block(levels, rows_here, 8 if partial is None else levels // 2)
    width = block * rows_here
    first = start // block
    height = sum(table.shape[0] for table in tables)
    grid_block = (block, rows_here, lon_count)

    def cut(begin):
        return first - begin // block

    specs, operands, aliases = [], [], {}
    for piece, begin in pieces:
        operands.append(piece)
        specs.append(pl.BlockSpec((piece.shape[0], width), lambda i, skip=cut(begin): (0, skip + i)))
    for table in tables:
        operands.append(table)
        specs.append(
            pl.BlockSpec(table.shape, lambda i: (0, 0), pipeline_mode=pl.Buffered(1))
        )
    if partial is not None:
        operands.append(partial[0])
        specs.append(pl.BlockSpec(grid_block, lambda i, skip=cut(partial[1]): (skip + i, 0, 0)))
    if current is not None:
        aliases = {len(operands): 0}
        operands.append(current)
        specs.append(pl.BlockSpec(memory_space=pl.ANY))
    out_first = 0 if dtype is not None else first
    out_shape = (levels, rows_here, lon_count) if dtype is not None else shape
    return pl.pallas_call(
        functools.partial(inverse_kernel, len(pieces), len(tables), partial is not None),
        out_shape=jax.ShapeDtypeStruct(out_shape, dtype or jnp.bfloat16),
        grid=(levels // block,),
        in_specs=specs,
        out_specs=pl.BlockSpec(grid_block, lambda i: (out_first + i, 0, 0)),
        input_output_aliases=aliases,
        compiler_params=pltpu.CompilerParams(vmem_limit_bytes=56 * 2**20),
        cost_estimate=pl.CostEstimate(
            flops=2 * height * levels * rows_here * lon_count,
            bytes_accessed=2 * levels * rows_here * (height + lon_count),
            transcendentals=0,
        ),
    )(*operands)


def column_kernel(sizes, waves, scalars, eig_ref, modes_in, modes_out, table, *refs):
    wave_size, level_size, group, tiles, half_count, wave_count, first = sizes
    places = wave_size * level_size
    pieces, (out, rows_in, rows_out) = refs[:-3], refs[-3:]
    eights = group // 8
    rows_here = LANES // 2
    parity = scalars[wave_size].astype(jnp.float32)
    low_half = lax.broadcasted_iota(jnp.int32, (tiles, LANES), 1) < LANES // 2

    def spread(start, part, value):
        for tile in range(tiles):
            for eight in range(eights):
                row = ((start * 2 + part) * eights + eight) * tiles + tile
                rows_in[pl.ds(pl.multiple_of(row * 8, 8), 8), :] = value(tile)[
                    eight * 8 : (eight + 1) * 8
                ]

    if len(pieces) == 2:
        own, other = pieces
        sign = 1.0 - 2.0 * parity

        def combined(index, carry):
            place, part = index // 2, index % 2

            def value(tile):
                lanes = slice(tile * LANES, (tile + 1) * LANES)
                both = other[place, part, :, lanes].astype(jnp.float32) + sign * own[
                    place, part, :, lanes
                ].astype(jnp.float32)
                return both.astype(jnp.bfloat16).astype(jnp.float32)

            spread(place, part, value)
            return carry

        lax.fori_loop(0, places * 2, combined, 0)
    else:
        for place, piece in enumerate(pieces):

            def arrived(part, carry, place=place, piece=piece):
                def value(tile):
                    return piece[part, :, tile * LANES : (tile + 1) * LANES].astype(jnp.float32)

                spread(place, part, value)
                return carry

            lax.fori_loop(0, 2, arrived, 0)

    def where_rows(place, part, slot):
        eight, within = slot // 8, slot % 8
        return pl.ds((((place * 2 + part) * eights + eight) * tiles) * 8 + within, tiles, 8)

    def one_slot(slot, carry):
        legendre = jnp.concatenate(
            [
                table[slot, pl.ds(pl.multiple_of(scalars[wave] * rows_here, rows_here), rows_here), :]
                for wave in range(wave_size)
            ],
            axis=0,
        )
        stacked = []
        for part in range(2):
            low_rows, high_rows = [], []
            for level in range(level_size):
                low_pieces, high_pieces = [], []
                for pair in range(wave_size // 2):
                    a = rows_in[where_rows(2 * pair * level_size + level, part, slot), :]
                    b = rows_in[where_rows((2 * pair + 1) * level_size + level, part, slot), :]
                    low_pieces.append(jnp.where(low_half, a, pltpu.roll(b, LANES // 2, 1)))
                    high_pieces.append(jnp.where(low_half, pltpu.roll(a, LANES // 2, 1), b))
                low_rows.append(jnp.concatenate(low_pieces, axis=1))
                high_rows.append(jnp.concatenate(high_pieces, axis=1))
            stacked += low_rows + high_rows
        field = jnp.concatenate(stacked, axis=0).astype(jnp.bfloat16)
        degree = (
            waves[first + slot] + 2 * lax.broadcasted_iota(jnp.int32, (1, half_count), 1)
        ).astype(jnp.float32) + parity
        inside = (degree <= float(wave_count - 1)).astype(jnp.float32)
        ratio = tau_scale * degree * (degree + 1.0) / float(wave_count * (wave_count - 1))
        factor = 1.0 / (1.0 + eig_ref[...] * ratio)
        spectral = jnp.dot(field, legendre, preferred_element_type=jnp.float32)
        spectral = (spectral * inside).astype(jnp.bfloat16)
        levels = modes_in.shape[0]
        solved = []
        for part in range(2):
            column = spectral[part * levels : (part + 1) * levels]
            modal = jnp.dot(modes_in[...], column, preferred_element_type=jnp.float32)
            modal = (modal * factor).astype(jnp.bfloat16)
            solved.append(
                jnp.dot(modes_out[...], modal, preferred_element_type=jnp.float32).astype(
                    jnp.bfloat16
                )
            )
        grid = lax.dot_general(
            jnp.concatenate(solved, axis=0),
            legendre,
            (((1,), (1,)), ((), ())),
            preferred_element_type=jnp.float32,
        )
        for part in range(2):
            for level in range(level_size):
                low_start = part * levels + level * tiles
                high_start = low_start + level_size * tiles
                for pair in range(wave_size // 2):
                    lanes = slice(pair * LANES, (pair + 1) * LANES)
                    low = grid[low_start : low_start + tiles, lanes]
                    high = grid[high_start : high_start + tiles, lanes]
                    a = jnp.where(low_half, low, pltpu.roll(high, LANES // 2, 1))
                    b = jnp.where(low_half, pltpu.roll(low, LANES // 2, 1), high)
                    rows_out[where_rows(2 * pair * level_size + level, part, slot), :] = a
                    rows_out[where_rows((2 * pair + 1) * level_size + level, part, slot), :] = b
        return carry

    lax.fori_loop(0, group, one_slot, 0)

    def gather(index, carry):
        place, part = index // 2, index % 2
        for tile in range(tiles):
            parts = []
            for eight in range(eights):
                start = pl.multiple_of(((index * eights + eight) * tiles + tile) * 8, 8)
                parts.append(rows_out[pl.ds(start, 8), :])
            out[place, part, :, tile * LANES : (tile + 1) * LANES] = jnp.concatenate(
                parts, axis=0
            ).astype(out.dtype)
        return carry

    lax.fori_loop(0, places * 2, gather, 0)


def columns_fused(pieces, legendre, waves, scalars, eig_rates, modes, sizes):
    wave_size, level_size, group, tiles, half_count, _, first = sizes
    places = wave_size * level_size
    half_rows = legendre.shape[1]
    width = tiles * LANES
    levels = modes[0].shape[0]
    whole = lambda shape: pl.BlockSpec(shape, lambda i: (0,) * len(shape))
    scratch = pltpu.VMEM((places * 2 * group * tiles, LANES), jnp.float32)
    values = places * 2 * group * width
    return pl.pallas_call(
        functools.partial(column_kernel, sizes),
        out_shape=jax.ShapeDtypeStruct((places, 2, group, width), jnp.bfloat16),
        grid=(1,),
        in_specs=[
            pl.BlockSpec(memory_space=pltpu.SMEM),
            pl.BlockSpec(memory_space=pltpu.SMEM),
            whole((levels, 1)),
            whole((levels, levels)),
            whole((levels, levels)),
            pl.BlockSpec((group, half_rows, half_count), lambda i: (first // group, 0, 0)),
        ]
        + [whole(piece.shape) for piece in pieces],
        out_specs=whole((places, 2, group, width)),
        scratch_shapes=[scratch, scratch],
        compiler_params=pltpu.CompilerParams(vmem_limit_bytes=56 * 2**20),
        cost_estimate=pl.CostEstimate(
            flops=values * half_rows * 6, bytes_accessed=6 * values, transcendentals=0
        ),
    )(waves, scalars, eig_rates[:, None], *modes, legendre, *pieces)


def columns_plain(mirrored, legendre, waves, parity, eig_rates, modes_in, modes_out, sizes):
    wave_size, level_size, count, first, wave_count = sizes
    levels = modes_in.shape[0]
    half_rows, half_count = legendre.shape[1:]
    local_levels, rows_here = levels // level_size, half_rows // wave_size
    shape = mirrored.shape
    mirrored = mirrored.reshape(wave_size, level_size, 2, count, local_levels, rows_here)
    field = mirrored.transpose(3, 2, 1, 4, 0, 5).reshape(count, 2, levels, half_rows)
    table = legendre[first : first + count]
    degree = (
        waves[first : first + count, None] + 2 * jnp.arange(half_count, dtype=jnp.int32)[None, :]
    ).astype(jnp.float32) + parity
    inside = (degree <= float(wave_count - 1)).astype(jnp.float32)
    ratio = tau_scale * degree * (degree + 1.0) / float(wave_count * (wave_count - 1))
    factor = 1.0 / (1.0 + ratio[:, None, :] * eig_rates[None, :, None])
    spectral = jnp.einsum("sclr,srj->sclj", field, table, preferred_element_type=jnp.float32)
    spectral = (spectral * inside[:, None, None, :]).astype(jnp.bfloat16)
    modal = jnp.einsum("kl,sclj->sckj", modes_in, spectral, preferred_element_type=jnp.float32)
    modal = (modal * factor[:, None, :, :]).astype(jnp.bfloat16)
    solved = jnp.einsum(
        "lk,sckj->sclj", modes_out, modal, preferred_element_type=jnp.float32
    ).astype(jnp.bfloat16)
    grid = jnp.einsum("sclj,srj->sclr", solved, table, preferred_element_type=jnp.float32)
    grid = grid.astype(jnp.bfloat16)
    grid = grid.reshape(count, 2, level_size, local_levels, wave_size, rows_here)
    return grid.transpose(4, 2, 1, 0, 3, 5).reshape(shape)


def shards(grid_state, legendre, wave_order, lat_order, eig_rates, modes_in, modes_out):
    out_shape = grid_state.shape
    local_levels, _, rows_here, lon_count = out_shape
    wave_size = lax.axis_size("wave")
    level_size = lax.axis_size("level")
    places = wave_size * level_size
    half_rows = lat_order.shape[0]
    wave_count = wave_order.shape[0]
    narrow, half_count = legendre.shape[0], legendre.shape[3]
    chunks = min(CHUNKS, narrow)
    count = narrow // chunks
    height = 2 * count
    width = local_levels * rows_here
    direct = (
        places <= DIRECT_LIMIT
        and rows_here * 2 == LANES
        and wave_size % 2 == 0
        and count % 16 == 0
        and local_levels % 32 == 0
    )
    parity = lax.axis_index("fld")
    wave_place = lax.axis_index("wave")
    level_place = lax.axis_index("level")
    place = wave_place * level_size + level_place
    legendre = legendre.reshape(narrow, half_rows, half_count)
    grid_state = grid_state.reshape(local_levels, rows_here, lon_count)
    hemi_sign = 1.0 - 2.0 * parity.astype(jnp.float32)
    waves = lax.dynamic_slice_in_dim(wave_order, place * narrow, narrow)
    where = jnp.stack([wave_place, level_place, parity]).astype(jnp.int32)

    def exchange(value):
        return lax.all_to_all(value, EXCHANGE_AXES, split_axis=0, concat_axis=0, tiled=True)

    def joined(other, own, scale):
        both = scale * (other.astype(jnp.float32) + hemi_sign * own.astype(jnp.float32))
        return both.astype(jnp.bfloat16)

    if not direct:
        returned, tables = [], []
        for chunk in range(chunks):
            sizes = (wave_size, level_size, chunks, chunk, False, places * height)
            value, table = fourier(grid_state, where, wave_order, lat_order, sizes)
            tables.append(table)
            own = exchange(value.reshape(places, height, width))
            mirrored = joined(partner(own, "fld"), own, 1.0)
            grid = columns_plain(
                mirrored.reshape(wave_size, level_size, 2, count, width),
                legendre,
                waves,
                parity.astype(jnp.float32),
                eig_rates,
                modes_in,
                modes_out,
                (wave_size, level_size, count, chunk * count, wave_count),
            ).reshape(places, height, width)
            hemi = exchange(joined(partner(grid, "fld"), grid, 0.5))
            returned.append((hemi.reshape(places * height, width), 0))
        current = inverse_fourier(returned, tables, grid_state.shape, 0, local_levels)
        return current.reshape(out_shape)

    tiles = width // LANES
    level_index = jnp.arange(local_levels, dtype=jnp.int32).reshape(tiles, 2).T
    sources = []
    for is_turned in (0, 1):
        shift = jnp.arange(level_size, dtype=jnp.int32)
        from_level = (level_place - shift) % level_size if is_turned else shift
        order = (from_level[None, :, None] * local_levels + level_index[:, None, :]).reshape(-1)
        shift = jnp.arange(wave_size, dtype=jnp.int32)
        from_wave = (wave_place - shift) % wave_size if is_turned else shift
        sources.append(
            (
                jnp.concatenate([from_wave, parity[None]]),
                (jnp.take(modes_in, order, axis=1), jnp.take(modes_out, order, axis=0)),
            )
        )
    shifts = [(wave, level) for wave in range(wave_size) for level in range(level_size)]

    arrived, tables = [], []
    for chunk in range(chunks):
        is_whole = chunk in WHOLE_CHUNKS
        sizes = (wave_size, level_size, chunks, chunk, not is_whole, places * height)
        value, table = fourier(grid_state, where, wave_order, lat_order, sizes)
        tables.append(table)
        if is_whole:
            arrived.append([exchange(value.reshape(places, 2, count, width))])
            continue
        other = partner(value, "fld")
        pieces = []
        for index, (wave, level) in enumerate(shifts):
            rows = slice(index * height, (index + 1) * height)
            mirrored = joined(other[rows], value[rows], 1.0)
            piece = shift_places(mirrored, wave, level)
            pieces.append(piece.reshape(2, count, width))
        arrived.append(pieces)

    half, fourth = local_levels // 2, local_levels // 4
    groups = [(0, half), (half, fourth), (half + fourth, fourth)]
    cuts = {chunk: [(0, local_levels)] for chunk in range(chunks)}
    cuts[1] = [(0, half), (half, half)]
    cuts[chunks - 1] = groups
    returned = []
    for chunk in range(chunks):
        is_whole = chunk in WHOLE_CHUNKS
        pieces = arrived[chunk]
        if is_whole:
            pieces = [pieces[0], partner(pieces[0], "fld")]
        scalars, modes = sources[0 if is_whole else 1]
        sizes = (wave_size, level_size, count, tiles, half_count, wave_count, chunk * count)
        grid = columns_fused(pieces, legendre, waves, scalars, eig_rates, modes, sizes)
        grid = grid.reshape(places, height, width)
        other = partner(grid, "fld")
        if is_whole:
            hemi = exchange(joined(other, grid, 0.5))
            returned.append([(0, local_levels, [hemi.reshape(places * height, width)])])
            continue
        sent = []
        for start, levels in cuts[chunk]:
            lanes = slice(start * rows_here, (start + levels) * rows_here)
            pieces = []
            for index, (wave, level) in enumerate(shifts):
                hemi = joined(other[index, :, lanes], grid[index, :, lanes], 0.5)
                wave, level = (wave_size - wave) % wave_size, (level_size - level) % level_size
                pieces.append(shift_places(hemi, wave, level))
            sent.append((start, levels, pieces))
        returned.append(sent)

    def pieces_at(chunk_list, start):
        return [
            (piece, begin)
            for chunk in chunk_list
            for begin, levels, pieces in returned[chunk]
            if begin <= start < begin + levels
            for piece in pieces
        ]

    shape = grid_state.shape
    everything = list(range(chunks))
    partials = []
    for start, levels in cuts[1]:
        partials.append(
            inverse_fourier(
                pieces_at(everything[:2], start),
                tables[:2],
                shape,
                start,
                levels,
                dtype=jnp.bfloat16,
            )
        )
    current = None
    for start, levels in groups:
        current = inverse_fourier(
            pieces_at(everything[2:], start),
            tables[2:],
            shape,
            start,
            levels,
            current=current,
            partial=(partials[0], 0) if start < half else (partials[1], half),
        )
    return current.reshape(out_shape)


def solution(mesh):
    placed = (
        P(("member", "level"), "fld", "wave", None),
        P(("wave", "level"), "fld", None, None),
        P(),
        P(),
        P(),
        P(),
        P(),
    )
    return jax.shard_map(
        shards,
        mesh=mesh,
        in_specs=placed,
        out_specs=P(("member", "level"), "fld", "wave", None),
        check_vma=False,
    )
```

```python
import functools
import math

import jax
import jax.numpy as jnp
from jax import lax
from jax.experimental import pallas as pl
from jax.experimental.pallas import tpu as pltpu
from jax.sharding import PartitionSpec as P


tau_scale = 2.0
LANES = 128
CHUNKS = 4
WHOLE_SENDS = (0, 2)
WHOLE_BACKS = (0,)
DIRECT_LIMIT = 16
EXCHANGE_AXES = ("wave", "level")


def partner(value, axis):
    pairs = [(source, source ^ 1) for source in range(lax.axis_size(axis))]
    return lax.ppermute(value, axis, pairs)


def shift_places(value, wave_shift, level_shift):
    if wave_shift == 0 and level_shift == 0:
        return value
    waves, levels = lax.axis_size("wave"), lax.axis_size("level")
    pairs = []
    for wave in range(waves):
        for level in range(levels):
            target = (wave + wave_shift) % waves * levels + (level + level_shift) % levels
            pairs.append((wave * levels + level, target))
    return lax.ppermute(value, EXCHANGE_AXES, pairs)


def level_block(levels, rows_here, most):
    whole = levels % most == 0 and most * rows_here % LANES == 0
    return most if whole else levels


def pick(values, index):
    rows, many = index.shape[0], values.shape[1]
    hit = lax.broadcasted_iota(jnp.int32, (rows, many), 1) == index
    return jnp.sum(jnp.where(hit, values, 0.0), axis=1, keepdims=True)


def write_table(sizes, place_ref, wave_order, table):
    wave_size, level_size, chunks, chunk, turned, _ = sizes
    rows, lon_count = table.shape
    places = wave_size * level_size
    count = rows // (2 * places)
    scale = math.sqrt(2.0 / lon_count)
    row = lax.broadcasted_iota(jnp.int32, (rows, 1), 0)
    slot, place = row % count, row // (2 * count)
    part = (row // count) % 2
    if turned:
        wave = (place // level_size + place_ref[0]) % wave_size
        place = wave * level_size + (place % level_size + place_ref[1]) % level_size
    wave = pick(wave_order[...].astype(jnp.float32), (place * chunks + chunk) * count + slot)
    lane = lax.broadcasted_iota(jnp.int32, (rows, LANES), 1).astype(jnp.float32)

    def angle(steps):
        steps = steps - lon_count * jnp.floor(steps * (1.0 / lon_count))
        return steps * (2.0 * math.pi / lon_count)

    low = angle(wave * lane)
    high = angle(wave * lane * float(LANES) + part.astype(jnp.float32) * (lon_count / 4))
    low_cos, low_sin = jnp.cos(low) * scale, jnp.sin(low) * scale
    high_cos, high_sin = jnp.cos(high), jnp.sin(high)
    for block in range(lon_count // LANES):
        values = (
            high_cos[:, block : block + 1] * low_cos - high_sin[:, block : block + 1] * low_sin
        )
        table[:, block * LANES : (block + 1) * LANES] = values.astype(table.dtype)


def fourier_kernel(
    sizes, place_ref, grid_ref, wave_order, lat_order, out, table, coupling, held, arrived
):
    _, levels, rows, lon_count = held.shape
    step, steps = pl.program_id(0), pl.num_programs(0)

    def fetch(index):
        slot = index % 2
        source = grid_ref.at[pl.ds(index * levels, levels)]
        return pltpu.make_async_copy(source, held.at[slot], arrived.at[slot])

    @pl.when(step == 0)
    def _():
        fetch(step).start()
        write_table(sizes, place_ref, wave_order, table)
        row = lax.broadcasted_iota(jnp.int32, (rows, 1), 0) + place_ref[0] * rows
        latitude = pick(lat_order[...].astype(jnp.float32), row) + 0.5
        sine = jnp.sin(latitude * (math.pi / (2.0 * lat_order.shape[1])))
        sign = 1.0 - 2.0 * place_ref[2].astype(jnp.float32)
        coupling[...] = jnp.broadcast_to(0.5 * sign * sine, coupling.shape)

    @pl.when(step + 1 < steps)
    def _():
        fetch(step + 1).start()

    fetch(step).wait()
    field = held[step % 2].astype(jnp.float32)
    forcing = (field + coupling[:, :1][None] * jnp.tanh(field)).astype(jnp.bfloat16)
    forcing = forcing.reshape(levels * rows, lon_count)
    out[...] = lax.dot_general(
        table[...], forcing, (((1,), (1,)), ((), ())), preferred_element_type=jnp.float32
    ).astype(out.dtype)


def fourier(grid_state, place, wave_order, lat_order, sizes):
    levels, rows_here, lon_count = grid_state.shape
    _, _, _, _, _, height = sizes
    block = level_block(levels, rows_here, 16)
    width = levels * rows_here
    whole = lambda *shape: pl.BlockSpec(shape, lambda i: (0,) * len(shape))
    return pl.pallas_call(
        functools.partial(fourier_kernel, sizes),
        out_shape=[
            jax.ShapeDtypeStruct((height, width), jnp.bfloat16),
            jax.ShapeDtypeStruct((height, lon_count), jnp.bfloat16),
        ],
        grid=(levels // block,),
        in_specs=[
            pl.BlockSpec(memory_space=pltpu.SMEM),
            pl.BlockSpec(memory_space=pl.ANY),
            whole(1, wave_order.shape[0]),
            whole(1, lat_order.shape[0]),
        ],
        out_specs=[
            pl.BlockSpec((height, block * rows_here), lambda i: (0, i)),
            whole(height, lon_count),
        ],
        scratch_shapes=[
            pltpu.VMEM((rows_here, LANES), jnp.float32),
            pltpu.VMEM((2, block, rows_here, lon_count), jnp.bfloat16),
            pltpu.SemaphoreType.DMA((2,)),
        ],
        compiler_params=pltpu.CompilerParams(vmem_limit_bytes=56 * 2**20),
        cost_estimate=pl.CostEstimate(
            flops=2 * height * width * lon_count,
            bytes_accessed=2 * (width * lon_count + height * (width + lon_count)),
            transcendentals=width * lon_count,
        ),
    )(place, grid_state, wave_order[None], lat_order[None])


def inverse_kernel(pieces, tables, has_partial, *refs):
    out = refs[-1]
    coeffs = jnp.concatenate([ref[...] for ref in refs[:pieces]], axis=0)
    levels, rows, lon_count = out.shape
    loops = 3 if not has_partial and lon_count % (3 * LANES) == 0 else 1
    some = lon_count // loops

    def longitudes(index, carry):
        lanes = pl.ds(pl.multiple_of(index * some, some), some)
        table = jnp.concatenate([ref[:, lanes] for ref in refs[pieces : pieces + tables]], axis=0)
        current = lax.dot_general(
            coeffs, table, (((0,), (0,)), ((), ())), preferred_element_type=jnp.float32
        ).reshape(levels, rows, some)
        if has_partial:
            current = current + refs[pieces + tables][:, :, lanes]
        out[:, :, lanes] = current.astype(out.dtype)
        return carry

    if loops == 1:
        longitudes(0, 0)
    else:
        lax.fori_loop(0, loops, longitudes, 0)


def inverse_fourier(pieces, tables, shape, start, levels, current=None, partial=None, dtype=None):
    _, rows_here, lon_count = shape
    block = level_block(levels, rows_here, 8 if partial is None else levels // 2)
    width = block * rows_here
    first = start // block
    height = sum(table.shape[0] for table in tables)
    grid_block = (block, rows_here, lon_count)

    def cut(begin):
        return first - begin // block

    specs, operands, aliases = [], [], {}
    for piece, begin in pieces:
        operands.append(piece)
        specs.append(pl.BlockSpec((piece.shape[0], width), lambda i, skip=cut(begin): (0, skip + i)))
    for table in tables:
        operands.append(table)
        specs.append(
            pl.BlockSpec(table.shape, lambda i: (0, 0), pipeline_mode=pl.Buffered(1))
        )
    if partial is not None:
        operands.append(partial[0])
        specs.append(pl.BlockSpec(grid_block, lambda i, skip=cut(partial[1]): (skip + i, 0, 0)))
    if current is not None:
        aliases = {len(operands): 0}
        operands.append(current)
        specs.append(pl.BlockSpec(memory_space=pl.ANY))
    out_first = 0 if dtype is not None else first
    out_shape = (levels, rows_here, lon_count) if dtype is not None else shape
    return pl.pallas_call(
        functools.partial(inverse_kernel, len(pieces), len(tables), partial is not None),
        out_shape=jax.ShapeDtypeStruct(out_shape, dtype or jnp.bfloat16),
        grid=(levels // block,),
        in_specs=specs,
        out_specs=pl.BlockSpec(grid_block, lambda i: (out_first + i, 0, 0)),
        input_output_aliases=aliases,
        compiler_params=pltpu.CompilerParams(vmem_limit_bytes=56 * 2**20),
        cost_estimate=pl.CostEstimate(
            flops=2 * height * levels * rows_here * lon_count,
            bytes_accessed=2 * levels * rows_here * (height + lon_count),
            transcendentals=0,
        ),
    )(*operands)


def column_kernel(sizes, waves, scalars, eig_ref, modes_in, modes_out, table, *refs):
    wave_size, level_size, group, tiles, half_count, wave_count, first = sizes
    places = wave_size * level_size
    pieces, (out, rows_in, rows_out) = refs[:-3], refs[-3:]
    eights = group // 8
    rows_here = LANES // 2
    parity = scalars[wave_size].astype(jnp.float32)
    low_half = lax.broadcasted_iota(jnp.int32, (tiles, LANES), 1) < LANES // 2

    def spread(start, part, value):
        for tile in range(tiles):
            for eight in range(eights):
                row = ((start * 2 + part) * eights + eight) * tiles + tile
                rows_in[pl.ds(pl.multiple_of(row * 8, 8), 8), :] = value(tile)[
                    eight * 8 : (eight + 1) * 8
                ]

    if len(pieces) == 2:
        own, other = pieces
        sign = 1.0 - 2.0 * parity

        def combined(index, carry):
            place, part = index // 2, index % 2

            def value(tile):
                lanes = slice(tile * LANES, (tile + 1) * LANES)
                both = other[place, part, :, lanes].astype(jnp.float32) + sign * own[
                    place, part, :, lanes
                ].astype(jnp.float32)
                return both.astype(jnp.bfloat16).astype(jnp.float32)

            spread(place, part, value)
            return carry

        lax.fori_loop(0, places * 2, combined, 0)
    else:
        for place, piece in enumerate(pieces):

            def arrived(part, carry, place=place, piece=piece):
                def value(tile):
                    return piece[part, :, tile * LANES : (tile + 1) * LANES].astype(jnp.float32)

                spread(place, part, value)
                return carry

            lax.fori_loop(0, 2, arrived, 0)

    def where_rows(place, part, slot):
        eight, within = slot // 8, slot % 8
        return pl.ds((((place * 2 + part) * eights + eight) * tiles) * 8 + within, tiles, 8)

    def one_slot(slot, carry):
        legendre = jnp.concatenate(
            [
                table[slot, pl.ds(pl.multiple_of(scalars[wave] * rows_here, rows_here), rows_here), :]
                for wave in range(wave_size)
            ],
            axis=0,
        )
        stacked = []
        for part in range(2):
            low_rows, high_rows = [], []
            for level in range(level_size):
                low_pieces, high_pieces = [], []
                for pair in range(wave_size // 2):
                    a = rows_in[where_rows(2 * pair * level_size + level, part, slot), :]
                    b = rows_in[where_rows((2 * pair + 1) * level_size + level, part, slot), :]
                    low_pieces.append(jnp.where(low_half, a, pltpu.roll(b, LANES // 2, 1)))
                    high_pieces.append(jnp.where(low_half, pltpu.roll(a, LANES // 2, 1), b))
                low_rows.append(jnp.concatenate(low_pieces, axis=1))
                high_rows.append(jnp.concatenate(high_pieces, axis=1))
            stacked += low_rows + high_rows
        field = jnp.concatenate(stacked, axis=0).astype(jnp.bfloat16)
        degree = (
            waves[first + slot] + 2 * lax.broadcasted_iota(jnp.int32, (1, half_count), 1)
        ).astype(jnp.float32) + parity
        inside = (degree <= float(wave_count - 1)).astype(jnp.float32)
        ratio = tau_scale * degree * (degree + 1.0) / float(wave_count * (wave_count - 1))
        factor = 1.0 / (1.0 + eig_ref[...] * ratio)
        spectral = jnp.dot(field, legendre, preferred_element_type=jnp.float32)
        spectral = (spectral * inside).astype(jnp.bfloat16)
        levels = modes_in.shape[0]
        solved = []
        for part in range(2):
            column = spectral[part * levels : (part + 1) * levels]
            modal = jnp.dot(modes_in[...], column, preferred_element_type=jnp.float32)
            modal = (modal * factor).astype(jnp.bfloat16)
            solved.append(
                jnp.dot(modes_out[...], modal, preferred_element_type=jnp.float32).astype(
                    jnp.bfloat16
                )
            )
        grid = lax.dot_general(
            jnp.concatenate(solved, axis=0),
            legendre,
            (((1,), (1,)), ((), ())),
            preferred_element_type=jnp.float32,
        )
        for part in range(2):
            for level in range(level_size):
                low_start = part * levels + level * tiles
                high_start = low_start + level_size * tiles
                for pair in range(wave_size // 2):
                    lanes = slice(pair * LANES, (pair + 1) * LANES)
                    low = grid[low_start : low_start + tiles, lanes]
                    high = grid[high_start : high_start + tiles, lanes]
                    a = jnp.where(low_half, low, pltpu.roll(high, LANES // 2, 1))
                    b = jnp.where(low_half, pltpu.roll(low, LANES // 2, 1), high)
                    rows_out[where_rows(2 * pair * level_size + level, part, slot), :] = a
                    rows_out[where_rows((2 * pair + 1) * level_size + level, part, slot), :] = b
        return carry

    lax.fori_loop(0, group, one_slot, 0)

    def gather(index, carry):
        place, part = index // 2, index % 2
        for tile in range(tiles):
            parts = []
            for eight in range(eights):
                start = pl.multiple_of(((index * eights + eight) * tiles + tile) * 8, 8)
                parts.append(rows_out[pl.ds(start, 8), :])
            out[place, part, :, tile * LANES : (tile + 1) * LANES] = jnp.concatenate(
                parts, axis=0
            ).astype(out.dtype)
        return carry

    lax.fori_loop(0, places * 2, gather, 0)


def columns_fused(pieces, legendre, waves, scalars, eig_rates, modes, sizes):
    wave_size, level_size, group, tiles, half_count, _, first = sizes
    places = wave_size * level_size
    half_rows = legendre.shape[1]
    width = tiles * LANES
    levels = modes[0].shape[0]
    whole = lambda shape: pl.BlockSpec(shape, lambda i: (0,) * len(shape))
    scratch = pltpu.VMEM((places * 2 * group * tiles, LANES), jnp.float32)
    values = places * 2 * group * width
    return pl.pallas_call(
        functools.partial(column_kernel, sizes),
        out_shape=jax.ShapeDtypeStruct((places, 2, group, width), jnp.bfloat16),
        grid=(1,),
        in_specs=[
            pl.BlockSpec(memory_space=pltpu.SMEM),
            pl.BlockSpec(memory_space=pltpu.SMEM),
            whole((levels, 1)),
            whole((levels, levels)),
            whole((levels, levels)),
            pl.BlockSpec((group, half_rows, half_count), lambda i: (first // group, 0, 0)),
        ]
        + [whole(piece.shape) for piece in pieces],
        out_specs=whole((places, 2, group, width)),
        scratch_shapes=[scratch, scratch],
        compiler_params=pltpu.CompilerParams(vmem_limit_bytes=56 * 2**20),
        cost_estimate=pl.CostEstimate(
            flops=values * half_rows * 6, bytes_accessed=6 * values, transcendentals=0
        ),
    )(waves, scalars, eig_rates[:, None], *modes, legendre, *pieces)


def columns_plain(mirrored, legendre, waves, parity, eig_rates, modes_in, modes_out, sizes):
    wave_size, level_size, count, first, wave_count = sizes
    levels = modes_in.shape[0]
    half_rows, half_count = legendre.shape[1:]
    local_levels, rows_here = levels // level_size, half_rows // wave_size
    shape = mirrored.shape
    mirrored = mirrored.reshape(wave_size, level_size, 2, count, local_levels, rows_here)
    field = mirrored.transpose(3, 2, 1, 4, 0, 5).reshape(count, 2, levels, half_rows)
    table = legendre[first : first + count]
    degree = (
        waves[first : first + count, None] + 2 * jnp.arange(half_count, dtype=jnp.int32)[None, :]
    ).astype(jnp.float32) + parity
    inside = (degree <= float(wave_count - 1)).astype(jnp.float32)
    ratio = tau_scale * degree * (degree + 1.0) / float(wave_count * (wave_count - 1))
    factor = 1.0 / (1.0 + ratio[:, None, :] * eig_rates[None, :, None])
    spectral = jnp.einsum("sclr,srj->sclj", field, table, preferred_element_type=jnp.float32)
    spectral = (spectral * inside[:, None, None, :]).astype(jnp.bfloat16)
    modal = jnp.einsum("kl,sclj->sckj", modes_in, spectral, preferred_element_type=jnp.float32)
    modal = (modal * factor[:, None, :, :]).astype(jnp.bfloat16)
    solved = jnp.einsum(
        "lk,sckj->sclj", modes_out, modal, preferred_element_type=jnp.float32
    ).astype(jnp.bfloat16)
    grid = jnp.einsum("sclj,srj->sclr", solved, table, preferred_element_type=jnp.float32)
    grid = grid.astype(jnp.bfloat16)
    grid = grid.reshape(count, 2, level_size, local_levels, wave_size, rows_here)
    return grid.transpose(4, 2, 1, 0, 3, 5).reshape(shape)


def shards(grid_state, legendre, wave_order, lat_order, eig_rates, modes_in, modes_out):
    out_shape = grid_state.shape
    local_levels, _, rows_here, lon_count = out_shape
    wave_size = lax.axis_size("wave")
    level_size = lax.axis_size("level")
    places = wave_size * level_size
    half_rows = lat_order.shape[0]
    wave_count = wave_order.shape[0]
    narrow, half_count = legendre.shape[0], legendre.shape[3]
    chunks = min(CHUNKS, narrow)
    count = narrow // chunks
    height = 2 * count
    width = local_levels * rows_here
    direct = (
        places <= DIRECT_LIMIT
        and rows_here * 2 == LANES
        and wave_size % 2 == 0
        and count % 16 == 0
        and local_levels % 32 == 0
    )
    parity = lax.axis_index("fld")
    wave_place = lax.axis_index("wave")
    level_place = lax.axis_index("level")
    place = wave_place * level_size + level_place
    legendre = legendre.reshape(narrow, half_rows, half_count)
    grid_state = grid_state.reshape(local_levels, rows_here, lon_count)
    hemi_sign = 1.0 - 2.0 * parity.astype(jnp.float32)
    waves = lax.dynamic_slice_in_dim(wave_order, place * narrow, narrow)
    where = jnp.stack([wave_place, level_place, parity]).astype(jnp.int32)

    def exchange(value):
        return lax.all_to_all(value, EXCHANGE_AXES, split_axis=0, concat_axis=0, tiled=True)

    def joined(other, own, scale):
        both = scale * (other.astype(jnp.float32) + hemi_sign * own.astype(jnp.float32))
        return both.astype(jnp.bfloat16)

    def block_at(value, wave, level):
        place = (wave_place + wave) % wave_size * level_size + (level_place + level) % level_size
        return lax.dynamic_index_in_dim(value, place, 0, keepdims=False)

    if not direct:
        returned, tables = [], []
        for chunk in range(chunks):
            sizes = (wave_size, level_size, chunks, chunk, False, places * height)
            value, table = fourier(grid_state, where, wave_order, lat_order, sizes)
            tables.append(table)
            own = exchange(value.reshape(places, height, width))
            mirrored = joined(partner(own, "fld"), own, 1.0)
            grid = columns_plain(
                mirrored.reshape(wave_size, level_size, 2, count, width),
                legendre,
                waves,
                parity.astype(jnp.float32),
                eig_rates,
                modes_in,
                modes_out,
                (wave_size, level_size, count, chunk * count, wave_count),
            ).reshape(places, height, width)
            hemi = exchange(joined(partner(grid, "fld"), grid, 0.5))
            returned.append((hemi.reshape(places * height, width), 0))
        current = inverse_fourier(returned, tables, grid_state.shape, 0, local_levels)
        return current.reshape(out_shape)

    tiles = width // LANES
    level_index = jnp.arange(local_levels, dtype=jnp.int32).reshape(tiles, 2).T
    sources = []
    for is_turned in (0, 1):
        shift = jnp.arange(level_size, dtype=jnp.int32)
        from_level = (level_place - shift) % level_size if is_turned else shift
        order = (from_level[None, :, None] * local_levels + level_index[:, None, :]).reshape(-1)
        shift = jnp.arange(wave_size, dtype=jnp.int32)
        from_wave = (wave_place - shift) % wave_size if is_turned else shift
        sources.append(
            (
                jnp.concatenate([from_wave, parity[None]]),
                (jnp.take(modes_in, order, axis=1), jnp.take(modes_out, order, axis=0)),
            )
        )
    shifts = [(wave, level) for wave in range(wave_size) for level in range(level_size)]

    arrived, tables = [], []
    for chunk in range(chunks):
        is_whole = chunk in WHOLE_SENDS
        sizes = (wave_size, level_size, chunks, chunk, not is_whole, places * height)
        value, table = fourier(grid_state, where, wave_order, lat_order, sizes)
        tables.append(table)
        if is_whole:
            arrived.append([exchange(value.reshape(places, 2, count, width))])
            continue
        other = partner(value, "fld")
        pieces = []
        for index, (wave, level) in enumerate(shifts):
            rows = slice(index * height, (index + 1) * height)
            mirrored = joined(other[rows], value[rows], 1.0)
            piece = shift_places(mirrored, wave, level)
            pieces.append(piece.reshape(2, count, width))
        arrived.append(pieces)

    half, fourth = local_levels // 2, local_levels // 4
    groups = [(0, half), (half, fourth), (half + fourth, fourth)]
    cuts = {chunk: [(0, local_levels)] for chunk in range(chunks)}
    cuts[1] = [(0, half), (half, half)]
    cuts[chunks - 1] = groups
    returned = []
    for chunk in range(chunks):
        is_whole = chunk in WHOLE_SENDS
        pieces = arrived[chunk]
        if is_whole:
            pieces = [pieces[0], partner(pieces[0], "fld")]
        scalars, modes = sources[0 if is_whole else 1]
        sizes = (wave_size, level_size, count, tiles, half_count, wave_count, chunk * count)
        grid = columns_fused(pieces, legendre, waves, scalars, eig_rates, modes, sizes)
        grid = grid.reshape(places, height, width)
        other = partner(grid, "fld")
        if chunk in WHOLE_BACKS:
            hemi = exchange(joined(other, grid, 0.5))
            returned.append([(0, local_levels, [hemi.reshape(places * height, width)])])
            continue
        sent = []
        if is_whole:
            blocks = tables[chunk].reshape(places, height, lon_count)
            blocks = [block_at(blocks, wave, level) for wave, level in shifts]
            tables[chunk] = jnp.concatenate(blocks, axis=0)
        for start, levels in cuts[chunk]:
            lanes = slice(start * rows_here, (start + levels) * rows_here)
            pieces = []
            for index, (wave, level) in enumerate(shifts):
                if is_whole:
                    pair = block_at(other, -wave, -level), block_at(grid, -wave, -level)
                else:
                    pair = other[index, :, lanes], grid[index, :, lanes]
                hemi = joined(*pair, 0.5)
                wave, level = (wave_size - wave) % wave_size, (level_size - level) % level_size
                pieces.append(shift_places(hemi, wave, level))
            sent.append((start, levels, pieces))
        returned.append(sent)

    def pieces_at(chunk_list, start):
        return [
            (piece, begin)
            for chunk in chunk_list
            for begin, levels, pieces in returned[chunk]
            if begin <= start < begin + levels
            for piece in pieces
        ]

    shape = grid_state.shape
    everything = list(range(chunks))
    partials = []
    for start, levels in cuts[1]:
        partials.append(
            inverse_fourier(
                pieces_at(everything[:2], start),
                tables[:2],
                shape,
                start,
                levels,
                dtype=jnp.bfloat16,
            )
        )
    current = None
    for start, levels in groups:
        current = inverse_fourier(
            pieces_at(everything[2:], start),
            tables[2:],
            shape,
            start,
            levels,
            current=current,
            partial=(partials[0], 0) if start < half else (partials[1], half),
        )
    return current.reshape(out_shape)


def solution(mesh):
    placed = (
        P(("member", "level"), "fld", "wave", None),
        P(("wave", "level"), "fld", None, None),
        P(),
        P(),
        P(),
        P(),
        P(),
    )
    return jax.shard_map(
        shards,
        mesh=mesh,
        in_specs=placed,
        out_specs=P(("member", "level"), "fld", "wave", None),
        check_vma=False,
    )
```

```python
import functools
import math

import jax
import jax.numpy as jnp
from jax import lax
from jax.experimental import pallas as pl
from jax.experimental.pallas import tpu as pltpu
from jax.sharding import PartitionSpec as P


tau_scale = 2.0
LANES = 128
CHUNKS = 4
WHOLE_SENDS = (0, 2)
WHOLE_BACKS = (0,)
DIRECT_LIMIT = 16
EXCHANGE_AXES = ("wave", "level")


def partner(value, axis):
    pairs = [(source, source ^ 1) for source in range(lax.axis_size(axis))]
    return lax.ppermute(value, axis, pairs)


def shift_places(value, wave_shift, level_shift):
    if wave_shift == 0 and level_shift == 0:
        return value
    waves, levels = lax.axis_size("wave"), lax.axis_size("level")
    pairs = []
    for wave in range(waves):
        for level in range(levels):
            target = (wave + wave_shift) % waves * levels + (level + level_shift) % levels
            pairs.append((wave * levels + level, target))
    return lax.ppermute(value, EXCHANGE_AXES, pairs)


def level_block(levels, rows_here, most):
    whole = levels % most == 0 and most * rows_here % LANES == 0
    return most if whole else levels


def pick(values, index):
    rows, many = index.shape[0], values.shape[1]
    hit = lax.broadcasted_iota(jnp.int32, (rows, many), 1) == index
    return jnp.sum(jnp.where(hit, values, 0.0), axis=1, keepdims=True)


def write_table(sizes, place_ref, wave_order, table):
    wave_size, level_size, chunks, chunk, turned, _ = sizes
    rows, lon_count = table.shape
    places = wave_size * level_size
    count = rows // (2 * places)
    scale = math.sqrt(2.0 / lon_count)
    row = lax.broadcasted_iota(jnp.int32, (rows, 1), 0)
    slot, place = row % count, row // (2 * count)
    part = (row // count) % 2
    if turned:
        wave = (place // level_size + place_ref[0]) % wave_size
        place = wave * level_size + (place % level_size + place_ref[1]) % level_size
    wave = pick(wave_order[...].astype(jnp.float32), (place * chunks + chunk) * count + slot)
    lane = lax.broadcasted_iota(jnp.int32, (rows, LANES), 1).astype(jnp.float32)

    def angle(steps):
        steps = steps - lon_count * jnp.floor(steps * (1.0 / lon_count))
        return steps * (2.0 * math.pi / lon_count)

    low = angle(wave * lane)
    high = angle(wave * lane * float(LANES) + part.astype(jnp.float32) * (lon_count / 4))
    low_cos, low_sin = jnp.cos(low) * scale, jnp.sin(low) * scale
    high_cos, high_sin = jnp.cos(high), jnp.sin(high)
    for block in range(lon_count // LANES):
        values = (
            high_cos[:, block : block + 1] * low_cos - high_sin[:, block : block + 1] * low_sin
        )
        table[:, block * LANES : (block + 1) * LANES] = values.astype(table.dtype)


def fourier_kernel(
    sizes, place_ref, grid_ref, wave_order, lat_order, out, table, coupling, held, arrived
):
    _, levels, rows, lon_count = held.shape
    step, steps = pl.program_id(0), pl.num_programs(0)

    def fetch(index):
        slot = index % 2
        source = grid_ref.at[pl.ds(index * levels, levels)]
        return pltpu.make_async_copy(source, held.at[slot], arrived.at[slot])

    @pl.when(step == 0)
    def _():
        fetch(step).start()
        write_table(sizes, place_ref, wave_order, table)
        row = lax.broadcasted_iota(jnp.int32, (rows, 1), 0) + place_ref[0] * rows
        latitude = pick(lat_order[...].astype(jnp.float32), row) + 0.5
        sine = jnp.sin(latitude * (math.pi / (2.0 * lat_order.shape[1])))
        sign = 1.0 - 2.0 * place_ref[2].astype(jnp.float32)
        coupling[...] = jnp.broadcast_to(0.5 * sign * sine, coupling.shape)

    @pl.when(step + 1 < steps)
    def _():
        fetch(step + 1).start()

    fetch(step).wait()
    field = held[step % 2].astype(jnp.float32)
    forcing = (field + coupling[:, :1][None] * jnp.tanh(field)).astype(jnp.bfloat16)
    forcing = forcing.reshape(levels * rows, lon_count)
    out[...] = lax.dot_general(
        table[...], forcing, (((1,), (1,)), ((), ())), preferred_element_type=jnp.float32
    ).astype(out.dtype)


def fourier(grid_state, place, wave_order, lat_order, sizes):
    levels, rows_here, lon_count = grid_state.shape
    _, _, _, _, _, height = sizes
    block = level_block(levels, rows_here, 16)
    width = levels * rows_here
    whole = lambda *shape: pl.BlockSpec(shape, lambda i: (0,) * len(shape))
    return pl.pallas_call(
        functools.partial(fourier_kernel, sizes),
        out_shape=[
            jax.ShapeDtypeStruct((height, width), jnp.bfloat16),
            jax.ShapeDtypeStruct((height, lon_count), jnp.bfloat16),
        ],
        grid=(levels // block,),
        in_specs=[
            pl.BlockSpec(memory_space=pltpu.SMEM),
            pl.BlockSpec(memory_space=pl.ANY),
            whole(1, wave_order.shape[0]),
            whole(1, lat_order.shape[0]),
        ],
        out_specs=[
            pl.BlockSpec((height, block * rows_here), lambda i: (0, i)),
            whole(height, lon_count),
        ],
        scratch_shapes=[
            pltpu.VMEM((rows_here, LANES), jnp.float32),
            pltpu.VMEM((2, block, rows_here, lon_count), jnp.bfloat16),
            pltpu.SemaphoreType.DMA((2,)),
        ],
        compiler_params=pltpu.CompilerParams(vmem_limit_bytes=56 * 2**20),
        cost_estimate=pl.CostEstimate(
            flops=2 * height * width * lon_count,
            bytes_accessed=2 * (width * lon_count + height * (width + lon_count)),
            transcendentals=width * lon_count,
        ),
    )(place, grid_state, wave_order[None], lat_order[None])


def inverse_kernel(pieces, tables, has_partial, *refs):
    out = refs[-1]
    coeffs = jnp.concatenate([ref[...] for ref in refs[:pieces]], axis=0)
    levels, rows, lon_count = out.shape
    loops = 3 if not has_partial and lon_count % (3 * LANES) == 0 else 1
    some = lon_count // loops

    def longitudes(index, carry):
        lanes = pl.ds(pl.multiple_of(index * some, some), some)
        table = jnp.concatenate([ref[:, lanes] for ref in refs[pieces : pieces + tables]], axis=0)
        current = lax.dot_general(
            coeffs, table, (((0,), (0,)), ((), ())), preferred_element_type=jnp.float32
        ).reshape(levels, rows, some)
        if has_partial:
            current = current + refs[pieces + tables][:, :, lanes]
        out[:, :, lanes] = current.astype(out.dtype)
        return carry

    if loops == 1:
        longitudes(0, 0)
    else:
        lax.fori_loop(0, loops, longitudes, 0)


def inverse_fourier(pieces, tables, shape, start, levels, current=None, partial=None, dtype=None):
    _, rows_here, lon_count = shape
    block = level_block(levels, rows_here, 8 if partial is None or levels <= 16 else 16)
    width = block * rows_here
    first = start // block
    height = sum(table.shape[0] for table in tables)
    grid_block = (block, rows_here, lon_count)

    def cut(begin):
        return first - begin // block

    specs, operands, aliases = [], [], {}
    for piece, begin in pieces:
        operands.append(piece)
        specs.append(pl.BlockSpec((piece.shape[0], width), lambda i, skip=cut(begin): (0, skip + i)))
    for table in tables:
        operands.append(table)
        specs.append(
            pl.BlockSpec(table.shape, lambda i: (0, 0), pipeline_mode=pl.Buffered(1))
        )
    if partial is not None:
        operands.append(partial[0])
        specs.append(pl.BlockSpec(grid_block, lambda i, skip=cut(partial[1]): (skip + i, 0, 0)))
    if current is not None:
        aliases = {len(operands): 0}
        operands.append(current)
        specs.append(pl.BlockSpec(memory_space=pl.ANY))
    out_first = 0 if dtype is not None else first
    out_shape = (levels, rows_here, lon_count) if dtype is not None else shape
    return pl.pallas_call(
        functools.partial(inverse_kernel, len(pieces), len(tables), partial is not None),
        out_shape=jax.ShapeDtypeStruct(out_shape, dtype or jnp.bfloat16),
        grid=(levels // block,),
        in_specs=specs,
        out_specs=pl.BlockSpec(grid_block, lambda i: (out_first + i, 0, 0)),
        input_output_aliases=aliases,
        compiler_params=pltpu.CompilerParams(vmem_limit_bytes=56 * 2**20),
        cost_estimate=pl.CostEstimate(
            flops=2 * height * levels * rows_here * lon_count,
            bytes_accessed=2 * levels * rows_here * (height + lon_count),
            transcendentals=0,
        ),
    )(*operands)


def column_kernel(sizes, waves, scalars, eig_ref, modes_in, modes_out, table, *refs):
    wave_size, level_size, group, tiles, half_count, wave_count, first = sizes
    places = wave_size * level_size
    pieces, (out, rows_in, rows_out) = refs[:-3], refs[-3:]
    eights = group // 8
    rows_here = LANES // 2
    parity = scalars[wave_size].astype(jnp.float32)
    low_half = lax.broadcasted_iota(jnp.int32, (tiles, LANES), 1) < LANES // 2

    def spread(start, part, value):
        for tile in range(tiles):
            for eight in range(eights):
                row = ((start * 2 + part) * eights + eight) * tiles + tile
                rows_in[pl.ds(pl.multiple_of(row * 8, 8), 8), :] = value(tile)[
                    eight * 8 : (eight + 1) * 8
                ]

    if len(pieces) == 2:
        own, other = pieces
        sign = 1.0 - 2.0 * parity

        def combined(index, carry):
            place, part = index // 2, index % 2

            def value(tile):
                lanes = slice(tile * LANES, (tile + 1) * LANES)
                both = other[place, part, :, lanes].astype(jnp.float32) + sign * own[
                    place, part, :, lanes
                ].astype(jnp.float32)
                return both.astype(jnp.bfloat16).astype(jnp.float32)

            spread(place, part, value)
            return carry

        lax.fori_loop(0, places * 2, combined, 0)
    else:
        for place, piece in enumerate(pieces):

            def arrived(part, carry, place=place, piece=piece):
                def value(tile):
                    return piece[part, :, tile * LANES : (tile + 1) * LANES].astype(jnp.float32)

                spread(place, part, value)
                return carry

            lax.fori_loop(0, 2, arrived, 0)

    def where_rows(place, part, slot):
        eight, within = slot // 8, slot % 8
        return pl.ds((((place * 2 + part) * eights + eight) * tiles) * 8 + within, tiles, 8)

    def one_slot(slot, carry):
        legendre = jnp.concatenate(
            [
                table[slot, pl.ds(pl.multiple_of(scalars[wave] * rows_here, rows_here), rows_here), :]
                for wave in range(wave_size)
            ],
            axis=0,
        )
        stacked = []
        for part in range(2):
            low_rows, high_rows = [], []
            for level in range(level_size):
                low_pieces, high_pieces = [], []
                for pair in range(wave_size // 2):
                    a = rows_in[where_rows(2 * pair * level_size + level, part, slot), :]
                    b = rows_in[where_rows((2 * pair + 1) * level_size + level, part, slot), :]
                    low_pieces.append(jnp.where(low_half, a, pltpu.roll(b, LANES // 2, 1)))
                    high_pieces.append(jnp.where(low_half, pltpu.roll(a, LANES // 2, 1), b))
                low_rows.append(jnp.concatenate(low_pieces, axis=1))
                high_rows.append(jnp.concatenate(high_pieces, axis=1))
            stacked += low_rows + high_rows
        field = jnp.concatenate(stacked, axis=0).astype(jnp.bfloat16)
        degree = (
            waves[first + slot] + 2 * lax.broadcasted_iota(jnp.int32, (1, half_count), 1)
        ).astype(jnp.float32) + parity
        inside = (degree <= float(wave_count - 1)).astype(jnp.float32)
        ratio = tau_scale * degree * (degree + 1.0) / float(wave_count * (wave_count - 1))
        factor = 1.0 / (1.0 + eig_ref[...] * ratio)
        spectral = jnp.dot(field, legendre, preferred_element_type=jnp.float32)
        spectral = (spectral * inside).astype(jnp.bfloat16)
        levels = modes_in.shape[0]
        solved = []
        for part in range(2):
            column = spectral[part * levels : (part + 1) * levels]
            modal = jnp.dot(modes_in[...], column, preferred_element_type=jnp.float32)
            modal = (modal * factor).astype(jnp.bfloat16)
            solved.append(
                jnp.dot(modes_out[...], modal, preferred_element_type=jnp.float32).astype(
                    jnp.bfloat16
                )
            )
        grid = lax.dot_general(
            jnp.concatenate(solved, axis=0),
            legendre,
            (((1,), (1,)), ((), ())),
            preferred_element_type=jnp.float32,
        )
        for part in range(2):
            for level in range(level_size):
                low_start = part * levels + level * tiles
                high_start = low_start + level_size * tiles
                for pair in range(wave_size // 2):
                    lanes = slice(pair * LANES, (pair + 1) * LANES)
                    low = grid[low_start : low_start + tiles, lanes]
                    high = grid[high_start : high_start + tiles, lanes]
                    a = jnp.where(low_half, low, pltpu.roll(high, LANES // 2, 1))
                    b = jnp.where(low_half, pltpu.roll(low, LANES // 2, 1), high)
                    rows_out[where_rows(2 * pair * level_size + level, part, slot), :] = a
                    rows_out[where_rows((2 * pair + 1) * level_size + level, part, slot), :] = b
        return carry

    lax.fori_loop(0, group, one_slot, 0)

    def gather(index, carry):
        place, part = index // 2, index % 2
        for tile in range(tiles):
            parts = []
            for eight in range(eights):
                start = pl.multiple_of(((index * eights + eight) * tiles + tile) * 8, 8)
                parts.append(rows_out[pl.ds(start, 8), :])
            out[place, part, :, tile * LANES : (tile + 1) * LANES] = jnp.concatenate(
                parts, axis=0
            ).astype(out.dtype)
        return carry

    lax.fori_loop(0, places * 2, gather, 0)


def columns_fused(pieces, legendre, waves, scalars, eig_rates, modes, sizes):
    wave_size, level_size, group, tiles, half_count, _, first = sizes
    places = wave_size * level_size
    half_rows = legendre.shape[1]
    width = tiles * LANES
    levels = modes[0].shape[0]
    whole = lambda shape: pl.BlockSpec(shape, lambda i: (0,) * len(shape))
    scratch = pltpu.VMEM((places * 2 * group * tiles, LANES), jnp.float32)
    values = places * 2 * group * width
    return pl.pallas_call(
        functools.partial(column_kernel, sizes),
        out_shape=jax.ShapeDtypeStruct((places, 2, group, width), jnp.bfloat16),
        grid=(1,),
        in_specs=[
            pl.BlockSpec(memory_space=pltpu.SMEM),
            pl.BlockSpec(memory_space=pltpu.SMEM),
            whole((levels, 1)),
            whole((levels, levels)),
            whole((levels, levels)),
            pl.BlockSpec((group, half_rows, half_count), lambda i: (first // group, 0, 0)),
        ]
        + [whole(piece.shape) for piece in pieces],
        out_specs=whole((places, 2, group, width)),
        scratch_shapes=[scratch, scratch],
        compiler_params=pltpu.CompilerParams(vmem_limit_bytes=56 * 2**20),
        cost_estimate=pl.CostEstimate(
            flops=values * half_rows * 6, bytes_accessed=6 * values, transcendentals=0
        ),
    )(waves, scalars, eig_rates[:, None], *modes, legendre, *pieces)


def columns_plain(mirrored, legendre, waves, parity, eig_rates, modes_in, modes_out, sizes):
    wave_size, level_size, count, first, wave_count = sizes
    levels = modes_in.shape[0]
    half_rows, half_count = legendre.shape[1:]
    local_levels, rows_here = levels // level_size, half_rows // wave_size
    shape = mirrored.shape
    mirrored = mirrored.reshape(wave_size, level_size, 2, count, local_levels, rows_here)
    field = mirrored.transpose(3, 2, 1, 4, 0, 5).reshape(count, 2, levels, half_rows)
    table = legendre[first : first + count]
    degree = (
        waves[first : first + count, None] + 2 * jnp.arange(half_count, dtype=jnp.int32)[None, :]
    ).astype(jnp.float32) + parity
    inside = (degree <= float(wave_count - 1)).astype(jnp.float32)
    ratio = tau_scale * degree * (degree + 1.0) / float(wave_count * (wave_count - 1))
    factor = 1.0 / (1.0 + ratio[:, None, :] * eig_rates[None, :, None])
    spectral = jnp.einsum("sclr,srj->sclj", field, table, preferred_element_type=jnp.float32)
    spectral = (spectral * inside[:, None, None, :]).astype(jnp.bfloat16)
    modal = jnp.einsum("kl,sclj->sckj", modes_in, spectral, preferred_element_type=jnp.float32)
    modal = (modal * factor[:, None, :, :]).astype(jnp.bfloat16)
    solved = jnp.einsum(
        "lk,sckj->sclj", modes_out, modal, preferred_element_type=jnp.float32
    ).astype(jnp.bfloat16)
    grid = jnp.einsum("sclj,srj->sclr", solved, table, preferred_element_type=jnp.float32)
    grid = grid.astype(jnp.bfloat16)
    grid = grid.reshape(count, 2, level_size, local_levels, wave_size, rows_here)
    return grid.transpose(4, 2, 1, 0, 3, 5).reshape(shape)


def shards(grid_state, legendre, wave_order, lat_order, eig_rates, modes_in, modes_out):
    out_shape = grid_state.shape
    local_levels, _, rows_here, lon_count = out_shape
    wave_size = lax.axis_size("wave")
    level_size = lax.axis_size("level")
    places = wave_size * level_size
    half_rows = lat_order.shape[0]
    wave_count = wave_order.shape[0]
    narrow, half_count = legendre.shape[0], legendre.shape[3]
    chunks = min(CHUNKS, narrow)
    count = narrow // chunks
    height = 2 * count
    width = local_levels * rows_here
    direct = (
        places <= DIRECT_LIMIT
        and rows_here * 2 == LANES
        and wave_size % 2 == 0
        and count % 16 == 0
        and local_levels % 32 == 0
    )
    parity = lax.axis_index("fld")
    wave_place = lax.axis_index("wave")
    level_place = lax.axis_index("level")
    place = wave_place * level_size + level_place
    legendre = legendre.reshape(narrow, half_rows, half_count)
    grid_state = grid_state.reshape(local_levels, rows_here, lon_count)
    hemi_sign = 1.0 - 2.0 * parity.astype(jnp.float32)
    waves = lax.dynamic_slice_in_dim(wave_order, place * narrow, narrow)
    where = jnp.stack([wave_place, level_place, parity]).astype(jnp.int32)

    def exchange(value):
        return lax.all_to_all(value, EXCHANGE_AXES, split_axis=0, concat_axis=0, tiled=True)

    def joined(other, own, scale):
        both = scale * (other.astype(jnp.float32) + hemi_sign * own.astype(jnp.float32))
        return both.astype(jnp.bfloat16)

    def block_at(value, wave, level):
        place = (wave_place + wave) % wave_size * level_size + (level_place + level) % level_size
        return lax.dynamic_index_in_dim(value, place, 0, keepdims=False)

    if not direct:
        returned, tables = [], []
        for chunk in range(chunks):
            sizes = (wave_size, level_size, chunks, chunk, False, places * height)
            value, table = fourier(grid_state, where, wave_order, lat_order, sizes)
            tables.append(table)
            own = exchange(value.reshape(places, height, width))
            mirrored = joined(partner(own, "fld"), own, 1.0)
            grid = columns_plain(
                mirrored.reshape(wave_size, level_size, 2, count, width),
                legendre,
                waves,
                parity.astype(jnp.float32),
                eig_rates,
                modes_in,
                modes_out,
                (wave_size, level_size, count, chunk * count, wave_count),
            ).reshape(places, height, width)
            hemi = exchange(joined(partner(grid, "fld"), grid, 0.5))
            returned.append((hemi.reshape(places * height, width), 0))
        current = inverse_fourier(returned, tables, grid_state.shape, 0, local_levels)
        return current.reshape(out_shape)

    tiles = width // LANES
    level_index = jnp.arange(local_levels, dtype=jnp.int32).reshape(tiles, 2).T
    sources = []
    for is_turned in (0, 1):
        shift = jnp.arange(level_size, dtype=jnp.int32)
        from_level = (level_place - shift) % level_size if is_turned else shift
        order = (from_level[None, :, None] * local_levels + level_index[:, None, :]).reshape(-1)
        shift = jnp.arange(wave_size, dtype=jnp.int32)
        from_wave = (wave_place - shift) % wave_size if is_turned else shift
        sources.append(
            (
                jnp.concatenate([from_wave, parity[None]]),
                (jnp.take(modes_in, order, axis=1), jnp.take(modes_out, order, axis=0)),
            )
        )
    shifts = [(wave, level) for wave in range(wave_size) for level in range(level_size)]

    arrived, tables = [], []
    for chunk in range(chunks):
        is_whole = chunk in WHOLE_SENDS
        sizes = (wave_size, level_size, chunks, chunk, not is_whole, places * height)
        value, table = fourier(grid_state, where, wave_order, lat_order, sizes)
        tables.append(table)
        if is_whole:
            arrived.append([exchange(value.reshape(places, 2, count, width))])
            continue
        other = partner(value, "fld")
        pieces = []
        for index, (wave, level) in enumerate(shifts):
            rows = slice(index * height, (index + 1) * height)
            mirrored = joined(other[rows], value[rows], 1.0)
            piece = shift_places(mirrored, wave, level)
            pieces.append(piece.reshape(2, count, width))
        arrived.append(pieces)

    most = local_levels // 4 * 3
    groups = [(0, most), (most, local_levels - most)]
    cuts = {chunk: [(0, local_levels)] for chunk in range(chunks)}
    cuts[1] = cuts[chunks - 1] = groups
    returned = []
    for chunk in range(chunks):
        is_whole = chunk in WHOLE_SENDS
        pieces = arrived[chunk]
        if is_whole:
            pieces = [pieces[0], partner(pieces[0], "fld")]
        scalars, modes = sources[0 if is_whole else 1]
        sizes = (wave_size, level_size, count, tiles, half_count, wave_count, chunk * count)
        grid = columns_fused(pieces, legendre, waves, scalars, eig_rates, modes, sizes)
        grid = grid.reshape(places, height, width)
        other = partner(grid, "fld")
        if chunk in WHOLE_BACKS:
            hemi = exchange(joined(other, grid, 0.5))
            returned.append([(0, local_levels, [hemi.reshape(places * height, width)])])
            continue
        sent = []
        if is_whole:
            blocks = tables[chunk].reshape(places, height, lon_count)
            blocks = [block_at(blocks, wave, level) for wave, level in shifts]
            tables[chunk] = jnp.concatenate(blocks, axis=0)
        for start, levels in cuts[chunk]:
            lanes = slice(start * rows_here, (start + levels) * rows_here)
            pieces = []
            for index, (wave, level) in enumerate(shifts):
                if is_whole:
                    pair = block_at(other, -wave, -level), block_at(grid, -wave, -level)
                else:
                    pair = other[index, :, lanes], grid[index, :, lanes]
                hemi = joined(*pair, 0.5)
                wave, level = (wave_size - wave) % wave_size, (level_size - level) % level_size
                pieces.append(shift_places(hemi, wave, level))
            sent.append((start, levels, pieces))
        returned.append(sent)

    def pieces_at(chunk_list, start):
        return [
            (piece, begin)
            for chunk in chunk_list
            for begin, levels, pieces in returned[chunk]
            if begin <= start < begin + levels
            for piece in pieces
        ]

    shape = grid_state.shape
    everything = list(range(chunks))
    partials = []
    for start, levels in cuts[1]:
        partials.append(
            inverse_fourier(
                pieces_at(everything[:2], start),
                tables[:2],
                shape,
                start,
                levels,
                dtype=jnp.bfloat16,
            )
        )
    current = None
    for cut, (start, levels) in enumerate(groups):
        current = inverse_fourier(
            pieces_at(everything[2:], start),
            tables[2:],
            shape,
            start,
            levels,
            current=current,
            partial=(partials[cut], start),
        )
    return current.reshape(out_shape)


def solution(mesh):
    placed = (
        P(("member", "level"), "fld", "wave", None),
        P(("wave", "level"), "fld", None, None),
        P(),
        P(),
        P(),
        P(),
        P(),
    )
    return jax.shard_map(
        shards,
        mesh=mesh,
        in_specs=placed,
        out_specs=P(("member", "level"), "fld", "wave", None),
        check_vma=False,
    )
```

```python
import functools
import math

import jax
import jax.numpy as jnp
from jax import lax
from jax.experimental import pallas as pl
from jax.experimental.pallas import tpu as pltpu
from jax.sharding import PartitionSpec as P


tau_scale = 2.0
LANES = 128
CHUNKS = 4
WHOLE_SENDS = (0, 2)
WHOLE_BACKS = (0,)
DIRECT_LIMIT = 16
EXCHANGE_AXES = ("wave", "level")


def partner(value, axis):
    pairs = [(source, source ^ 1) for source in range(lax.axis_size(axis))]
    return lax.ppermute(value, axis, pairs)


def shift_places(value, wave_shift, level_shift):
    if wave_shift == 0 and level_shift == 0:
        return value
    waves, levels = lax.axis_size("wave"), lax.axis_size("level")
    pairs = []
    for wave in range(waves):
        for level in range(levels):
            target = (wave + wave_shift) % waves * levels + (level + level_shift) % levels
            pairs.append((wave * levels + level, target))
    return lax.ppermute(value, EXCHANGE_AXES, pairs)


def level_block(levels, rows_here, most):
    whole = levels % most == 0 and most * rows_here % LANES == 0
    return most if whole else levels


def pick(values, index):
    rows, many = index.shape[0], values.shape[1]
    hit = lax.broadcasted_iota(jnp.int32, (rows, many), 1) == index
    return jnp.sum(jnp.where(hit, values, 0.0), axis=1, keepdims=True)


def write_table(sizes, place_ref, wave_order, table):
    wave_size, level_size, chunks, chunk, turned, _ = sizes
    rows, lon_count = table.shape
    places = wave_size * level_size
    count = rows // (2 * places)
    scale = math.sqrt(2.0 / lon_count)
    row = lax.broadcasted_iota(jnp.int32, (rows, 1), 0)
    slot, place = row % count, row // (2 * count)
    part = (row // count) % 2
    if turned:
        wave = (place // level_size + place_ref[0]) % wave_size
        place = wave * level_size + (place % level_size + place_ref[1]) % level_size
    wave = pick(wave_order[...].astype(jnp.float32), (place * chunks + chunk) * count + slot)
    lane = lax.broadcasted_iota(jnp.int32, (rows, LANES), 1).astype(jnp.float32)

    def angle(steps):
        steps = steps - lon_count * jnp.floor(steps * (1.0 / lon_count))
        return steps * (2.0 * math.pi / lon_count)

    low = angle(wave * lane)
    high = angle(wave * lane * float(LANES) + part.astype(jnp.float32) * (lon_count / 4))
    low_cos, low_sin = jnp.cos(low) * scale, jnp.sin(low) * scale
    high_cos, high_sin = jnp.cos(high), jnp.sin(high)
    for block in range(lon_count // LANES):
        values = (
            high_cos[:, block : block + 1] * low_cos - high_sin[:, block : block + 1] * low_sin
        )
        table[:, block * LANES : (block + 1) * LANES] = values.astype(table.dtype)


def fourier_kernel(
    sizes, place_ref, grid_ref, wave_order, lat_order, out, table, coupling, held, arrived
):
    _, levels, rows, lon_count = held.shape
    step, steps = pl.program_id(0), pl.num_programs(0)

    def fetch(index):
        slot = index % 2
        source = grid_ref.at[pl.ds(index * levels, levels)]
        return pltpu.make_async_copy(source, held.at[slot], arrived.at[slot])

    @pl.when(step == 0)
    def _():
        fetch(step).start()
        write_table(sizes, place_ref, wave_order, table)
        row = lax.broadcasted_iota(jnp.int32, (rows, 1), 0) + place_ref[0] * rows
        latitude = pick(lat_order[...].astype(jnp.float32), row) + 0.5
        sine = jnp.sin(latitude * (math.pi / (2.0 * lat_order.shape[1])))
        sign = 1.0 - 2.0 * place_ref[2].astype(jnp.float32)
        coupling[...] = jnp.broadcast_to(0.5 * sign * sine, coupling.shape)

    @pl.when(step + 1 < steps)
    def _():
        fetch(step + 1).start()

    fetch(step).wait()
    field = held[step % 2].astype(jnp.float32)
    forcing = (field + coupling[:, :1][None] * jnp.tanh(field)).astype(jnp.bfloat16)
    forcing = forcing.reshape(levels * rows, lon_count)
    out[...] = lax.dot_general(
        table[...], forcing, (((1,), (1,)), ((), ())), preferred_element_type=jnp.float32
    ).astype(out.dtype)


def fourier(grid_state, place, wave_order, lat_order, sizes):
    levels, rows_here, lon_count = grid_state.shape
    _, _, _, _, _, height = sizes
    block = level_block(levels, rows_here, 16)
    width = levels * rows_here
    whole = lambda *shape: pl.BlockSpec(shape, lambda i: (0,) * len(shape))
    return pl.pallas_call(
        functools.partial(fourier_kernel, sizes),
        out_shape=[
            jax.ShapeDtypeStruct((height, width), jnp.bfloat16),
            jax.ShapeDtypeStruct((height, lon_count), jnp.bfloat16),
        ],
        grid=(levels // block,),
        in_specs=[
            pl.BlockSpec(memory_space=pltpu.SMEM),
            pl.BlockSpec(memory_space=pl.ANY),
            whole(1, wave_order.shape[0]),
            whole(1, lat_order.shape[0]),
        ],
        out_specs=[
            pl.BlockSpec((height, block * rows_here), lambda i: (0, i)),
            whole(height, lon_count),
        ],
        scratch_shapes=[
            pltpu.VMEM((rows_here, LANES), jnp.float32),
            pltpu.VMEM((2, block, rows_here, lon_count), jnp.bfloat16),
            pltpu.SemaphoreType.DMA((2,)),
        ],
        compiler_params=pltpu.CompilerParams(vmem_limit_bytes=56 * 2**20),
        cost_estimate=pl.CostEstimate(
            flops=2 * height * width * lon_count,
            bytes_accessed=2 * (width * lon_count + height * (width + lon_count)),
            transcendentals=width * lon_count,
        ),
    )(place, grid_state, wave_order[None], lat_order[None])


def inverse_kernel(pieces, tables, has_partial, *refs):
    out = refs[-1]
    coeffs = jnp.concatenate([ref[...] for ref in refs[:pieces]], axis=0)
    levels, rows, lon_count = out.shape
    loops = 3 if not has_partial and lon_count % (3 * LANES) == 0 else 1
    some = lon_count // loops

    def longitudes(index, carry):
        lanes = pl.ds(pl.multiple_of(index * some, some), some)
        table = jnp.concatenate([ref[:, lanes] for ref in refs[pieces : pieces + tables]], axis=0)
        current = lax.dot_general(
            coeffs, table, (((0,), (0,)), ((), ())), preferred_element_type=jnp.float32
        ).reshape(levels, rows, some)
        if has_partial:
            current = current + refs[pieces + tables][:, :, lanes]
        out[:, :, lanes] = current.astype(out.dtype)
        return carry

    if loops == 1:
        longitudes(0, 0)
    else:
        lax.fori_loop(0, loops, longitudes, 0)


def inverse_fourier(pieces, tables, shape, start, levels, current=None, partial=None, dtype=None):
    _, rows_here, lon_count = shape
    block = level_block(levels, rows_here, 8 if partial is None else levels // 2)
    width = block * rows_here
    first = start // block
    height = sum(table.shape[0] for table in tables)
    grid_block = (block, rows_here, lon_count)

    def cut(begin):
        return first - begin // block

    specs, operands, aliases = [], [], {}
    for piece, begin in pieces:
        operands.append(piece)
        specs.append(pl.BlockSpec((piece.shape[0], width), lambda i, skip=cut(begin): (0, skip + i)))
    for table in tables:
        operands.append(table)
        specs.append(
            pl.BlockSpec(table.shape, lambda i: (0, 0), pipeline_mode=pl.Buffered(1))
        )
    if partial is not None:
        operands.append(partial[0])
        specs.append(pl.BlockSpec(grid_block, lambda i, skip=cut(partial[1]): (skip + i, 0, 0)))
    if current is not None:
        aliases = {len(operands): 0}
        operands.append(current)
        specs.append(pl.BlockSpec(memory_space=pl.ANY))
    out_first = 0 if dtype is not None else first
    out_shape = (levels, rows_here, lon_count) if dtype is not None else shape
    return pl.pallas_call(
        functools.partial(inverse_kernel, len(pieces), len(tables), partial is not None),
        out_shape=jax.ShapeDtypeStruct(out_shape, dtype or jnp.bfloat16),
        grid=(levels // block,),
        in_specs=specs,
        out_specs=pl.BlockSpec(grid_block, lambda i: (out_first + i, 0, 0)),
        input_output_aliases=aliases,
        compiler_params=pltpu.CompilerParams(vmem_limit_bytes=56 * 2**20),
        cost_estimate=pl.CostEstimate(
            flops=2 * height * levels * rows_here * lon_count,
            bytes_accessed=2 * levels * rows_here * (height + lon_count),
            transcendentals=0,
        ),
    )(*operands)


def column_kernel(sizes, waves, scalars, eig_ref, modes_in, modes_out, table, *refs):
    wave_size, level_size, group, tiles, half_count, wave_count, first = sizes
    places = wave_size * level_size
    pieces, (out, rows_in, rows_out) = refs[:-3], refs[-3:]
    eights = group // 8
    rows_here = LANES // 2
    parity = scalars[wave_size].astype(jnp.float32)
    low_half = lax.broadcasted_iota(jnp.int32, (tiles, LANES), 1) < LANES // 2

    def spread(start, part, value):
        for tile in range(tiles):
            for eight in range(eights):
                row = ((start * 2 + part) * eights + eight) * tiles + tile
                rows_in[pl.ds(pl.multiple_of(row * 8, 8), 8), :] = value(tile)[
                    eight * 8 : (eight + 1) * 8
                ]

    if len(pieces) == 2:
        own, other = pieces
        sign = 1.0 - 2.0 * parity

        def combined(index, carry):
            place, part = index // 2, index % 2

            def value(tile):
                lanes = slice(tile * LANES, (tile + 1) * LANES)
                both = other[place, part, :, lanes].astype(jnp.float32) + sign * own[
                    place, part, :, lanes
                ].astype(jnp.float32)
                return both.astype(jnp.bfloat16).astype(jnp.float32)

            spread(place, part, value)
            return carry

        lax.fori_loop(0, places * 2, combined, 0)
    else:
        for place, piece in enumerate(pieces):

            def arrived(part, carry, place=place, piece=piece):
                def value(tile):
                    return piece[part, :, tile * LANES : (tile + 1) * LANES].astype(jnp.float32)

                spread(place, part, value)
                return carry

            lax.fori_loop(0, 2, arrived, 0)

    def where_rows(place, part, slot):
        eight, within = slot // 8, slot % 8
        return pl.ds((((place * 2 + part) * eights + eight) * tiles) * 8 + within, tiles, 8)

    def one_slot(slot, carry):
        legendre = jnp.concatenate(
            [
                table[slot, pl.ds(pl.multiple_of(scalars[wave] * rows_here, rows_here), rows_here), :]
                for wave in range(wave_size)
            ],
            axis=0,
        )
        stacked = []
        for part in range(2):
            low_rows, high_rows = [], []
            for level in range(level_size):
                low_pieces, high_pieces = [], []
                for pair in range(wave_size // 2):
                    a = rows_in[where_rows(2 * pair * level_size + level, part, slot), :]
                    b = rows_in[where_rows((2 * pair + 1) * level_size + level, part, slot), :]
                    low_pieces.append(jnp.where(low_half, a, pltpu.roll(b, LANES // 2, 1)))
                    high_pieces.append(jnp.where(low_half, pltpu.roll(a, LANES // 2, 1), b))
                low_rows.append(jnp.concatenate(low_pieces, axis=1))
                high_rows.append(jnp.concatenate(high_pieces, axis=1))
            stacked += low_rows + high_rows
        field = jnp.concatenate(stacked, axis=0).astype(jnp.bfloat16)
        degree = (
            waves[first + slot] + 2 * lax.broadcasted_iota(jnp.int32, (1, half_count), 1)
        ).astype(jnp.float32) + parity
        inside = (degree <= float(wave_count - 1)).astype(jnp.float32)
        ratio = tau_scale * degree * (degree + 1.0) / float(wave_count * (wave_count - 1))
        factor = 1.0 / (1.0 + eig_ref[...] * ratio)
        spectral = jnp.dot(field, legendre, preferred_element_type=jnp.float32)
        spectral = (spectral * inside).astype(jnp.bfloat16)
        levels = modes_in.shape[0]
        solved = []
        for part in range(2):
            column = spectral[part * levels : (part + 1) * levels]
            modal = jnp.dot(modes_in[...], column, preferred_element_type=jnp.float32)
            modal = (modal * factor).astype(jnp.bfloat16)
            solved.append(
                jnp.dot(modes_out[...], modal, preferred_element_type=jnp.float32).astype(
                    jnp.bfloat16
                )
            )
        grid = lax.dot_general(
            jnp.concatenate(solved, axis=0),
            legendre,
            (((1,), (1,)), ((), ())),
            preferred_element_type=jnp.float32,
        )
        for part in range(2):
            for level in range(level_size):
                low_start = part * levels + level * tiles
                high_start = low_start + level_size * tiles
                for pair in range(wave_size // 2):
                    lanes = slice(pair * LANES, (pair + 1) * LANES)
                    low = grid[low_start : low_start + tiles, lanes]
                    high = grid[high_start : high_start + tiles, lanes]
                    a = jnp.where(low_half, low, pltpu.roll(high, LANES // 2, 1))
                    b = jnp.where(low_half, pltpu.roll(low, LANES // 2, 1), high)
                    rows_out[where_rows(2 * pair * level_size + level, part, slot), :] = a
                    rows_out[where_rows((2 * pair + 1) * level_size + level, part, slot), :] = b
        return carry

    lax.fori_loop(0, group, one_slot, 0)

    def gather(index, carry):
        place, part = index // 2, index % 2
        for tile in range(tiles):
            parts = []
            for eight in range(eights):
                start = pl.multiple_of(((index * eights + eight) * tiles + tile) * 8, 8)
                parts.append(rows_out[pl.ds(start, 8), :])
            out[place, part, :, tile * LANES : (tile + 1) * LANES] = jnp.concatenate(
                parts, axis=0
            ).astype(out.dtype)
        return carry

    lax.fori_loop(0, places * 2, gather, 0)


def columns_fused(pieces, legendre, waves, scalars, eig_rates, modes, sizes):
    wave_size, level_size, group, tiles, half_count, _, first = sizes
    places = wave_size * level_size
    half_rows = legendre.shape[1]
    width = tiles * LANES
    levels = modes[0].shape[0]
    whole = lambda shape: pl.BlockSpec(shape, lambda i: (0,) * len(shape))
    scratch = pltpu.VMEM((places * 2 * group * tiles + 8, LANES), jnp.float32)
    values = places * 2 * group * width
    return pl.pallas_call(
        functools.partial(column_kernel, sizes),
        out_shape=jax.ShapeDtypeStruct((places, 2, group, width), jnp.bfloat16),
        grid=(1,),
        in_specs=[
            pl.BlockSpec(memory_space=pltpu.SMEM),
            pl.BlockSpec(memory_space=pltpu.SMEM),
            whole((levels, 1)),
            whole((levels, levels)),
            whole((levels, levels)),
            pl.BlockSpec((group, half_rows, half_count), lambda i: (first // group, 0, 0)),
        ]
        + [whole(piece.shape) for piece in pieces],
        out_specs=whole((places, 2, group, width)),
        scratch_shapes=[scratch, scratch],
        compiler_params=pltpu.CompilerParams(vmem_limit_bytes=56 * 2**20),
        cost_estimate=pl.CostEstimate(
            flops=values * half_rows * 6, bytes_accessed=6 * values, transcendentals=0
        ),
    )(waves, scalars, eig_rates[:, None], *modes, legendre, *pieces)


def columns_plain(mirrored, legendre, waves, parity, eig_rates, modes_in, modes_out, sizes):
    wave_size, level_size, count, first, wave_count = sizes
    levels = modes_in.shape[0]
    half_rows, half_count = legendre.shape[1:]
    local_levels, rows_here = levels // level_size, half_rows // wave_size
    shape = mirrored.shape
    mirrored = mirrored.reshape(wave_size, level_size, 2, count, local_levels, rows_here)
    field = mirrored.transpose(3, 2, 1, 4, 0, 5).reshape(count, 2, levels, half_rows)
    table = legendre[first : first + count]
    degree = (
        waves[first : first + count, None] + 2 * jnp.arange(half_count, dtype=jnp.int32)[None, :]
    ).astype(jnp.float32) + parity
    inside = (degree <= float(wave_count - 1)).astype(jnp.float32)
    ratio = tau_scale * degree * (degree + 1.0) / float(wave_count * (wave_count - 1))
    factor = 1.0 / (1.0 + ratio[:, None, :] * eig_rates[None, :, None])
    spectral = jnp.einsum("sclr,srj->sclj", field, table, preferred_element_type=jnp.float32)
    spectral = (spectral * inside[:, None, None, :]).astype(jnp.bfloat16)
    modal = jnp.einsum("kl,sclj->sckj", modes_in, spectral, preferred_element_type=jnp.float32)
    modal = (modal * factor[:, None, :, :]).astype(jnp.bfloat16)
    solved = jnp.einsum(
        "lk,sckj->sclj", modes_out, modal, preferred_element_type=jnp.float32
    ).astype(jnp.bfloat16)
    grid = jnp.einsum("sclj,srj->sclr", solved, table, preferred_element_type=jnp.float32)
    grid = grid.astype(jnp.bfloat16)
    grid = grid.reshape(count, 2, level_size, local_levels, wave_size, rows_here)
    return grid.transpose(4, 2, 1, 0, 3, 5).reshape(shape)


def shards(grid_state, legendre, wave_order, lat_order, eig_rates, modes_in, modes_out):
    out_shape = grid_state.shape
    local_levels, _, rows_here, lon_count = out_shape
    wave_size = lax.axis_size("wave")
    level_size = lax.axis_size("level")
    places = wave_size * level_size
    half_rows = lat_order.shape[0]
    wave_count = wave_order.shape[0]
    narrow, half_count = legendre.shape[0], legendre.shape[3]
    chunks = min(CHUNKS, narrow)
    count = narrow // chunks
    height = 2 * count
    width = local_levels * rows_here
    direct = (
        places <= DIRECT_LIMIT
        and rows_here * 2 == LANES
        and wave_size % 2 == 0
        and count % 16 == 0
        and local_levels % 32 == 0
    )
    parity = lax.axis_index("fld")
    wave_place = lax.axis_index("wave")
    level_place = lax.axis_index("level")
    place = wave_place * level_size + level_place
    legendre = legendre.reshape(narrow, half_rows, half_count)
    grid_state = grid_state.reshape(local_levels, rows_here, lon_count)
    hemi_sign = 1.0 - 2.0 * parity.astype(jnp.float32)
    waves = lax.dynamic_slice_in_dim(wave_order, place * narrow, narrow)
    where = jnp.stack([wave_place, level_place, parity]).astype(jnp.int32)

    def exchange(value):
        return lax.all_to_all(value, EXCHANGE_AXES, split_axis=0, concat_axis=0, tiled=True)

    def joined(other, own, scale):
        both = scale * (other.astype(jnp.float32) + hemi_sign * own.astype(jnp.float32))
        return both.astype(jnp.bfloat16)

    def block_at(value, wave, level):
        place = (wave_place + wave) % wave_size * level_size + (level_place + level) % level_size
        return lax.dynamic_index_in_dim(value, place, 0, keepdims=False)

    if not direct:
        returned, tables = [], []
        for chunk in range(chunks):
            sizes = (wave_size, level_size, chunks, chunk, False, places * height)
            value, table = fourier(grid_state, where, wave_order, lat_order, sizes)
            tables.append(table)
            own = exchange(value.reshape(places, height, width))
            mirrored = joined(partner(own, "fld"), own, 1.0)
            grid = columns_plain(
                mirrored.reshape(wave_size, level_size, 2, count, width),
                legendre,
                waves,
                parity.astype(jnp.float32),
                eig_rates,
                modes_in,
                modes_out,
                (wave_size, level_size, count, chunk * count, wave_count),
            ).reshape(places, height, width)
            hemi = exchange(joined(partner(grid, "fld"), grid, 0.5))
            returned.append((hemi.reshape(places * height, width), 0))
        current = inverse_fourier(returned, tables, grid_state.shape, 0, local_levels)
        return current.reshape(out_shape)

    tiles = width // LANES
    level_index = jnp.arange(local_levels, dtype=jnp.int32).reshape(tiles, 2).T
    sources = []
    for is_turned in (0, 1):
        shift = jnp.arange(level_size, dtype=jnp.int32)
        from_level = (level_place - shift) % level_size if is_turned else shift
        order = (from_level[None, :, None] * local_levels + level_index[:, None, :]).reshape(-1)
        shift = jnp.arange(wave_size, dtype=jnp.int32)
        from_wave = (wave_place - shift) % wave_size if is_turned else shift
        sources.append(
            (
                jnp.concatenate([from_wave, parity[None]]),
                (jnp.take(modes_in, order, axis=1), jnp.take(modes_out, order, axis=0)),
            )
        )
    shifts = [(wave, level) for wave in range(wave_size) for level in range(level_size)]

    arrived, tables = [], []
    for chunk in range(chunks):
        is_whole = chunk in WHOLE_SENDS
        sizes = (wave_size, level_size, chunks, chunk, not is_whole, places * height)
        value, table = fourier(grid_state, where, wave_order, lat_order, sizes)
        tables.append(table)
        if is_whole:
            arrived.append([exchange(value.reshape(places, 2, count, width))])
            continue
        other = partner(value, "fld")
        pieces = []
        for index, (wave, level) in enumerate(shifts):
            rows = slice(index * height, (index + 1) * height)
            mirrored = joined(other[rows], value[rows], 1.0)
            piece = shift_places(mirrored, wave, level)
            pieces.append(piece.reshape(2, count, width))
        arrived.append(pieces)

    half = local_levels // 2
    groups = [(0, half), (half, half)]
    cuts = {chunk: [(0, local_levels)] for chunk in range(chunks)}
    cuts[1] = cuts[chunks - 1] = groups
    returned = []
    for chunk in range(chunks):
        is_whole = chunk in WHOLE_SENDS
        pieces = arrived[chunk]
        if is_whole:
            pieces = [pieces[0], partner(pieces[0], "fld")]
        scalars, modes = sources[0 if is_whole else 1]
        sizes = (wave_size, level_size, count, tiles, half_count, wave_count, chunk * count)
        grid = columns_fused(pieces, legendre, waves, scalars, eig_rates, modes, sizes)
        grid = grid.reshape(places, height, width)
        other = partner(grid, "fld")
        if chunk in WHOLE_BACKS:
            hemi = exchange(joined(other, grid, 0.5))
            returned.append([(0, local_levels, [hemi.reshape(places * height, width)])])
            continue
        sent = []
        if is_whole:
            blocks = tables[chunk].reshape(places, height, lon_count)
            blocks = [block_at(blocks, wave, level) for wave, level in shifts]
            tables[chunk] = jnp.concatenate(blocks, axis=0)
        for start, levels in cuts[chunk]:
            lanes = slice(start * rows_here, (start + levels) * rows_here)
            pieces = []
            for index, (wave, level) in enumerate(shifts):
                if is_whole:
                    pair = block_at(other, -wave, -level), block_at(grid, -wave, -level)
                else:
                    pair = other[index, :, lanes], grid[index, :, lanes]
                hemi = joined(*pair, 0.5)
                wave, level = (wave_size - wave) % wave_size, (level_size - level) % level_size
                pieces.append(shift_places(hemi, wave, level))
            sent.append((start, levels, pieces))
        returned.append(sent)

    def pieces_at(chunk_list, start):
        return [
            (piece, begin)
            for chunk in chunk_list
            for begin, levels, pieces in returned[chunk]
            if begin <= start < begin + levels
            for piece in pieces
        ]

    shape = grid_state.shape
    everything = list(range(chunks))
    partials = []
    for start, levels in cuts[1]:
        partials.append(
            inverse_fourier(
                pieces_at(everything[:2], start),
                tables[:2],
                shape,
                start,
                levels,
                dtype=jnp.bfloat16,
            )
        )
    current = None
    for cut, (start, levels) in enumerate(groups):
        current = inverse_fourier(
            pieces_at(everything[2:], start),
            tables[2:],
            shape,
            start,
            levels,
            current=current,
            partial=(partials[cut], start),
        )
    return current.reshape(out_shape)


def solution(mesh):
    placed = (
        P(("member", "level"), "fld", "wave", None),
        P(("wave", "level"), "fld", None, None),
        P(),
        P(),
        P(),
        P(),
        P(),
    )
    return jax.shard_map(
        shards,
        mesh=mesh,
        in_specs=placed,
        out_specs=P(("member", "level"), "fld", "wave", None),
        check_vma=False,
    )
```
